32 devices in a mesh: dp: 4 (over y, x), fsdp: 8 (over z, core).
Axes of the slice: x: 2, y: 2, z: 4, core: 2. Of those that a mesh axis runs over, the one named last changes fastest.
Arguments:
- latents: float32 [128, 128, 384], P(('dp', 'fsdp')), may hold values from -6 to 6
- conditioning: float32 [128, 384], P(('dp', 'fsdp')), may hold values from -6 to 6
- counts: int32 [32], P(('dp', 'fsdp')), may hold values from 1 to 4, as said below
- cotangent: float32 [128, 128, 384], P(('dp', 'fsdp')), may hold values from -6 to 6
- ada_weights: bfloat16 [884736], P(('dp', 'fsdp')), may hold values from -0.3125 to 0.3125
- attn_weights: bfloat16 [589824], P(('dp', 'fsdp'))
- mlp_weights: bfloat16 [1179648], P(('dp', 'fsdp'))
- flat_biases: bfloat16 [5376], P(('dp', 'fsdp')), may hold values from -3 to 3
Outputs:
- output: float32 [128, 128, 384], P(('dp', 'fsdp'))
- grad_latents: float32 [128, 128, 384], P(('dp', 'fsdp'))
- grad_conditioning: float32 [128, 384], P(('dp', 'fsdp'))
- grad_ada_weights: float32 [884736], P(('dp', 'fsdp'))
- grad_attn_weights: float32 [589824], P(('dp', 'fsdp'))
- grad_mlp_weights: float32 [1179648], P(('dp', 'fsdp'))
- grad_biases: float32 [5376], P(('dp', 'fsdp'))
The draws below stay inside these ranges and needn't reach their ends.
Inputs may be any that keep to these rules, and one draw needn't show every extreme that they name: `counts`: slots of a device at or beyond its count hold padding; in every draw some device holds 4 live latents and some holds 1.
All inputs are finite; a program needn't handle non-finite values.
Results may differ from the reference program's by a relative error of at most 0.0095.
The reference program's roundings to bfloat16 on the way count: a program that leaves them out, or rounds other values in their place, can miss the bound.
Values may be sent and summed in bfloat16 or wider, within the bound.
A program may use at most 128 MiB of HBM per device.

```python
import jax
import jax.numpy as jnp
from jax import lax

D = 384
FF = 1536
HEADS = 6
SEQ = 128
LAT_CAP = 4
SHARDS = 32
SLOTS = 128
ADA_TOTAL = 884736
ATTN_TOTAL = 589824
MLP_TOTAL = 1179648
B_TOTAL = 5376


def draw_counts(key, part):
    first, second, third = jax.random.split(jax.random.fold_in(key, 11), 3)
    values = jax.random.randint(first, (SHARDS,), 1, LAT_CAP + 1, dtype=jnp.int32)
    busiest = jax.random.randint(second, (), 0, SHARDS, dtype=jnp.int32)
    lightest = (busiest + 1 + jax.random.randint(third, (), 0, SHARDS - 1, dtype=jnp.int32)) % SHARDS
    position = jnp.arange(SHARDS, dtype=jnp.int32)
    values = jnp.where(position == busiest, LAT_CAP, values)
    values = jnp.where(position == lightest, 1, values)
    return values.astype(jnp.int32)


def unit_values(key, total_count):
    values = jax.random.truncated_normal(key, -4.0, 4.0, (total_count,), jnp.float32)
    return values


def draw_attn_weights(key, part):
    position = jnp.arange(ATTN_TOTAL, dtype=jnp.int32)
    base = D ** (-0.5)
    spread = jnp.where(position < 3 * D * D, base, 6.0 * base)
    values = unit_values(jax.random.fold_in(key, 5), ATTN_TOTAL)
    return (values * spread).astype(jnp.bfloat16)


def draw_mlp_weights(key, part):
    position = jnp.arange(MLP_TOTAL, dtype=jnp.int32)
    spread = jnp.where(position < D * FF, D ** (-0.5), FF ** (-0.5))
    values = unit_values(jax.random.fold_in(key, 7), MLP_TOTAL)
    return (values * spread).astype(jnp.bfloat16)


def shard_levels(rng, extent, cuts, smallest, largest):
    level, own = 1.0, jax.random.fold_in(rng, 6)
    for dim, blocks in cuts:
        steps = jnp.exp(jax.random.uniform(jax.random.fold_in(own, dim), (blocks,), jnp.float32, smallest / len(cuts), largest / len(cuts)))
        level = level * jnp.repeat(steps, extent[dim] // blocks).reshape([-1 if axis == dim else 1 for axis in range(len(extent))])
    return level


def bell_draw(rng, extent, scale, reach, cuts=(), kind=jnp.bfloat16):
    level = shard_levels(rng, extent, cuts, -0.22, 0.18) if cuts else 1.0
    values = jax.random.normal(rng, extent, jnp.float32) * scale * level
    return jnp.minimum(jnp.maximum(values, -reach), reach).astype(kind)


def setup_inputs(seed: int = 0) -> dict:
    seeds = jax.random.split(jax.random.key(seed), 9)
    return {
        "latents": bell_draw(seeds[0], (SLOTS, SEQ, D), 1.0, 6.0, ((0, 32),), jnp.float32),
        "conditioning": bell_draw(seeds[1], (SLOTS, D), 1.0, 6.0, ((0, 32),), jnp.float32),
        "counts": draw_counts(jax.random.fold_in(seeds[8], 71), 0),
        "cotangent": bell_draw(seeds[3], (SLOTS, SEQ, D), 1.0, 6.0, ((0, 32),), jnp.float32),
        "ada_weights": bell_draw(seeds[4], (ADA_TOTAL,), D ** -0.5, 0.3125, ((0, 32),)),
        "attn_weights": draw_attn_weights(jax.random.fold_in(seeds[8], 71), 0),
        "mlp_weights": draw_mlp_weights(jax.random.fold_in(seeds[8], 71), 0),
        "flat_biases": bell_draw(seeds[7], (B_TOTAL,), 0.5, 3.0, ((0, 32),)),
    }


EPSILON = 1e-06
GELU_COEF = 0.044715
ROOT_TWO_OVER_PI = 0.7978845608028654

def layer_norm(values):
    centre = values - lax.optimization_barrier(jnp.mean(values, axis=-1, keepdims=True))
    inverse = lax.rsqrt(lax.optimization_barrier(jnp.mean(centre * centre, axis=-1, keepdims=True)) + EPSILON)
    return (centre * inverse, inverse)

def norm_backward(grad_norm, normed, inverse):
    first = lax.optimization_barrier(jnp.mean(grad_norm, axis=-1, keepdims=True))
    second = lax.optimization_barrier(jnp.mean(grad_norm * normed, axis=-1, keepdims=True))
    return (grad_norm - first - normed * second) * inverse

def gelu_value(pre_act):
    inner = ROOT_TWO_OVER_PI * (pre_act + GELU_COEF * pre_act * pre_act * pre_act)
    return 0.5 * pre_act * (1.0 + jnp.tanh(inner))

def gelu_slope(pre_act):
    tanh_part = jnp.tanh(ROOT_TWO_OVER_PI * (pre_act + GELU_COEF * pre_act * pre_act * pre_act))
    return 0.5 * (1.0 + tanh_part) + 0.5 * pre_act * (1.0 - tanh_part * tanh_part) * ROOT_TWO_OVER_PI * (1.0 + 3.0 * GELU_COEF * pre_act * pre_act)

def silu_slope(values):
    sigma = jax.nn.sigmoid(values)
    return sigma * (1.0 + values * (1.0 - sigma))

def product(form, left, right):
    return jnp.einsum(form, left.astype(jnp.float32), right.astype(jnp.float32))

def mat_dot(left, right):
    return jnp.dot(left, right, preferred_element_type=jnp.float32)

def unpack(ada_flat, attn_flat, mlp_flat, bias_flat, model_width, hidden_units):
    qkv_size = 3 * model_width * model_width
    fc1_size = model_width * hidden_units
    pieces = [ada_flat.reshape(model_width, 6 * model_width), attn_flat[:qkv_size].reshape(model_width, 3 * model_width), attn_flat[qkv_size:].reshape(model_width, model_width), mlp_flat[:fc1_size].reshape(model_width, hidden_units), mlp_flat[fc1_size:].reshape(hidden_units, model_width)]
    offset = 0
    for extent_now in [6 * model_width, model_width, model_width, model_width, hidden_units, model_width]:
        pieces.append(bias_flat[offset:offset + extent_now])
        offset = offset + extent_now
    return tuple(pieces)

def forward_group(latent_rows, cond_rows, live_rows, weights, head_count):
    w_ada, w_qkv, w_proj, w_fc1, w_fc2, b_ada, b_query, b_value, b_proj, b_fc1, b_fc2 = weights
    groups, length, model_width = latent_rows.shape
    head_dim = model_width // head_count
    row_count = groups * length
    score_scale = head_dim ** (-0.5)
    cond_act = jax.nn.silu(cond_rows).astype(jnp.bfloat16)
    modulation = mat_dot(cond_act, w_ada) + b_ada.astype(jnp.float32)
    parts = [modulation[:, None, k * model_width:(k + 1) * model_width] for k in range(6)]
    shift_attn, scale_attn, gate_attn, shift_mlp, scale_mlp, gate_mlp = parts
    norm_one, inverse_one = layer_norm(latent_rows)
    modulated_one = (norm_one * (1.0 + scale_attn) + shift_attn).astype(jnp.bfloat16)
    projected = mat_dot(modulated_one.reshape(row_count, model_width), w_qkv)
    query_rows = (projected[:, :model_width] + b_query.astype(jnp.float32)).astype(jnp.bfloat16).reshape(groups, length, model_width)
    key_rows = projected[:, model_width:2 * model_width].astype(jnp.bfloat16).reshape(groups, length, model_width)
    value_rows = (projected[:, 2 * model_width:] + b_value.astype(jnp.float32)).astype(jnp.bfloat16).reshape(groups, length, model_width)
    split_shape = (groups, length, head_count, head_dim)
    scores = product('gqhe,gkhe->ghqk', query_rows.reshape(split_shape), key_rows.reshape(split_shape)) * score_scale
    log_total = jnp.log(lax.optimization_barrier(jnp.sum(jnp.exp(scores), axis=-1, keepdims=True)))
    probs = jnp.exp(scores - log_total).astype(jnp.bfloat16)
    mixed = product('ghqk,gkhe->gqhe', probs, value_rows.reshape(split_shape)).astype(jnp.bfloat16).reshape(row_count, model_width)
    branch = (mat_dot(mixed, w_proj) + b_proj.astype(jnp.float32)).reshape(groups, length, model_width)
    after_attn = latent_rows + gate_attn * branch
    norm_two, inverse_two = layer_norm(after_attn)
    modulated_two = (norm_two * (1.0 + scale_mlp) + shift_mlp).astype(jnp.bfloat16)
    pre_act = mat_dot(modulated_two.reshape(row_count, model_width), w_fc1) + b_fc1.astype(jnp.float32)
    activated = gelu_value(pre_act).astype(jnp.bfloat16)
    mlp_rows = (mat_dot(activated, w_fc2) + b_fc2.astype(jnp.float32)).reshape(groups, length, model_width)
    output = jnp.where(live_rows[:, None, None], after_attn + gate_mlp * mlp_rows, 0.0)
    hidden_units = pre_act.shape[1]
    saved = (cond_act, modulation, norm_one, inverse_one, modulated_one, query_rows, key_rows, value_rows, log_total[..., 0], mixed.reshape(groups, length, model_width), branch, norm_two, inverse_two, modulated_two, pre_act.reshape(groups, length, hidden_units), activated.reshape(groups, length, hidden_units), mlp_rows)
    return (output, saved)

def mlp_backward(saved, cotangent_rows, live_rows, weights):
    w_fc1 = weights[3]
    w_fc2 = weights[4]
    cond_act, modulation, norm_one, inverse_one, modulated_one, query_rows, key_rows, value_rows, log_total, mixed, branch, norm_two, inverse_two, modulated_two, pre_act, activated, mlp_rows = saved
    groups, length, model_width = cotangent_rows.shape
    hidden_units = pre_act.shape[2]
    row_count = groups * length
    scale_mlp = modulation[:, None, 4 * model_width:5 * model_width]
    gate_mlp = modulation[:, None, 5 * model_width:6 * model_width]
    grad_out = jnp.where(live_rows[:, None, None], cotangent_rows, 0.0)
    grad_gate_mlp = lax.optimization_barrier(jnp.sum(grad_out * mlp_rows, axis=1))
    grad_mlp_full = grad_out * gate_mlp
    bias_fc2 = lax.optimization_barrier(jnp.sum(grad_mlp_full, axis=(0, 1)))
    grad_mlp = grad_mlp_full.astype(jnp.bfloat16).reshape(row_count, model_width)
    weight_fc2 = mat_dot(activated.reshape(row_count, hidden_units).T, grad_mlp)
    grad_pre_full = mat_dot(grad_mlp, w_fc2.T) * gelu_slope(pre_act.reshape(row_count, hidden_units))
    bias_fc1 = lax.optimization_barrier(jnp.sum(grad_pre_full, axis=0))
    grad_pre = grad_pre_full.astype(jnp.bfloat16)
    weight_fc1 = mat_dot(modulated_two.reshape(row_count, model_width).T, grad_pre)
    grad_two = mat_dot(grad_pre, w_fc1.T).reshape(groups, length, model_width)
    grad_scale_mlp = lax.optimization_barrier(jnp.sum(grad_two * norm_two, axis=1))
    grad_shift_mlp = lax.optimization_barrier(jnp.sum(grad_two, axis=1))
    grad_after = grad_out + norm_backward(grad_two * (1.0 + scale_mlp), norm_two, inverse_two)
    mod_tail = jnp.concatenate([grad_shift_mlp, grad_scale_mlp, grad_gate_mlp], axis=1)
    return (grad_after, mod_tail, (weight_fc1, weight_fc2, bias_fc1, bias_fc2))

def attention_backward(saved, cond_rows, grad_after, mod_tail, weights, head_count):
    w_ada = weights[0]
    w_qkv = weights[1]
    w_proj = weights[2]
    cond_act, modulation, norm_one, inverse_one, modulated_one, query_rows, key_rows, value_rows, log_total, mixed, branch, norm_two, inverse_two, modulated_two, pre_act, activated, mlp_rows = saved
    groups, length, model_width = grad_after.shape
    head_dim = model_width // head_count
    row_count = groups * length
    score_scale = head_dim ** (-0.5)
    scale_attn = modulation[:, None, model_width:2 * model_width]
    gate_attn = modulation[:, None, 2 * model_width:3 * model_width]
    grad_gate_attn = lax.optimization_barrier(jnp.sum(grad_after * branch, axis=1))
    grad_branch_full = grad_after * gate_attn
    bias_proj = lax.optimization_barrier(jnp.sum(grad_branch_full, axis=(0, 1)))
    grad_branch = grad_branch_full.astype(jnp.bfloat16).reshape(row_count, model_width)
    weight_proj = mat_dot(mixed.reshape(row_count, model_width).T, grad_branch)
    grad_mixed = mat_dot(grad_branch, w_proj.T).astype(jnp.bfloat16)
    split_shape = (groups, length, head_count, head_dim)
    query_split = query_rows.reshape(split_shape)
    key_split = key_rows.reshape(split_shape)
    value_split = value_rows.reshape(split_shape)
    mixed_split = grad_mixed.reshape(split_shape)
    scores = product('gqhe,gkhe->ghqk', query_split, key_split) * score_scale
    probs_full = jnp.exp(scores - log_total[..., None])
    grad_probs = product('gqhe,gkhe->ghqk', mixed_split, value_split)
    grad_value = product('ghqk,gqhe->gkhe', probs_full.astype(jnp.bfloat16), mixed_split).astype(jnp.bfloat16)
    delta_rows = lax.optimization_barrier(jnp.sum(probs_full * grad_probs, axis=-1, keepdims=True))
    grad_scores = (probs_full * (grad_probs - delta_rows) * score_scale).astype(jnp.bfloat16)
    grad_query = product('ghqk,gkhe->gqhe', grad_scores, key_split).astype(jnp.bfloat16)
    grad_key = product('ghqk,gqhe->gkhe', grad_scores, query_split).astype(jnp.bfloat16)
    grad_query = grad_query.reshape(row_count, model_width)
    grad_key = grad_key.reshape(row_count, model_width)
    grad_value = grad_value.reshape(row_count, model_width)
    grad_proj_in = jnp.concatenate([grad_query, grad_key, grad_value], axis=1)
    weight_qkv = mat_dot(modulated_one.reshape(row_count, model_width).T, grad_proj_in)
    bias_query = lax.optimization_barrier(jnp.sum(grad_query.astype(jnp.float32), axis=0))
    bias_value = lax.optimization_barrier(jnp.sum(grad_value.astype(jnp.float32), axis=0))
    grad_one = mat_dot(grad_proj_in, w_qkv.T).reshape(groups, length, model_width)
    grad_scale_attn = lax.optimization_barrier(jnp.sum(grad_one * norm_one, axis=1))
    grad_shift_attn = lax.optimization_barrier(jnp.sum(grad_one, axis=1))
    grad_input = grad_after + norm_backward(grad_one * (1.0 + scale_attn), norm_one, inverse_one)
    grad_mod_full = jnp.concatenate([grad_shift_attn, grad_scale_attn, grad_gate_attn, mod_tail], axis=1)
    bias_ada = lax.optimization_barrier(jnp.sum(grad_mod_full, axis=0))
    grad_mod = grad_mod_full.astype(jnp.bfloat16)
    weight_ada = mat_dot(cond_act.T, grad_mod)
    grad_cond = mat_dot(grad_mod, w_ada.T) * silu_slope(cond_rows)
    return (grad_input, grad_cond, (weight_ada, weight_qkv, weight_proj, bias_ada, bias_query, bias_value, bias_proj))

def reference(latents, conditioning, counts, cotangent, ada_weights, attn_weights, mlp_weights, flat_biases):
    weights = unpack(ada_weights, attn_weights, mlp_weights, flat_biases, D, FF)
    slot_count = latents.shape[0]
    slot_ids = jnp.arange(slot_count, dtype=jnp.int32)
    live = slot_ids % LAT_CAP < counts[slot_ids // LAT_CAP]
    group_size = 16
    turns = slot_count // group_size

    def grouped(array):
        return array.reshape((turns, group_size) + array.shape[1:])
    zero_attn = tuple((jnp.zeros(weights[k].shape, jnp.float32) for k in (0, 1, 2, 5, 6, 7, 8)))
    zero_mlp = tuple((jnp.zeros(weights[k].shape, jnp.float32) for k in (3, 4, 9, 10)))

    def step(totals, inputs):
        attn_totals, mlp_totals = totals
        latent_rows, cond_rows, cotangent_rows, live_rows = inputs
        output, saved = forward_group(latent_rows, cond_rows, live_rows, weights, HEADS)
        grad_after, mod_tail, mlp_grads = mlp_backward(saved, cotangent_rows, live_rows, weights)
        grad_input, grad_cond, attn_grads = attention_backward(saved, cond_rows, grad_after, mod_tail, weights, HEADS)
        attn_totals = tuple((total + grad for total, grad in zip(attn_totals, attn_grads)))
        mlp_totals = tuple((total + grad for total, grad in zip(mlp_totals, mlp_grads)))
        return ((attn_totals, mlp_totals), (output, grad_input, grad_cond))
    totals, stacked = lax.scan(step, (zero_attn, zero_mlp), (grouped(latents), grouped(conditioning), grouped(cotangent), grouped(live)))
    attn_totals, mlp_totals = totals
    output = stacked[0].reshape(latents.shape)
    grad_latents = stacked[1].reshape(latents.shape)
    grad_conditioning = stacked[2].reshape(conditioning.shape)
    grad_ada = attn_totals[0].reshape(-1)
    grad_attn = jnp.concatenate([attn_totals[1].reshape(-1), attn_totals[2].reshape(-1)])
    grad_mlp = jnp.concatenate([mlp_totals[0].reshape(-1), mlp_totals[1].reshape(-1)])
    grad_biases = jnp.concatenate([attn_totals[3], attn_totals[4], attn_totals[5], attn_totals[6], mlp_totals[2], mlp_totals[3]])
    return (output, grad_latents, grad_conditioning, grad_ada, grad_attn, grad_mlp, grad_biases)
```

```python
from functools import partial
import math

import jax
import jax.numpy as jnp
from jax import lax
from jax.experimental import pallas as pl
from jax.experimental.pallas import tpu as pltpu
from jax.sharding import PartitionSpec as P

FF = 1536
HEADS = 6


EPSILON = 1e-06
GELU_COEF = 0.044715
ROOT_TWO_OVER_PI = 0.7978845608028654


def layer_norm(values):
    centre = values - jnp.mean(values, axis=-1, keepdims=True)
    inverse = lax.rsqrt(jnp.mean(centre * centre, axis=-1, keepdims=True) + EPSILON)
    return (centre * inverse, inverse)


def norm_backward(grad_norm, normed, inverse):
    first = jnp.mean(grad_norm, axis=-1, keepdims=True)
    second = jnp.mean(grad_norm * normed, axis=-1, keepdims=True)
    return (grad_norm - first - normed * second) * inverse


def gelu_value(pre_act):
    inner = ROOT_TWO_OVER_PI * (pre_act + GELU_COEF * pre_act * pre_act * pre_act)
    return 0.5 * pre_act * (1.0 + jnp.tanh(inner))


def gelu_slope(pre_act):
    tanh_part = jnp.tanh(ROOT_TWO_OVER_PI * (pre_act + GELU_COEF * pre_act * pre_act * pre_act))
    return 0.5 * (1.0 + tanh_part) + 0.5 * pre_act * (
        1.0 - tanh_part * tanh_part
    ) * ROOT_TWO_OVER_PI * (1.0 + 3.0 * GELU_COEF * pre_act * pre_act)


def silu_slope(values):
    sigma = jax.nn.sigmoid(values)
    return sigma * (1.0 + values * (1.0 - sigma))


LANES = 128
SUBLANES = 16
AXES = ("dp", "fsdp")
MESH = pl.DeviceIdType.MESH


class Grid:
    def __init__(self, mesh):
        dp, fsdp = mesh.shape["dp"], mesh.shape["fsdp"]
        side = math.isqrt(dp)
        self.high = side if side * side == dp else 1
        self.low = dp // self.high
        self.pair = 2 if fsdp % 2 == 0 else 1
        self.depth = fsdp // self.pair
        self.count = dp * fsdp
        self.sizes = (self.high, self.low, self.depth, self.pair)

    def here(self):
        a, f = lax.axis_index("dp"), lax.axis_index("fsdp")
        return [a // self.low, a % self.low, f // self.pair, f % self.pair]

    def peer(self, here, axis, step):
        spot = list(here)
        spot[axis] = lax.rem(here[axis] + step, self.sizes[axis])
        return spot

    def ident(self, spot):
        return (spot[0] * self.low + spot[1], spot[2] * self.pair + spot[3])

    def barrier(self, here):
        sem = pltpu.get_barrier_semaphore()
        total = 0
        for axis in range(4):
            for step in range(1, self.sizes[axis]):
                pl.semaphore_signal(
                    sem, inc=1, device_id=self.ident(self.peer(here, axis, step)), device_id_type=MESH
                )
                total += 1
        pl.semaphore_wait(sem, total)


def chunk_rows(arrays):
    chunks = []
    for n, array in enumerate(arrays):
        rows = array.shape[-2]
        if rows % (2 * SUBLANES) == 0:
            chunks += [(n, 0, rows // 2), (n, rows // 2, rows // 2)]
        else:
            chunks.append((n, 0, rows))
    return chunks


class Mover:
    def __init__(self, grid, send_sem, recv_sem):
        self.grid, self.here = grid, grid.here()
        self.send_sem, self.recv_sem = send_sem, recv_sem
        self.started = []

    def push(self, src, dst, spot):
        k = len(self.started)
        copy = pltpu.make_async_remote_copy(
            src_ref=src, dst_ref=dst, send_sem=self.send_sem.at[k], recv_sem=self.recv_sem.at[k],
            device_id=self.grid.ident(spot), device_id_type=MESH,
        )
        copy.start()
        self.started.append(copy)
        return copy

    def spots(self, axis):
        return [self.grid.peer(self.here, axis, s) for s in range(1, self.grid.sizes[axis])]

    def pushes(self, ref, axis):
        return [self.push(ref, ref, spot) for spot in self.spots(axis)]

    def drain(self):
        for copy in self.started:
            copy.wait_send()


def arrive(copies):
    for copy in copies:
        copy.wait_recv()


class Spread:
    def __init__(self, mover, in_ref, out_ref, rows, low_first):
        self.mover, self.in_ref, self.out_ref, self.rows = mover, in_ref, out_ref, rows
        self.low_first = low_first
        self.swap = []

    def begin(self):
        hi, lo, z, c = self.mover.here
        src, dst = self.in_ref.at[self.rows], self.out_ref.at[hi, lo, z, c, self.rows]
        self.pending = [self.mover.push(src, dst, spot) for spot in self.mover.spots(2)]

    def first(self):
        hi, lo, z, c = self.mover.here
        arrive(self.pending)
        part = self.out_ref.at[hi, lo, :, c, self.rows]
        self.pending = self.mover.pushes(part, 1 if self.low_first else 0)
        self.swap += self.mover.pushes(part, 3)

    def second(self):
        hi, lo, z, c = self.mover.here
        arrive(self.pending)
        out, rows = self.out_ref, self.rows
        if self.low_first:
            self.pending = self.mover.pushes(out.at[hi, :, :, c, rows], 0)
            others = [out.at[hi, spot[1], :, c, rows] for spot in self.mover.spots(1)]
        else:
            self.pending = self.mover.pushes(out.at[:, lo, :, c, rows], 1)
            others = [out.at[spot[0], lo, :, c, rows] for spot in self.mover.spots(0)]
        for other in others:
            self.swap += self.mover.pushes(other, 3)

    def third(self):
        hi, lo, z, c = self.mover.here
        arrive(self.pending)
        out, rows = self.out_ref, self.rows
        if self.low_first:
            others = [out.at[spot[0], :, :, c, rows] for spot in self.mover.spots(0)]
        else:
            others = [out.at[:, spot[1], :, c, rows] for spot in self.mover.spots(1)]
        for other in others:
            self.swap += self.mover.pushes(other, 3)

    def end(self):
        arrive(self.swap)

    @staticmethod
    def copies(grid):
        high, low, depth, pair = grid.sizes
        return depth - 1 + (high + low - 2) + (pair - 1) * (1 + high + low - 2)


def gather_kernel(grid, chunks, arrays, *refs):
    in_refs, out_refs = refs[:arrays], refs[arrays : 2 * arrays]
    send_sem, recv_sem, own_sem = refs[2 * arrays :]
    mover = Mover(grid, send_sem, recv_sem)
    hi, lo, z, c = mover.here
    grid.barrier(mover.here)
    own = [
        pltpu.make_async_copy(in_refs[n], out_refs[n].at[hi, lo, z, c], own_sem.at[n])
        for n in range(arrays)
    ]
    for copy in own:
        copy.start()
    spreads = [
        Spread(mover, in_refs[n], out_refs[n], pl.ds(start, size), k % 2 == 0)
        for k, (n, start, size) in enumerate(chunks)
    ]
    for spread in spreads:
        spread.begin()
    for copy in own:
        copy.wait()
    for spread in spreads:
        spread.first()
    for spread in spreads:
        spread.second()
    for spread in spreads:
        spread.third()
    for spread in spreads:
        spread.end()
    mover.drain()


def gather_all(grid, arrays):
    chunks = chunk_rows(arrays)
    copies = Spread.copies(grid) * len(chunks)
    vmem = pl.BlockSpec(memory_space=pltpu.VMEM)
    return pl.pallas_call(
        partial(gather_kernel, grid, chunks, len(arrays)),
        out_shape=[jax.ShapeDtypeStruct(grid.sizes + array.shape, array.dtype) for array in arrays],
        in_specs=[vmem] * len(arrays),
        out_specs=[vmem] * len(arrays),
        scratch_shapes=[
            pltpu.SemaphoreType.DMA((copies,)),
            pltpu.SemaphoreType.DMA((copies,)),
            pltpu.SemaphoreType.DMA((len(arrays),)),
        ],
        compiler_params=pltpu.CompilerParams(
            collective_id=0, has_side_effects=True, vmem_limit_bytes=48 * 1024 * 1024
        ),
    )(*arrays)


def scatter_kernel(grid, chunks, arrays, extra, *refs):
    note_refs, refs = refs[:extra], refs[extra:]
    g_refs, refs = refs[:arrays], refs[arrays:]
    note_outs, refs = refs[:extra], refs[extra:]
    out_refs, refs = refs[:arrays], refs[arrays:]
    pair_bufs, refs = refs[:arrays], refs[arrays:]
    accs, refs = refs[:arrays], refs[arrays:]
    one_bufs, refs = refs[:arrays], refs[arrays:]
    two_bufs, refs = refs[:arrays], refs[arrays:]
    z_bufs, (send_sem, recv_sem, own_sem) = refs[:arrays], refs[arrays:]
    mover = Mover(grid, send_sem, recv_sem)
    here, push = mover.here, mover.push
    hi, lo, z, c = here
    grid.barrier(here)
    owns = [
        pltpu.make_async_copy(note_refs[n], note_outs[n].at[hi, lo, z, c], own_sem.at[n])
        for n in range(extra)
    ]
    notes = [
        Spread(mover, note_refs[n], note_outs[n], pl.ds(0, note_refs[n].shape[0]), n % 2 == 0)
        for n in range(extra)
    ]
    for own, note in zip(owns, notes):
        own.start()
        note.begin()

    def steps(axis):
        return [(s - 1, grid.peer(here, axis, s)) for s in range(1, grid.sizes[axis])]

    def add(into, terms, first, second):
        def body(t, _):
            i, j = t // second, t % second
            total = terms[0](i, j)[...].astype(jnp.float32)
            for term in terms[1:]:
                total = total + term(i, j)[...].astype(jnp.float32)
            target = into(i, j)
            target[...] = total.astype(target.dtype)
            return 0

        lax.fori_loop(0, first * second, body, 0)

    high, low, depth, pair = grid.sizes
    swaps, ones, twos, lines = [], [], [], []
    for n, start, size in chunks:
        rows = pl.ds(start, size)
        g_ref, pair_buf = g_refs[n], pair_bufs[n]
        swaps.append(
            [push(g_ref.at[:, :, :, spot[3], rows], pair_buf.at[:, :, :, rows], spot) for _, spot in steps(3)]
        )
    for own, note in zip(owns, notes):
        own.wait()
        note.first()
    for k, (n, start, size) in enumerate(chunks):
        rows = pl.ds(start, size)
        g_ref, pair_buf, acc, buf_one = g_refs[n], pair_bufs[n], accs[n], one_bufs[n]
        arrive(swaps[k])
        terms = [lambda i, j: g_ref.at[i // low, i % low, j, c, rows]]
        if pair > 1:
            terms.append(lambda i, j: pair_buf.at[i // low, i % low, j, rows])
        add(lambda i, j: acc.at[i // low, i % low, j, rows], terms, high * low, depth)
        if k % 2 == 0:
            ones.append(
                [push(acc.at[spot[0], :, :, rows], buf_one.at[s, 0:low, :, rows], spot) for s, spot in steps(0)]
            )
        else:
            ones.append(
                [push(acc.at[:, spot[1], :, rows], buf_one.at[s, 0:high, :, rows], spot) for s, spot in steps(1)]
            )
    for note in notes:
        note.second()
    for k, (n, start, size) in enumerate(chunks):
        rows = pl.ds(start, size)
        acc, buf_one, buf_two = accs[n], one_bufs[n], two_bufs[n]
        arrive(ones[k])
        even = k % 2 == 0
        mine = (lambda i, j: acc.at[hi, i, j, rows]) if even else (lambda i, j: acc.at[i, lo, j, rows])
        terms = [mine] + [
            (lambda i, j, s=s: buf_one.at[s, i, j, rows]) for s, _ in steps(0 if even else 1)
        ]
        add(mine, terms, low if even else high, depth)
        if even:
            twos.append(
                [push(acc.at[hi, spot[1], :, rows], buf_two.at[s, :, rows], spot) for s, spot in steps(1)]
            )
        else:
            twos.append(
                [push(acc.at[spot[0], lo, :, rows], buf_two.at[s, :, rows], spot) for s, spot in steps(0)]
            )
    for note in notes:
        note.third()
    for k, (n, start, size) in enumerate(chunks):
        rows = pl.ds(start, size)
        acc, buf_two, buf_z = accs[n], two_bufs[n], z_bufs[n]
        arrive(twos[k])
        mine = lambda i, j: acc.at[hi, lo, j, rows]
        terms = [mine] + [
            (lambda i, j, s=s: buf_two.at[s, j, rows]) for s, _ in steps(1 if k % 2 == 0 else 0)
        ]
        add(mine, terms, 1, depth)
        lines.append(
            [push(acc.at[hi, lo, spot[2], rows], buf_z.at[s, rows], spot) for s, spot in steps(2)]
        )
    for k, (n, start, size) in enumerate(chunks):
        rows = pl.ds(start, size)
        acc, buf_z = accs[n], z_bufs[n]
        arrive(lines[k])
        total = acc[hi, lo, z, rows].astype(jnp.float32)
        for s in range(depth - 1):
            total = total + buf_z[s, rows].astype(jnp.float32)
        out_refs[n][rows, :] = total
    for note in notes:
        note.end()
    mover.drain()


def scatter_sum(grid, arrays, notes):
    high, low, depth, pair = grid.sizes
    chunks = chunk_rows(arrays)
    copies = len(chunks) * (high + low + depth + pair - 4) + Spread.copies(grid) * len(notes)
    kind = arrays[0].dtype
    tails = [array.shape[-2:] for array in arrays]
    side = max(high, low)
    shapes = [
        (high, low, depth), (high, low, depth), (max(side - 1, 1), side, depth),
        (max(side - 1, 1), depth), (max(depth - 1, 1),),
    ]
    vmem = pl.BlockSpec(memory_space=pltpu.VMEM)
    return pl.pallas_call(
        partial(scatter_kernel, grid, chunks, len(arrays), len(notes)),
        out_shape=[jax.ShapeDtypeStruct(grid.sizes + note.shape, note.dtype) for note in notes]
        + [jax.ShapeDtypeStruct(tail, jnp.float32) for tail in tails],
        in_specs=[vmem] * (len(notes) + len(arrays)),
        out_specs=[vmem] * (len(notes) + len(arrays)),
        scratch_shapes=[pltpu.VMEM(shape + tail, kind) for shape in shapes for tail in tails]
        + [pltpu.SemaphoreType.DMA((copies,)), pltpu.SemaphoreType.DMA((copies,)), pltpu.SemaphoreType.DMA((len(notes),))],
        compiler_params=pltpu.CompilerParams(
            collective_id=1, has_side_effects=True, vmem_limit_bytes=48 * 1024 * 1024
        ),
    )(*notes, *arrays)


def padded_rows(extent):
    return -(-extent // LANES)


def pack(pieces, lead):
    parts = []
    for piece in pieces:
        extent = piece.shape[-1]
        rows = padded_rows(extent)
        gap = rows * LANES - extent
        if gap:
            piece = jnp.pad(piece, [(0, 0)] * len(lead) + [(0, gap)])
        parts.append(piece.reshape(lead + (rows, LANES)))
    if len(parts) == 1:
        return parts[0]
    return jnp.concatenate(parts, axis=-2)


def dot(left, right, contract=(1, 0)):
    return lax.dot_general(
        left, right, (((contract[0],), (contract[1],)), ((), ())), preferred_element_type=jnp.float32
    )


def block_kernel(
    count_ref, x_ref, cond_ref, cot_ref, w_ada, attn_ref, mlp_ref, bias_ref,
    out_ref, gx_ref, gcond_ref, act_ref, dmod_ref, g_attn, g_mlp, gbias_ref,
    line, w_qkv, w_proj, w_one, w_two, g_qkv, g_proj, g_one, g_two,
    mod, norm_one, inv_one, h_one, qkv, probs, mixed, branch, norm_two, inv_two, h_two,
    pre, act, mlp, wide, back, dx, small, dqkv, dmod,
):
    slots, length, width = x_ref.shape
    hidden = w_one.shape[1]
    rows_all = slots * length
    heads = probs.shape[1]
    head_dim = width // heads
    score_scale = head_dim ** (-0.5)
    f32, b16 = jnp.float32, jnp.bfloat16
    tile = 256 if hidden % 256 == 0 else hidden
    count = count_ref[0]
    o_query, o_value = 6 * width, 7 * width
    o_proj, o_one, o_two = 8 * width, 9 * width, 9 * width + hidden
    lane = lax.broadcasted_iota(jnp.int32, (length, 2 * head_dim), 1)
    lower = lane < head_dim

    def slot_loop(body):
        def step(s, _):
            body(s, pl.ds(pl.multiple_of(s * length, length), length))
            return 0

        lax.fori_loop(0, slots, step, 0)

    def part(s, k):
        return mod[pl.ds(s, 1), k * width : (k + 1) * width]

    def only(pair_block, first):
        return jnp.where(lower if first else jnp.logical_not(lower), pair_block, jnp.zeros_like(pair_block))

    def column_sum(values):
        return jnp.sum(values, axis=0, keepdims=True)

    def load_matrix(flat_ref, top, matrix):
        height, across = matrix.shape[0], matrix.shape[1] // LANES
        total = height * across

        def widen(t, _):
            at = pl.multiple_of(t * LANES, LANES)
            line[pl.ds(at, LANES), :] = flat_ref[pl.ds(top + at, LANES), :].astype(f32)
            return 0

        lax.fori_loop(0, total // LANES, widen, 0)
        for j in range(across):
            matrix[:, j * LANES : (j + 1) * LANES] = line[pl.ds(j, height, stride=across), :].astype(b16)

    def store_matrix(matrix, flat_ref, top):
        height, across = matrix.shape[0], matrix.shape[1] // LANES
        total = height * across
        for j in range(across):
            line[pl.ds(j, height, stride=across), :] = matrix[:, j * LANES : (j + 1) * LANES].astype(f32)

        def narrow(t, _):
            at = pl.multiple_of(t * LANES, LANES)
            flat_ref[pl.ds(top + at, LANES), :] = line[pl.ds(at, LANES), :].astype(b16)
            return 0

        lax.fori_loop(0, total // LANES, narrow, 0)

    proj_top, two_top = 3 * width * width // LANES, width * hidden // LANES
    load_matrix(attn_ref, 0, w_qkv)
    load_matrix(attn_ref, proj_top, w_proj)
    load_matrix(mlp_ref, 0, w_one)
    load_matrix(mlp_ref, two_top, w_two)
    cond = cond_ref[...]
    cond_act = (cond * jax.nn.sigmoid(cond)).astype(b16)
    mod[...] = dot(cond_act, w_ada[...]) + bias_ref[:, : 6 * width]

    def norm_first(s, rows):
        normed, inverse = layer_norm(x_ref[s])
        norm_one[rows, :] = normed
        inv_one[rows, :] = inverse
        h_one[rows, :] = (normed * (1.0 + part(s, 1)) + part(s, 0)).astype(b16)

    slot_loop(norm_first)
    for k, offset in enumerate((o_query, None, o_value)):
        cols = slice(k * width, (k + 1) * width)
        value = dot(h_one[...], w_qkv[:, cols])
        if offset is not None:
            value = value + bias_ref[:, offset : offset + width]
        qkv[:, cols] = value.astype(b16)

    def attend(s, rows):
        for pair in range(heads // 2):
            at = pair * 2 * head_dim
            query = qkv[rows, at : at + 2 * head_dim]
            key = qkv[rows, width + at : width + at + 2 * head_dim]
            value = qkv[rows, 2 * width + at : 2 * width + at + 2 * head_dim]
            halves = []
            for h in range(2):
                scores = dot(only(query, h == 0), key, (1, 1)) * score_scale
                total = jnp.log(jnp.sum(jnp.exp(scores), axis=-1, keepdims=True))
                prob = jnp.exp(scores - total)
                probs[s, 2 * pair + h] = prob
                halves.append(dot(prob.astype(b16), value))
            mixed[rows, at : at + 2 * head_dim] = jnp.where(lower, halves[0], halves[1]).astype(b16)

    slot_loop(attend)
    branch[...] = dot(mixed[...], w_proj[...]) + bias_ref[:, o_proj : o_proj + width]

    def norm_second(s, rows):
        after = x_ref[s] + part(s, 2) * branch[rows, :]
        dx[rows, :] = after
        normed, inverse = layer_norm(after)
        norm_two[rows, :] = normed
        inv_two[rows, :] = inverse
        h_two[rows, :] = (normed * (1.0 + part(s, 4)) + part(s, 3)).astype(b16)

    slot_loop(norm_second)

    def up(t, _):
        cols = pl.ds(pl.multiple_of(t * tile, tile), tile)
        shift = bias_ref[:, pl.ds(pl.multiple_of(o_one + t * tile, LANES), tile)]
        value = dot(h_two[...], w_one[:, cols]) + shift
        pre[:, cols] = value
        act[:, cols] = gelu_value(value).astype(b16)
        return 0

    lax.fori_loop(0, hidden // tile, up, 0)
    mlp[...] = dot(act[...], w_two[...]) + bias_ref[:, o_two : o_two + width]

    gbias_ref[...] = jnp.zeros_like(gbias_ref)

    def finish(s, rows):
        live = s < count
        value = mlp[rows, :]
        out_ref[s] = jnp.where(live, dx[rows, :] + part(s, 5) * value, 0.0)
        grad = jnp.where(live, cot_ref[s], 0.0)
        dmod[pl.ds(s, 1), 5 * width :] = column_sum(grad * value)
        full = grad * part(s, 5)
        gbias_ref[:, o_two : o_two + width] += column_sum(full)
        small[rows, :] = full.astype(b16)

    slot_loop(finish)

    def down(t, _):
        cols = pl.ds(pl.multiple_of(t * tile, tile), tile)
        full = dot(small[...], w_two[cols, :], (1, 1)) * gelu_slope(pre[:, cols])
        gbias_ref[:, pl.ds(pl.multiple_of(o_one + t * tile, LANES), tile)] = column_sum(full)
        grad = full.astype(b16)
        wide[:, cols] = grad
        g_two[cols, :] = dot(act[:, cols], small[...], (0, 0)).astype(g_two.dtype)
        g_one[:, cols] = dot(h_two[...], grad, (0, 0)).astype(g_one.dtype)
        return 0

    lax.fori_loop(0, hidden // tile, down, 0)
    back[...] = dot(wide[...], w_one[...], (1, 1))

    def mlp_back(s, rows):
        grad_two = back[rows, :]
        normed = norm_two[rows, :]
        dmod[pl.ds(s, 1), 4 * width : 5 * width] = column_sum(grad_two * normed)
        dmod[pl.ds(s, 1), 3 * width : 4 * width] = column_sum(grad_two)
        after = jnp.where(s < count, cot_ref[s], 0.0) + norm_backward(
            grad_two * (1.0 + part(s, 4)), normed, inv_two[rows, :]
        )
        dx[rows, :] = after
        dmod[pl.ds(s, 1), 2 * width : 3 * width] = column_sum(after * branch[rows, :])
        full = after * part(s, 2)
        gbias_ref[:, o_proj : o_proj + width] += column_sum(full)
        small[rows, :] = full.astype(b16)

    slot_loop(mlp_back)
    g_proj[...] = dot(mixed[...], small[...], (0, 0)).astype(g_proj.dtype)
    mixed[...] = dot(small[...], w_proj[...], (1, 1)).astype(b16)

    def attend_back(s, rows):
        for pair in range(heads // 2):
            at = pair * 2 * head_dim
            span = slice(at, at + 2 * head_dim)
            query = qkv[rows, span]
            key = qkv[rows, width + at : width + at + 2 * head_dim]
            value = qkv[rows, 2 * width + at : 2 * width + at + 2 * head_dim]
            grad = mixed[rows, span]
            d_query, d_key, d_value = [], [], []
            for h in range(2):
                prob = probs[s, 2 * pair + h]
                d_prob = dot(only(grad, h == 0), value, (1, 1))
                d_value.append(dot(prob.astype(b16), grad, (0, 0)))
                delta = jnp.sum(prob * d_prob, axis=-1, keepdims=True)
                d_score = (prob * (d_prob - delta) * score_scale).astype(b16)
                d_query.append(dot(d_score, key))
                d_key.append(dot(d_score, query, (0, 0)))
            d_query = jnp.where(lower, d_query[0], d_query[1]).astype(b16)
            d_key = jnp.where(lower, d_key[0], d_key[1]).astype(b16)
            d_value = jnp.where(lower, d_value[0], d_value[1]).astype(b16)
            dqkv[rows, span] = d_query
            dqkv[rows, width + at : width + at + 2 * head_dim] = d_key
            dqkv[rows, 2 * width + at : 2 * width + at + 2 * head_dim] = d_value
            gbias_ref[:, o_query + at : o_query + at + 2 * head_dim] += column_sum(d_query.astype(f32))
            gbias_ref[:, o_value + at : o_value + at + 2 * head_dim] += column_sum(d_value.astype(f32))

    slot_loop(attend_back)
    for k in range(3):
        cols = slice(k * width, (k + 1) * width)
        g_qkv[:, cols] = dot(h_one[...], dqkv[:, cols], (0, 0)).astype(g_qkv.dtype)
    back[...] = dot(dqkv[...], w_qkv[...], (1, 1))

    def attn_back(s, rows):
        grad_one = back[rows, :]
        normed = norm_one[rows, :]
        dmod[pl.ds(s, 1), width : 2 * width] = column_sum(grad_one * normed)
        dmod[pl.ds(s, 1), :width] = column_sum(grad_one)
        gx_ref[s] = dx[rows, :] + norm_backward(
            grad_one * (1.0 + part(s, 1)), normed, inv_one[rows, :]
        )

    slot_loop(attn_back)
    gbias_ref[:, : 6 * width] = column_sum(dmod[...])
    grad_mod = dmod[...].astype(b16)
    store_matrix(g_qkv, g_attn, 0)
    store_matrix(g_proj, g_attn, proj_top)
    store_matrix(g_one, g_mlp, 0)
    store_matrix(g_two, g_mlp, two_top)
    act_ref[...] = cond_act
    dmod_ref[...] = grad_mod
    gcond_ref[...] = dot(grad_mod, w_ada[...], (1, 1)) * silu_slope(cond)


def run_block(counts, latents, conditioning, cotangent, weights, biases):
    slots, length, width = latents.shape
    w_ada, attn, mlp = weights
    hidden = mlp.size // (2 * width)
    rows = slots * length
    f32, b16 = jnp.float32, jnp.bfloat16
    outs = [
        (latents.shape, f32), (latents.shape, f32), (conditioning.shape, f32),
        (conditioning.shape, b16), ((slots, 6 * width), b16),
        (attn.shape, b16), (mlp.shape, b16), (biases.shape, f32),
    ]
    matrices = [(width, 3 * width), (width, width), (width, hidden), (hidden, width)]
    scratch = [((max(h * w for h, w in matrices) // LANES, LANES), f32)]
    scratch += [(shape, b16) for shape in matrices + matrices]
    scratch += [
        ((slots, 6 * width), f32), ((rows, width), f32), ((rows, 1), f32), ((rows, width), b16),
        ((rows, 3 * width), b16), ((slots, HEADS, length, length), f32), ((rows, width), b16),
        ((rows, width), f32), ((rows, width), f32), ((rows, 1), f32), ((rows, width), b16),
        ((rows, hidden), f32), ((rows, hidden), b16), ((rows, width), f32), ((rows, hidden), b16),
        ((rows, width), f32), ((rows, width), f32), ((rows, width), b16), ((rows, 3 * width), b16),
        ((slots, 6 * width), f32),
    ]
    vmem = pl.BlockSpec(memory_space=pltpu.VMEM)
    return pl.pallas_call(
        block_kernel,
        out_shape=[jax.ShapeDtypeStruct(shape, kind) for shape, kind in outs],
        in_specs=[pl.BlockSpec(memory_space=pltpu.SMEM)] + [vmem] * 7,
        out_specs=[vmem] * len(outs),
        scratch_shapes=[pltpu.VMEM(shape, kind) for shape, kind in scratch],
        compiler_params=pltpu.CompilerParams(vmem_limit_bytes=60 * 1024 * 1024),
    )(counts, latents, conditioning, cotangent, *weights, biases)


class Flow:
    def __init__(self):
        self.steps = []

    def add(self, name, action):
        self.steps.append((name, action))

    def tick(self, count=1):
        for _ in range(count):
            if self.steps:
                self.steps.pop(0)[1]()

    def until(self, name):
        while any(n == name for n, _ in self.steps):
            self.tick()


class Share:
    def __init__(self, mover, ref, start, size, low_first):
        self.mover, self.ref, self.rows, self.low_first = mover, ref, pl.ds(start, size), low_first
        self.swap = []

    def begin(self):
        hi, lo, z, c = self.mover.here
        self.pending = self.mover.pushes(self.ref.at[hi, lo, z, c, self.rows], 2)

    def first(self):
        hi, lo, z, c = self.mover.here
        arrive(self.pending)
        part = self.ref.at[hi, lo, :, c, self.rows]
        self.pending = self.mover.pushes(part, 1 if self.low_first else 0)
        self.swap += self.mover.pushes(part, 3)

    def second(self):
        hi, lo, z, c = self.mover.here
        arrive(self.pending)
        ref, rows = self.ref, self.rows
        if self.low_first:
            self.pending = self.mover.pushes(ref.at[hi, :, :, c, rows], 0)
            others = [ref.at[hi, spot[1], :, c, rows] for spot in self.mover.spots(1)]
        else:
            self.pending = self.mover.pushes(ref.at[:, lo, :, c, rows], 1)
            others = [ref.at[spot[0], lo, :, c, rows] for spot in self.mover.spots(0)]
        for other in others:
            self.swap += self.mover.pushes(other, 3)

    def third(self):
        hi, lo, z, c = self.mover.here
        arrive(self.pending)
        ref, rows = self.ref, self.rows
        if self.low_first:
            others = [ref.at[spot[0], :, :, c, rows] for spot in self.mover.spots(0)]
        else:
            others = [ref.at[:, spot[1], :, c, rows] for spot in self.mover.spots(1)]
        for other in others:
            self.swap += self.mover.pushes(other, 3)

    def end(self):
        arrive(self.swap)


class Reduce:
    def __init__(self, mover, bufs, start, size, even):
        self.mover, self.even = mover, even
        self.grad, self.pair, self.acc, self.one_buf, self.two_buf, self.line_buf, self.total = bufs
        self.start, self.size, self.rows = start, size, pl.ds(start, size)

    def steps(self, axis):
        grid, here = self.mover.grid, self.mover.here
        return [(s - 1, grid.peer(here, axis, s)) for s in range(1, grid.sizes[axis])]

    def begin(self):
        self.pending = [
            self.mover.push(self.grad.at[:, :, :, spot[3], self.rows], self.pair.at[:, :, :, self.rows], spot)
            for _, spot in self.steps(3)
        ]

    def add(self, into, terms, first, second):
        def body(i, _):
            for j in range(second):
                total = terms[0](i, j)[...]
                for term in terms[1:]:
                    total = total + term(i, j)[...]
                into(i, j)[...] = total
            return 0

        lax.fori_loop(0, first, body, 0)

    def one(self):
        high, low, depth, pair = self.mover.grid.sizes
        c, rows = self.mover.here[3], self.rows
        grad, pair_buf, acc, buf, push = self.grad, self.pair, self.acc, self.one_buf, self.mover.push
        arrive(self.pending)
        terms = [lambda i, j: grad.at[i // low, i % low, j, c, rows]]
        if pair > 1:
            terms.append(lambda i, j: pair_buf.at[i // low, i % low, j, rows])
        self.add(lambda i, j: acc.at[i // low, i % low, j, rows], terms, high * low, depth)
        if self.even:
            self.pending = [
                push(acc.at[spot[0], :, :, rows], buf.at[s, 0:low, :, rows], spot) for s, spot in self.steps(0)
            ]
        else:
            self.pending = [
                push(acc.at[:, spot[1], :, rows], buf.at[s, 0:high, :, rows], spot) for s, spot in self.steps(1)
            ]

    def two(self):
        high, low, depth, pair = self.mover.grid.sizes
        hi, lo, z, c = self.mover.here
        rows, acc, one, buf, push = self.rows, self.acc, self.one_buf, self.two_buf, self.mover.push
        arrive(self.pending)
        mine = (lambda i, j: acc.at[hi, i, j, rows]) if self.even else (lambda i, j: acc.at[i, lo, j, rows])
        terms = [mine] + [
            (lambda i, j, s=s: one.at[s, i, j, rows]) for s, _ in self.steps(0 if self.even else 1)
        ]
        self.add(mine, terms, low if self.even else high, depth)
        if self.even:
            self.pending = [
                push(acc.at[hi, spot[1], :, rows], buf.at[s, :, rows], spot) for s, spot in self.steps(1)
            ]
        else:
            self.pending = [
                push(acc.at[spot[0], lo, :, rows], buf.at[s, :, rows], spot) for s, spot in self.steps(0)
            ]

    def three(self):
        depth = self.mover.grid.sizes[2]
        hi, lo, z, c = self.mover.here
        rows, acc, two, buf, push = self.rows, self.acc, self.two_buf, self.line_buf, self.mover.push
        arrive(self.pending)
        mine = lambda i, j: acc.at[hi, lo, j, rows]
        terms = [mine] + [
            (lambda i, j, s=s: two.at[s, j, rows]) for s, _ in self.steps(1 if self.even else 0)
        ]
        self.add(mine, terms, 1, depth)
        self.pending = [
            push(acc.at[hi, lo, spot[2], rows], buf.at[s, rows], spot) for s, spot in self.steps(2)
        ]

    def finish(self):
        depth = self.mover.grid.sizes[2]
        hi, lo, z, c = self.mover.here
        arrive(self.pending)
        total = self.acc[hi, lo, z, self.rows].astype(jnp.float32)
        for s in range(depth - 1):
            total = total + self.line_buf[s, self.rows].astype(jnp.float32)
        self.total[self.rows, :] = total


class Sizes:
    def __init__(self, grid, latents, shards):
        ada, attn, mlp, bias = (shard.shape[0] for shard in shards)
        self.slots, self.length, width = latents.shape
        self.width, self.bias = width, bias
        self.hidden = mlp * grid.count // (2 * width)
        self.parts = self.hidden // width
        self.ada_rows, self.qkv_rows = ada // (6 * width), attn // (3 * width)
        self.attn_rows, self.one_rows, self.mlp_rows = attn // width, mlp // self.hidden, mlp // width
        self.qkv_devices, self.one_devices = 3 * width * width // attn, width * self.hidden // mlp
        self.lead = 2 * SUBLANES - (2 * self.ada_rows) % (2 * SUBLANES)
        self.head_rows = self.lead + 2 * self.ada_rows
        self.tail_rows = 4 * self.ada_rows
        group = grid.depth * grid.pair
        exact = (
            self.hidden == self.parts * width, ada == self.ada_rows * 6 * width, attn == self.qkv_rows * 3 * width,
            mlp == self.one_rows * self.hidden, mlp == self.mlp_rows * width,
            self.qkv_devices * attn == 3 * width * width, self.one_devices * mlp == width * self.hidden,
        )
        whole = (
            self.qkv_rows % SUBLANES, (2 * self.one_rows) % SUBLANES, self.one_rows % 8, self.tail_rows % SUBLANES,
            self.qkv_devices % group, self.one_devices % group, width % LANES, (4 * self.slots) % SUBLANES,
            (2 * self.slots + 4 + self.parts) % SUBLANES, self.parts % grid.pair, self.mlp_rows % SUBLANES,
            (self.length % LANES), (2 * self.width // HEADS) % LANES,
        )
        per_tile = width // self.mlp_rows if width % self.mlp_rows == 0 else 0
        self.fits = (
            all(exact) and not any(whole) and grid.pair == 2 and self.slots < self.lead and bias <= 2 * LANES
            and bias <= width and per_tile > 0 and per_tile % grid.pair == 0 and group % per_tile == 0
            and grid.count * bias == (9 + self.parts + 1) * width and grid.high * grid.low * group == grid.count
        )


def fused_kernel(
    grid, sizes, count_ref, x_hbm, cond_ref, cot_hbm, ada_ref, attn_ref, mlp_ref, bias_ref,
    out_hbm, gx_hbm, gcond_ref, g_ada_out, g_attn_out, g_mlp_out, g_bias_out,
    all_ada, all_attn, all_mlp, note_a, note_b, grad_attn, grad_mlp,
    pair_attn, pair_mlp, acc_attn, acc_mlp, one_attn, one_mlp, two_attn, two_mlp, line_attn, line_mlp,
    sum_attn, sum_mlp, swap_out, swap_in, back_in,
    x_ref, cot_ref, out_ref, gx_ref, line, unit, local_rows, pick_head, pick_tail, spread, bias_rows,
    mod, norm_one, inv_one, h_one, qkv, probs, mixed, branch, norm_two, inv_two, h_two,
    slope, act, mlp, wide, back, dx, small, dqkv, dmod, gbias,
    send_sem, recv_sem, own_sem,
):
    mover = Mover(grid, send_sem, recv_sem)
    here = mover.here
    hi, lo, z, c = here
    high, low, depth, pair = grid.sizes
    me = ((hi * low + lo) * depth + z) * pair + c
    slots, length, width, hidden = sizes.slots, sizes.length, sizes.width, sizes.hidden
    rows_all = slots * length
    heads = probs.shape[1]
    head_dim = width // heads
    score_scale = head_dim ** (-0.5)
    f32, b16 = jnp.float32, jnp.bfloat16
    count = count_ref[0]
    parts, tiles = sizes.parts, width // LANES
    ada_rows, lead, head_rows, tail_rows = sizes.ada_rows, sizes.lead, sizes.head_rows, sizes.tail_rows
    group = depth * pair

    x_in = pltpu.make_async_copy(x_hbm, x_ref, own_sem.at[0])
    cot_in = pltpu.make_async_copy(cot_hbm, cot_ref, own_sem.at[1])
    x_in.start()
    cot_in.start()

    def strided(start, rows, stride):
        return line[pl.ds(start, rows, stride=stride), :]

    def lanes(t):
        return slice(t * LANES, (t + 1) * LANES)

    def column_sum(values):
        return jnp.sum(values, axis=0, keepdims=True)

    cond = cond_ref[...]
    cond_act = (cond * jax.nn.sigmoid(cond)).astype(b16)
    line[0 : ada_ref.shape[0], :] = ada_ref[...].astype(f32)
    unit[0:lead, :] = jnp.zeros((lead, width), f32)
    for k in range(6):
        for t in range(tiles):
            unit[lead + ada_rows * k : lead + ada_rows * (k + 1), lanes(t)] = strided(
                tiles * k + t, ada_rows, 6 * tiles
            )
    for t in range(bias_ref.shape[0]):
        unit[0:1, lanes(t)] = bias_ref[t : t + 1, :].astype(f32)
    unit[1 : 1 + slots, :] = cond_act.astype(f32)
    all_ada[hi, lo, z, c] = unit[0 : head_rows + tail_rows, :].astype(b16)

    def halves(ref, start, size, flip):
        cut = size // (2 * SUBLANES) * SUBLANES
        if flip:
            cut = size - cut
        return [Share(mover, ref, start, cut, True), Share(mover, ref, start + cut, size - cut, False)]

    mlp_half = sizes.mlp_rows // 2
    shares = {
        "a": halves(all_ada, 0, head_rows, False),
        "b": halves(all_attn, 0, sizes.attn_rows, False),
        "c": halves(all_ada, head_rows, tail_rows, True),
        "d": halves(all_mlp, 0, mlp_half, False),
        "e": halves(all_mlp, mlp_half, sizes.mlp_rows - mlp_half, True),
    }
    flow = Flow()

    def stage(key, name):
        def action():
            for share in shares[key]:
                getattr(share, name)()

        flow.add(key + name, action)

    grid.barrier(here)
    order = "abcde"
    names = ("begin", "first", "second", "third", "end")
    for share in shares["a"]:
        share.begin()

    line[0 : attn_ref.shape[0], :] = attn_ref[...].astype(f32)

    @pl.when(me < sizes.qkv_devices)
    def _():
        rows = sizes.qkv_rows
        for k in range(3):
            for t in range(tiles):
                unit[rows * k : rows * (k + 1), lanes(t)] = strided(tiles * k + t, rows, 3 * tiles)

    @pl.when(me >= sizes.qkv_devices)
    def _():
        for t in range(tiles):
            unit[0 : sizes.attn_rows, lanes(t)] = strided(t, sizes.attn_rows, tiles)

    all_attn[hi, lo, z, c] = unit[0 : sizes.attn_rows, :].astype(b16)
    for share in shares["b"]:
        share.begin()

    one_rows, per_core = sizes.one_rows, parts // pair
    line[0 : mlp_ref.shape[0], :] = mlp_ref[...].astype(f32)

    @pl.when(me < sizes.one_devices)
    def _():
        for k in range(parts):
            for t in range(tiles):
                local_rows[one_rows * k : one_rows * (k + 1), lanes(t)] = strided(
                    tiles * k + t, one_rows, parts * tiles
                )
        for k in range(per_core):
            unit[pl.ds(pl.multiple_of(2 * one_rows * k + one_rows * c, 8), one_rows), :] = local_rows[
                pl.ds(pl.multiple_of(one_rows * (per_core * c + k), 8), one_rows), :
            ]

    @pl.when(me >= sizes.one_devices)
    def _():
        for t in range(tiles):
            unit[0 : sizes.mlp_rows, lanes(t)] = strided(t, sizes.mlp_rows, tiles)
        local_rows[...] = jnp.zeros_like(local_rows)

    cut = one_rows * per_core
    swap_out[...] = local_rows[pl.ds(pl.multiple_of(cut * (1 - c), 8), cut), :].astype(b16)
    partner = grid.peer(here, 3, 1)
    swap = mover.push(swap_out, swap_in, partner)

    def picks(total, span, skip, target):
        at = lax.broadcasted_iota(jnp.int32, (1, total), 1)
        device, row = at // span, at % span - skip
        entry = jnp.where(row >= 0, device * ada_rows + row % ada_rows, -1)
        source = lax.broadcasted_iota(jnp.int32, (width, total), 0)
        target[...] = jnp.where(source == entry, 1.0, 0.0).astype(b16)

    def owner_mask(total, span, skip, blocks):
        at = lax.broadcasted_iota(jnp.int32, (blocks * slots, total), 1)
        block = lax.broadcasted_iota(jnp.int32, (blocks * slots, total), 0) // slots
        row = at % span - skip
        return jnp.logical_and(row >= 0, row // ada_rows == block)

    def spread_cond(pick, total, span, skip, blocks):
        wide_cond = dot(cond_act, pick[...])
        stacked = jnp.concatenate([wide_cond] * blocks, axis=0)
        return jnp.where(owner_mask(total, span, skip, blocks), stacked, 0.0).astype(b16)

    head_total, tail_total = grid.count * head_rows, grid.count * tail_rows

    def norm_first(s):
        rows = slice(s * length, (s + 1) * length)
        normed, inverse = layer_norm(x_ref[s])
        norm_one[rows, :] = normed
        inv_one[rows, :] = inverse

    def part(s, k):
        return mod[k * slots + s : k * slots + s + 1, :]

    for step in range(len(order) + len(names) - 1):
        for k, key in enumerate(order):
            n = step - k
            if 0 <= n < len(names) and not (n == 0 and key in "ab"):
                stage(key, names[n])
    flow.until("afirst")

    picks(head_total, head_rows, lead, pick_head)
    head_cond = spread_cond(pick_head, head_total, head_rows, lead, 2)
    swap.wait_recv()

    @pl.when(me < sizes.one_devices)
    def _():
        local_rows[0:cut, :] = swap_in[...].astype(f32)
        for k in range(per_core):
            unit[pl.ds(pl.multiple_of(2 * one_rows * k + one_rows * (1 - c), 8), one_rows), :] = local_rows[
                one_rows * k : one_rows * (k + 1), :
            ]

    all_mlp[hi, lo, z, c] = unit[0 : sizes.mlp_rows, :].astype(b16)
    flow.until("asecond")
    x_in.wait()
    norm_first(0)
    flow.until("bfirst")
    norm_first(1)
    flow.until("athird")
    norm_first(2)
    norm_first(3) if slots > 3 else None
    for s in range(4, slots):
        norm_first(s)
    flow.until("aend")

    def rows_of(ref, start, size):
        return ref[:, :, :, :, start : start + size, :].reshape(grid.count * size, width)

    mod[0 : 2 * slots, :] = dot(head_cond, rows_of(all_ada, 0, head_rows))

    bias_rows[...] = jnp.zeros_like(bias_rows)
    lane = lax.broadcasted_iota(jnp.int32, (1, width), 1)
    for d in range(grid.count):
        values = all_ada[d // (low * group), d // group % low, d // pair % depth, d % pair, 0:SUBLANES, :].astype(f32)[0:1]
        row, shift = divmod(d * sizes.bias, width)
        turned = pltpu.roll(values, shift, 1) if shift else values
        end = shift + sizes.bias
        bias_rows[row : row + 1, :] += jnp.where(jnp.logical_and(lane >= shift, lane < end), turned, 0.0)
        if end > width:
            bias_rows[row + 1 : row + 2, :] += jnp.where(lane < end - width, turned, 0.0)

    def add_mod_bias(first, last):
        for k in range(first, last):
            span = slice(k * slots, (k + 1) * slots)
            mod[span, :] = mod[span, :] + bias_rows[k : k + 1, :]

    add_mod_bias(0, 2)

    def modulate_first(s):
        rows = slice(s * length, (s + 1) * length)
        h_one[rows, :] = (norm_one[rows, :] * (1.0 + part(s, 1)) + part(s, 0)).astype(b16)

    for s in range(slots):
        modulate_first(s)
    flow.until("bend")

    def devices(ref, first, last, rows):
        pieces = []
        for g in range(first // group, last // group):
            piece = ref[g // low, g % low, :, :, rows, :]
            pieces.append(piece.reshape(group * piece.shape[2], width))
        return pieces[0] if len(pieces) == 1 else jnp.concatenate(pieces, axis=0)

    def qkv_weight(k):
        return devices(all_attn, 0, sizes.qkv_devices, slice(sizes.qkv_rows * k, sizes.qkv_rows * (k + 1)))

    def proj_weight():
        return devices(all_attn, sizes.qkv_devices, grid.count, slice(0, sizes.attn_rows))

    tall = 2 * one_rows

    def one_weight(t):
        core, k = t // per_core, t % per_core
        pieces = [
            all_mlp[g // low, g % low, :, core, tall * k : tall * (k + 1), :].reshape(depth * tall, width)
            for g in range(sizes.one_devices // group)
        ]
        return pieces[0] if len(pieces) == 1 else jnp.concatenate(pieces, axis=0)

    per_tile = width // sizes.mlp_rows

    def two_place(t):
        first = sizes.one_devices + per_tile * t
        g, at = first // group, first % group // pair
        return g // low, g % low, slice(at, at + per_tile // pair)

    def two_weight(t):
        a, b, zs = two_place(t)
        return all_mlp[a, b, zs, :, :, :].reshape(width, width)

    cut_head = 2 * head_dim
    upper = lax.broadcasted_iota(jnp.int32, (length, cut_head), 1) >= head_dim

    def both(block):
        zero = jnp.zeros_like(block)
        return jnp.concatenate([jnp.where(upper, zero, block), jnp.where(upper, block, zero)], axis=0)

    for k, row in enumerate((6, None, 7)):
        value = dot(h_one[...], qkv_weight(k))
        if row is not None:
            value = value + bias_rows[row : row + 1, :]
        qkv[:, k * width : (k + 1) * width] = value.astype(b16)
    flow.until("csecond")

    def attend(s):
        rows = slice(s * length, (s + 1) * length)
        for p in range(heads // 2):
            at = p * cut_head
            query = qkv[rows, at : at + cut_head]
            key = qkv[rows, width + at : width + at + cut_head]
            value = qkv[rows, 2 * width + at : 2 * width + at + cut_head]
            scores = dot(both(query), key, (1, 1)) * score_scale
            total = jnp.log(jnp.sum(jnp.exp(scores), axis=-1, keepdims=True))
            prob = jnp.exp(scores - total)
            probs[s, 2 * p] = prob[:length]
            probs[s, 2 * p + 1] = prob[length:]
            prob = prob.astype(b16)
            side = jnp.concatenate([prob[:length], prob[length:]], axis=1)
            mixed[rows, at : at + cut_head] = dot(side, both(value)).astype(b16)

    for s in range(slots):
        attend(s)
        flow.tick(1)
    picks(tail_total, tail_rows, 0, pick_tail)
    tail_cond = spread_cond(pick_tail, tail_total, tail_rows, 0, 4)
    branch[...] = dot(mixed[...], proj_weight()) + bias_rows[8:9, :]
    flow.until("cend")
    mod[2 * slots :, :] = dot(tail_cond, rows_of(all_ada, head_rows, tail_rows))
    add_mod_bias(2, 6)

    def norm_second(s):
        rows = slice(s * length, (s + 1) * length)
        after = x_ref[s] + part(s, 2) * branch[rows, :]
        dx[rows, :] = after
        normed, inverse = layer_norm(after)
        norm_two[rows, :] = normed
        inv_two[rows, :] = inverse
        h_two[rows, :] = (normed * (1.0 + part(s, 4)) + part(s, 3)).astype(b16)

    for s in range(slots):
        norm_second(s)
        flow.tick(1)

    note_rows = note_a.shape[4]
    own_lane = lax.broadcasted_iota(jnp.int32, (SUBLANES, width), 1)
    own_row = lax.broadcasted_iota(jnp.int32, (SUBLANES, width), 0)
    own_pick = jnp.where(own_lane == own_row + me * ada_rows, 1.0, 0.0).astype(b16)
    columns = dot(own_pick, rows_of(all_ada, 0, head_rows), (1, 1)).astype(b16)
    note_total = grid.count * note_rows
    at = lax.broadcasted_iota(jnp.int32, (1, note_total), 1)
    wanted = at // note_rows * head_rows + 1 + at % note_rows % slots
    source = lax.broadcasted_iota(jnp.int32, (head_total, note_total), 0)
    spread[...] = dot(columns, jnp.where(source == wanted, 1.0, 0.0).astype(b16)).astype(b16)

    def up(t):
        cols = slice(t * width, (t + 1) * width)
        pre = dot(h_two[...], one_weight(t)) + bias_rows[9 + t : 10 + t, :]
        square = pre * pre
        tanh_part = jnp.tanh(ROOT_TWO_OVER_PI * (pre + GELU_COEF * pre * square))
        half = 0.5 * (1.0 + tanh_part)
        act[:, cols] = (pre * half).astype(b16)
        slope[:, cols] = half + 0.5 * pre * (1.0 - tanh_part * tanh_part) * ROOT_TWO_OVER_PI * (
            1.0 + 3.0 * GELU_COEF * square
        )

    flow.until("dend")
    for k in range(per_core):
        if k == 1:
            flow.until("eend")
        for core in range(pair):
            up(core * per_core + k)
            flow.tick(1)
    flow.until("eend")
    two_all = jnp.concatenate([two_weight(t) for t in range(parts)], axis=0)
    mlp[...] = dot(act[...], two_all) + bias_rows[9 + parts : 10 + parts, :]

    gbias[...] = jnp.zeros_like(gbias)
    last = gbias.shape[0] - 1
    cot_in.wait()

    def finish(s):
        rows = slice(s * length, (s + 1) * length)
        live = s < count
        value = mlp[rows, :]
        out_ref[s] = jnp.where(live, dx[rows, :] + part(s, 5) * value, 0.0)
        grad = jnp.where(live, cot_ref[s], 0.0)
        cot_ref[s] = grad
        dmod[5 * slots + s : 5 * slots + s + 1, :] = column_sum(grad * value)
        full = grad * part(s, 5)
        gbias[last : last + 1, :] += column_sum(full)
        small[rows, :] = full.astype(b16)

    for s in range(slots):
        finish(s)
    out_copy = pltpu.make_async_copy(out_ref, out_hbm, own_sem.at[2])
    out_copy.start()

    def reduces(bufs, start, size, flip):
        return [Reduce(mover, bufs, start, size, not flip)]

    bufs_mlp = (grad_mlp, pair_mlp, acc_mlp, one_mlp, two_mlp, line_mlp, sum_mlp)
    bufs_attn = (grad_attn, pair_attn, acc_attn, one_attn, two_attn, line_attn, sum_attn)
    shares["n"] = [Share(mover, note_a, 0, note_rows, True)]
    shares["m"] = [Share(mover, note_b, 0, note_rows, False)]
    shares["f"] = reduces(bufs_mlp, 0, mlp_half, False)
    shares["g"] = reduces(bufs_mlp, mlp_half, sizes.mlp_rows - mlp_half, True)
    attn_cut = sizes.attn_rows // (2 * SUBLANES) * SUBLANES
    shares["h"] = reduces(bufs_attn, 0, attn_cut, False)
    shares["i"] = reduces(bufs_attn, attn_cut, sizes.attn_rows - attn_cut, True)

    for t in range(parts):
        cols = slice(t * width, (t + 1) * width)
        full = dot(small[...], two_weight(t), (1, 1)) * slope[:, cols]
        gbias[3 + t : 4 + t, :] = column_sum(full)
        grad = full.astype(b16)
        wide[:, cols] = grad
        a, b, zs = two_place(t)
        grad_mlp[a, b, zs, :, :, :] = (
            dot(act[:, cols], small[...], (0, 0)).astype(b16).reshape(per_tile // pair, pair, sizes.mlp_rows, width)
        )
        core, k = t // per_core, t % per_core
        whole = dot(h_two[...], grad, (0, 0)).astype(b16)
        for g in range(sizes.one_devices // group):
            grad_mlp[g // low, g % low, :, core, tall * k : tall * (k + 1), :] = whole[
                g * depth * tall : (g + 1) * depth * tall
            ].reshape(depth, tall, width)

    for key in "fg":
        for reduce in shares[key]:
            reduce.begin()
    for name in ("one", "two", "three", "finish"):
        for key in "fg":
            stage(key, name)
    one_all = jnp.concatenate([one_weight(t) for t in range(parts)], axis=1)
    back[...] = dot(wide[...], one_all, (1, 1))
    flow.tick(1)

    def mlp_back(s):
        rows = slice(s * length, (s + 1) * length)
        grad_two = back[rows, :]
        normed = norm_two[rows, :]
        dmod[4 * slots + s : 4 * slots + s + 1, :] = column_sum(grad_two * normed)
        dmod[3 * slots + s : 3 * slots + s + 1, :] = column_sum(grad_two)
        after = cot_ref[s] + norm_backward(grad_two * (1.0 + part(s, 4)), normed, inv_two[rows, :])
        dx[rows, :] = after
        dmod[2 * slots + s : 2 * slots + s + 1, :] = column_sum(after * branch[rows, :])
        full = after * part(s, 2)
        gbias[2:3, :] += column_sum(full)
        small[rows, :] = full.astype(b16)

    for s in range(slots):
        mlp_back(s)
        if s == 0:
            flow.tick(1)
    note_a[hi, lo, z, c] = dmod[2 * slots :, :].astype(b16)
    for name in names:
        stage("n", name)
    whole = dot(mixed[...], small[...], (0, 0)).astype(b16)
    for g in range(sizes.qkv_devices // group, grid.count // group):
        base = (g * group - sizes.qkv_devices) * sizes.attn_rows
        grad_attn[g // low, g % low] = whole[base : base + group * sizes.attn_rows].reshape(
            depth, pair, sizes.attn_rows, width
        )
    mixed[...] = dot(small[...], proj_weight(), (1, 1)).astype(b16)

    def attend_back(s):
        rows = slice(s * length, (s + 1) * length)
        for p in range(heads // 2):
            at = p * cut_head
            span = slice(at, at + cut_head)
            query = qkv[rows, span]
            key = qkv[rows, width + at : width + at + cut_head]
            value = qkv[rows, 2 * width + at : 2 * width + at + cut_head]
            grad = both(mixed[rows, span])
            prob = jnp.concatenate([probs[s, 2 * p], probs[s, 2 * p + 1]], axis=0)
            d_prob = dot(grad, value, (1, 1))
            d_value = dot(prob.astype(b16), grad, (0, 0)).astype(b16)
            delta = jnp.sum(prob * d_prob, axis=-1, keepdims=True)
            d_score = (prob * (d_prob - delta) * score_scale).astype(b16)
            side = jnp.concatenate([d_score[:length], d_score[length:]], axis=1)
            d_query = dot(side, both(key)).astype(b16)
            d_key = dot(d_score, both(query), (0, 0)).astype(b16)
            dqkv[rows, span] = d_query
            dqkv[rows, width + at : width + at + cut_head] = d_key
            dqkv[rows, 2 * width + at : 2 * width + at + cut_head] = d_value
            gbias[0:1, span] += column_sum(d_query.astype(f32))
            gbias[1:2, span] += column_sum(d_value.astype(f32))

    for s in range(slots):
        attend_back(s)
        flow.tick(2)
    for k in range(3):
        cols = slice(k * width, (k + 1) * width)
        whole = dot(h_one[...], dqkv[:, cols], (0, 0)).astype(b16)
        for g in range(sizes.qkv_devices // group):
            base = g * group * sizes.qkv_rows
            grad_attn[g // low, g % low, :, :, sizes.qkv_rows * k : sizes.qkv_rows * (k + 1), :] = whole[
                base : base + group * sizes.qkv_rows
            ].reshape(depth, pair, sizes.qkv_rows, width)
    for key in "hi":
        for reduce in shares[key]:
            reduce.begin()
    back[...] = dot(dqkv[:, 0:width], qkv_weight(0), (1, 1)) + (
        dot(dqkv[:, width : 2 * width], qkv_weight(1), (1, 1)) + dot(dqkv[:, 2 * width :], qkv_weight(2), (1, 1))
    )
    for key in "hi":
        stage(key, "one")
    flow.until("ione")

    def attn_back(s):
        rows = slice(s * length, (s + 1) * length)
        grad_one = back[rows, :]
        normed = norm_one[rows, :]
        dmod[slots + s : slots + s + 1, :] = column_sum(grad_one * normed)
        dmod[s : s + 1, :] = column_sum(grad_one)
        gx_ref[s] = dx[rows, :] + norm_backward(grad_one * (1.0 + part(s, 1)), normed, inv_one[rows, :])

    for s in range(slots):
        attn_back(s)
    note_b[hi, lo, z, c] = jnp.concatenate([dmod[0 : 2 * slots, :], gbias[...]], axis=0).astype(b16)
    for share in shares["m"]:
        share.begin()
    gx_copy = pltpu.make_async_copy(gx_ref, gx_hbm, own_sem.at[3])
    gx_copy.start()
    stage("h", "two"), stage("m", "first"), stage("i", "two")
    stage("h", "three"), stage("m", "second"), stage("i", "three"), stage("m", "third")

    def gather_entries(first, blocks, start, rows, total, span, skip, pick):
        grad_mod = dmod[first * slots : (first + blocks) * slots, :].astype(b16)
        values = dot(grad_mod, rows_of(all_ada, start, rows), (1, 1))
        values = jnp.where(owner_mask(total, span, skip, blocks), values, 0.0)
        merged = values[0:slots]
        for k in range(1, blocks):
            merged = merged + values[k * slots : (k + 1) * slots]
        upper_part = merged.astype(b16)
        lower_part = (merged - upper_part.astype(f32)).astype(b16)
        return dot(upper_part, pick[...], (1, 1)) + dot(lower_part, pick[...], (1, 1))

    flow.tick(2)
    grad_act = gather_entries(0, 2, 0, head_rows, head_total, head_rows, lead, pick_head)
    grad_act = grad_act + gather_entries(2, 4, head_rows, tail_rows, tail_total, tail_rows, 0, pick_tail)
    gcond_ref[...] = grad_act * silu_slope(cond)
    flow.until("mthird")

    def from_notes(note, blocks, extra):
        kept = []
        entry = lax.broadcasted_iota(jnp.int32, (SUBLANES, note_total), 1) % note_rows
        for k in range(blocks):
            kept.append(jnp.where(entry // slots == k, spread[...].astype(f32), 0.0))
        line_at = lax.broadcasted_iota(jnp.int32, (SUBLANES, note_total), 0)
        wanted = jnp.where(entry < blocks * slots, entry // slots, entry - blocks * slots + blocks)
        kept.append(jnp.where(wanted == line_at, 1.0, 0.0))
        left = jnp.concatenate(kept, axis=0).astype(b16)
        return dot(left, rows_of(note, 0, note_rows))

    for share in shares["m"]:
        share.end()
    late = from_notes(note_b, 2, gbias.shape[0])
    early = from_notes(note_a, 4, 0)
    for k in range(6):
        source, base = (late, k * SUBLANES) if k < 2 else (early, (k - 2) * SUBLANES)
        for t in range(tiles):
            g_ada_out[pl.ds(tiles * k + t, ada_rows, stride=6 * tiles), :] = source[
                base : base + ada_rows, lanes(t)
            ]
    bias_rows[0:2, :] = late[2 * SUBLANES : 2 * SUBLANES + 2]
    bias_rows[2:6, :] = early[4 * SUBLANES : 4 * SUBLANES + 4]
    bias_rows[6 : 6 + gbias.shape[0], :] = late[2 * SUBLANES + 2 : 2 * SUBLANES + 2 + gbias.shape[0]]
    begin = me * sizes.bias
    row, shift = begin // width, begin % width
    pair_rows = jnp.concatenate(
        [bias_rows[pl.ds(row, 1), :], bias_rows[pl.ds(row + 1, 1), :]], axis=1
    )
    turned = pltpu.roll(pair_rows, 2 * width - shift, 1)
    for t in range(g_bias_out.shape[0]):
        g_bias_out[t : t + 1, :] = turned[:, lanes(t)]

    home = [
        mover.push(
            sum_mlp.at[pl.ds(pl.multiple_of(tall * k + one_rows * (1 - c), 8), one_rows)], back_in.at[k], partner
        )
        for k in range(per_core)
    ]
    stage("h", "finish"), stage("i", "finish")
    flow.until("ifinish")

    @pl.when(me < sizes.qkv_devices)
    def _():
        rows = sizes.qkv_rows
        for k in range(3):
            for t in range(tiles):
                g_attn_out[pl.ds(tiles * k + t, rows, stride=3 * tiles), :] = sum_attn[rows * k : rows * (k + 1), lanes(t)]

    @pl.when(me >= sizes.qkv_devices)
    def _():
        for t in range(tiles):
            g_attn_out[pl.ds(t, sizes.attn_rows, stride=tiles), :] = sum_attn[:, lanes(t)]

    arrive(home)
    for core in range(pair):
        @pl.when(jnp.logical_and(me < sizes.one_devices, c == core))
        def _():
            for k in range(per_core):
                for t in range(tiles):
                    own_at, far_at = per_core * core + k, per_core * (1 - core) + k
                    base = tall * k + one_rows * core
                    g_mlp_out[pl.ds(tiles * own_at + t, one_rows, stride=parts * tiles), :] = sum_mlp[
                        base : base + one_rows, lanes(t)
                    ]
                    g_mlp_out[pl.ds(tiles * far_at + t, one_rows, stride=parts * tiles), :] = back_in[k, :, lanes(t)]

    @pl.when(me >= sizes.one_devices)
    def _():
        for t in range(tiles):
            g_mlp_out[pl.ds(t, sizes.mlp_rows, stride=tiles), :] = sum_mlp[:, lanes(t)]

    out_copy.wait()
    gx_copy.wait()
    mover.drain()


def run_fused(grid, sizes, counts, latents, conditioning, cotangent, shards, bias):
    slots, length, width, hidden = sizes.slots, sizes.length, sizes.width, sizes.hidden
    high, low, depth, pair = grid.sizes
    f32, b16 = jnp.float32, jnp.bfloat16
    rows = slots * length
    ada, attn, mlp = (shard.reshape(-1, LANES) for shard in shards)
    attn_rows, mlp_rows, one_rows = sizes.attn_rows, sizes.mlp_rows, sizes.one_rows
    ada_all = sizes.head_rows + sizes.tail_rows
    note_rows = 4 * slots
    extra = 4 + sizes.parts
    per_core = sizes.parts // pair
    side = max(high, low)
    tails = [(attn_rows, width), (mlp_rows, width)]
    leads = [
        (high, low, depth), (high, low, depth), (max(side - 1, 1), side, depth),
        (max(side - 1, 1), depth), (max(depth - 1, 1),),
    ]
    scratch = [(grid.sizes + (n, width), b16) for n in (ada_all, attn_rows, mlp_rows, note_rows, note_rows)]
    scratch += [(grid.sizes + tail, b16) for tail in tails]
    scratch += [(lead + tail, b16) for lead in leads for tail in tails]
    scratch += [(tail, f32) for tail in tails]
    cut = per_core * one_rows
    scratch += [((cut, width), b16), ((cut, width), b16), ((per_core, one_rows, width), f32)]
    scratch += [(latents.shape, f32)] * 4
    scratch += [
        ((max(ada.shape[0], attn.shape[0], mlp.shape[0]), LANES), f32), ((max(mlp_rows, attn_rows, ada_all), width), f32),
        ((sizes.parts * one_rows, width), f32),
        ((width, grid.count * sizes.head_rows), b16), ((width, grid.count * sizes.tail_rows), b16),
        ((SUBLANES, grid.count * note_rows), b16), ((-(-(7 + extra) // 8) * 8, width), f32),
    ]
    scratch += [
        ((6 * slots, width), f32), ((rows, width), f32), ((rows, 1), f32), ((rows, width), b16),
        ((rows, 3 * width), b16), ((slots, HEADS, length, length), f32), ((rows, width), b16),
        ((rows, width), f32), ((rows, width), f32), ((rows, 1), f32), ((rows, width), b16),
        ((rows, hidden), f32), ((rows, hidden), b16), ((rows, width), f32), ((rows, hidden), b16),
        ((rows, width), f32), ((rows, width), f32), ((rows, width), b16), ((rows, 3 * width), b16),
        ((6 * slots, width), f32), ((extra, width), f32),
    ]
    copies = 12 * Spread.copies(grid) + 4 * (high + low + depth + pair - 4) + 1 + per_core
    vmem, anywhere = pl.BlockSpec(memory_space=pltpu.VMEM), pl.BlockSpec(memory_space=pl.ANY)
    outs = [
        (latents.shape, f32), (latents.shape, f32), (conditioning.shape, f32),
        (ada.shape, f32), (attn.shape, f32), (mlp.shape, f32), (bias.shape, f32),
    ]
    return pl.pallas_call(
        partial(fused_kernel, grid, sizes),
        out_shape=[jax.ShapeDtypeStruct(shape, kind) for shape, kind in outs],
        in_specs=[pl.BlockSpec(memory_space=pltpu.SMEM), anywhere, vmem, anywhere, vmem, vmem, vmem, vmem],
        out_specs=[anywhere, anywhere, vmem, vmem, vmem, vmem, vmem],
        scratch_shapes=[pltpu.VMEM(shape, kind) for shape, kind in scratch]
        + [pltpu.SemaphoreType.DMA((copies,)), pltpu.SemaphoreType.DMA((copies,)), pltpu.SemaphoreType.DMA((4,))],
        compiler_params=pltpu.CompilerParams(
            collective_id=2, has_side_effects=True, vmem_limit_bytes=60 * 1024 * 1024
        ),
    )(counts, latents, conditioning, cotangent, ada, attn, mlp, bias)


def local(
    grid, latents, conditioning, counts, cotangent, ada_weights, attn_weights, mlp_weights, flat_biases
):
    model_width = latents.shape[-1]
    slots = latents.shape[0]
    shards = (ada_weights, attn_weights, mlp_weights, flat_biases)
    sizes = Sizes(grid, latents, shards)
    if sizes.fits:
        outs = run_fused(
            grid, sizes, counts, latents, conditioning, cotangent, shards[:3], pack([flat_biases], ())
        )
        return tuple(outs[:3]) + tuple(
            total.reshape(-1)[: shard.shape[0]] for total, shard in zip(outs[3:], shards)
        )
    whole_ada, whole_attn, whole_mlp, whole_bias = gather_all(
        grid, [pack([shard], ()) for shard in shards]
    )
    bias_flat = whole_bias.reshape(grid.count, -1)[:, : flat_biases.shape[0]].reshape(-1)
    weights = (
        whole_ada.reshape(model_width, 6 * model_width),
        whole_attn.reshape(-1, LANES),
        whole_mlp.reshape(-1, LANES),
    )
    biases = bias_flat.astype(jnp.float32)[None]
    output, grad_latents, grad_conditioning, cond_act, grad_mod, g_attn, g_mlp, g_bias = (
        run_block(counts, latents, conditioning, cotangent, weights, biases)
    )

    gap = padded_rows(flat_biases.shape[0]) * LANES - flat_biases.shape[0]
    bias_lines = jnp.pad(
        g_bias.astype(jnp.bfloat16).reshape(grid.count, -1), ((0, 0), (0, gap))
    )
    all_mod, all_act, *sums = scatter_sum(
        grid,
        [flat.reshape(grid.sizes + (-1, LANES)) for flat in (g_attn, g_mlp, bias_lines)],
        [grad_mod, cond_act],
    )
    all_mod = all_mod.reshape(grid.count * slots, -1)
    all_act = all_act.reshape(grid.count * slots, -1)
    grads = [own_rows(all_act, all_mod, ada_weights.shape[0])]
    grads += [total.reshape(-1)[: shard.shape[0]] for total, shard in zip(sums, shards[1:])]
    return (output, grad_latents, grad_conditioning) + tuple(grads)


def own_rows(left, right, extent):
    wide = right.shape[1]
    start = lax.axis_index(AXES) * extent
    rows = min(-(-extent // wide) + (1 if extent % wide else 0), left.shape[1])
    top = jnp.minimum(start // wide, left.shape[1] - rows)
    part = lax.dynamic_slice_in_dim(left, top, rows, 1)
    whole = dot(part, right, (0, 0)).reshape(-1)
    if rows * wide == extent:
        return whole
    return lax.dynamic_slice_in_dim(whole, start - top * wide, extent, 0)


def solution(mesh):
    in_specs = (
        P(("dp", "fsdp"), None, None),
        P(("dp", "fsdp"), None),
        P(("dp", "fsdp")),
        P(("dp", "fsdp"), None, None),
        P(("dp", "fsdp")),
        P(("dp", "fsdp")),
        P(("dp", "fsdp")),
        P(("dp", "fsdp")),
    )
    out_specs = (
        P(("dp", "fsdp"), None, None),
        P(("dp", "fsdp"), None, None),
        P(("dp", "fsdp"), None),
        P(("dp", "fsdp")),
        P(("dp", "fsdp")),
        P(("dp", "fsdp")),
        P(("dp", "fsdp")),
    )
    return jax.shard_map(partial(local, Grid(mesh)), mesh=mesh, in_specs=in_specs, out_specs=out_specs, check_vma=False)
```

```python
from functools import partial
import math

import jax
import jax.numpy as jnp
from jax import lax
from jax.experimental import pallas as pl
from jax.experimental.pallas import tpu as pltpu
from jax.sharding import PartitionSpec as P

FF = 1536
HEADS = 6


EPSILON = 1e-06
GELU_COEF = 0.044715
ROOT_TWO_OVER_PI = 0.7978845608028654


def layer_norm(values):
    centre = values - jnp.mean(values, axis=-1, keepdims=True)
    inverse = lax.rsqrt(jnp.mean(centre * centre, axis=-1, keepdims=True) + EPSILON)
    return (centre * inverse, inverse)


def norm_backward(grad_norm, normed, inverse):
    first = jnp.mean(grad_norm, axis=-1, keepdims=True)
    second = jnp.mean(grad_norm * normed, axis=-1, keepdims=True)
    return (grad_norm - first - normed * second) * inverse


def gelu_value(pre_act):
    inner = ROOT_TWO_OVER_PI * (pre_act + GELU_COEF * pre_act * pre_act * pre_act)
    return 0.5 * pre_act * (1.0 + jnp.tanh(inner))


def gelu_slope(pre_act):
    tanh_part = jnp.tanh(ROOT_TWO_OVER_PI * (pre_act + GELU_COEF * pre_act * pre_act * pre_act))
    return 0.5 * (1.0 + tanh_part) + 0.5 * pre_act * (
        1.0 - tanh_part * tanh_part
    ) * ROOT_TWO_OVER_PI * (1.0 + 3.0 * GELU_COEF * pre_act * pre_act)


def silu_slope(values):
    sigma = jax.nn.sigmoid(values)
    return sigma * (1.0 + values * (1.0 - sigma))


LANES = 128
SUBLANES = 16
AXES = ("dp", "fsdp")
MESH = pl.DeviceIdType.MESH


class Grid:
    def __init__(self, mesh):
        dp, fsdp = mesh.shape["dp"], mesh.shape["fsdp"]
        side = math.isqrt(dp)
        self.high = side if side * side == dp else 1
        self.low = dp // self.high
        self.pair = 2 if fsdp % 2 == 0 else 1
        self.depth = fsdp // self.pair
        self.count = dp * fsdp
        self.sizes = (self.high, self.low, self.depth, self.pair)

    def here(self):
        a, f = lax.axis_index("dp"), lax.axis_index("fsdp")
        return [a // self.low, a % self.low, f // self.pair, f % self.pair]

    def peer(self, here, axis, step):
        spot = list(here)
        spot[axis] = lax.rem(here[axis] + step, self.sizes[axis])
        return spot

    def ident(self, spot):
        return (spot[0] * self.low + spot[1], spot[2] * self.pair + spot[3])

    def barrier(self, here):
        sem = pltpu.get_barrier_semaphore()
        total = 0
        for axis in range(4):
            for step in range(1, self.sizes[axis]):
                pl.semaphore_signal(
                    sem, inc=1, device_id=self.ident(self.peer(here, axis, step)), device_id_type=MESH
                )
                total += 1
        pl.semaphore_wait(sem, total)


def chunk_rows(arrays):
    chunks = []
    for n, array in enumerate(arrays):
        rows = array.shape[-2]
        if rows % (2 * SUBLANES) == 0:
            chunks += [(n, 0, rows // 2), (n, rows // 2, rows // 2)]
        else:
            chunks.append((n, 0, rows))
    return chunks


class Mover:
    def __init__(self, grid, send_sem, recv_sem):
        self.grid, self.here = grid, grid.here()
        self.send_sem, self.recv_sem = send_sem, recv_sem
        self.started = []

    def push(self, src, dst, spot):
        k = len(self.started)
        copy = pltpu.make_async_remote_copy(
            src_ref=src, dst_ref=dst, send_sem=self.send_sem.at[k], recv_sem=self.recv_sem.at[k],
            device_id=self.grid.ident(spot), device_id_type=MESH,
        )
        copy.start()
        self.started.append(copy)
        return copy

    def spots(self, axis):
        return [self.grid.peer(self.here, axis, s) for s in range(1, self.grid.sizes[axis])]

    def pushes(self, ref, axis):
        return [self.push(ref, ref, spot) for spot in self.spots(axis)]

    def drain(self):
        for copy in self.started:
            copy.wait_send()


def arrive(copies):
    for copy in copies:
        copy.wait_recv()


class Spread:
    def __init__(self, mover, in_ref, out_ref, rows, low_first):
        self.mover, self.in_ref, self.out_ref, self.rows = mover, in_ref, out_ref, rows
        self.low_first = low_first
        self.swap = []

    def begin(self):
        hi, lo, z, c = self.mover.here
        src, dst = self.in_ref.at[self.rows], self.out_ref.at[hi, lo, z, c, self.rows]
        self.pending = [self.mover.push(src, dst, spot) for spot in self.mover.spots(2)]

    def first(self):
        hi, lo, z, c = self.mover.here
        arrive(self.pending)
        part = self.out_ref.at[hi, lo, :, c, self.rows]
        self.pending = self.mover.pushes(part, 1 if self.low_first else 0)
        self.swap += self.mover.pushes(part, 3)

    def second(self):
        hi, lo, z, c = self.mover.here
        arrive(self.pending)
        out, rows = self.out_ref, self.rows
        if self.low_first:
            self.pending = self.mover.pushes(out.at[hi, :, :, c, rows], 0)
            others = [out.at[hi, spot[1], :, c, rows] for spot in self.mover.spots(1)]
        else:
            self.pending = self.mover.pushes(out.at[:, lo, :, c, rows], 1)
            others = [out.at[spot[0], lo, :, c, rows] for spot in self.mover.spots(0)]
        for other in others:
            self.swap += self.mover.pushes(other, 3)

    def third(self):
        hi, lo, z, c = self.mover.here
        arrive(self.pending)
        out, rows = self.out_ref, self.rows
        if self.low_first:
            others = [out.at[spot[0], :, :, c, rows] for spot in self.mover.spots(0)]
        else:
            others = [out.at[:, spot[1], :, c, rows] for spot in self.mover.spots(1)]
        for other in others:
            self.swap += self.mover.pushes(other, 3)

    def end(self):
        arrive(self.swap)

    @staticmethod
    def copies(grid):
        high, low, depth, pair = grid.sizes
        return depth - 1 + (high + low - 2) + (pair - 1) * (1 + high + low - 2)


def gather_kernel(grid, chunks, arrays, *refs):
    in_refs, out_refs = refs[:arrays], refs[arrays : 2 * arrays]
    send_sem, recv_sem, own_sem = refs[2 * arrays :]
    mover = Mover(grid, send_sem, recv_sem)
    hi, lo, z, c = mover.here
    grid.barrier(mover.here)
    own = [
        pltpu.make_async_copy(in_refs[n], out_refs[n].at[hi, lo, z, c], own_sem.at[n])
        for n in range(arrays)
    ]
    for copy in own:
        copy.start()
    spreads = [
        Spread(mover, in_refs[n], out_refs[n], pl.ds(start, size), k % 2 == 0)
        for k, (n, start, size) in enumerate(chunks)
    ]
    for spread in spreads:
        spread.begin()
    for copy in own:
        copy.wait()
    for spread in spreads:
        spread.first()
    for spread in spreads:
        spread.second()
    for spread in spreads:
        spread.third()
    for spread in spreads:
        spread.end()
    mover.drain()


def gather_all(grid, arrays):
    chunks = chunk_rows(arrays)
    copies = Spread.copies(grid) * len(chunks)
    vmem = pl.BlockSpec(memory_space=pltpu.VMEM)
    return pl.pallas_call(
        partial(gather_kernel, grid, chunks, len(arrays)),
        out_shape=[jax.ShapeDtypeStruct(grid.sizes + array.shape, array.dtype) for array in arrays],
        in_specs=[vmem] * len(arrays),
        out_specs=[vmem] * len(arrays),
        scratch_shapes=[
            pltpu.SemaphoreType.DMA((copies,)),
            pltpu.SemaphoreType.DMA((copies,)),
            pltpu.SemaphoreType.DMA((len(arrays),)),
        ],
        compiler_params=pltpu.CompilerParams(
            collective_id=0, has_side_effects=True, vmem_limit_bytes=48 * 1024 * 1024
        ),
    )(*arrays)


def scatter_kernel(grid, chunks, arrays, extra, *refs):
    note_refs, refs = refs[:extra], refs[extra:]
    g_refs, refs = refs[:arrays], refs[arrays:]
    note_outs, refs = refs[:extra], refs[extra:]
    out_refs, refs = refs[:arrays], refs[arrays:]
    pair_bufs, refs = refs[:arrays], refs[arrays:]
    accs, refs = refs[:arrays], refs[arrays:]
    one_bufs, refs = refs[:arrays], refs[arrays:]
    two_bufs, refs = refs[:arrays], refs[arrays:]
    z_bufs, (send_sem, recv_sem, own_sem) = refs[:arrays], refs[arrays:]
    mover = Mover(grid, send_sem, recv_sem)
    here, push = mover.here, mover.push
    hi, lo, z, c = here
    grid.barrier(here)
    owns = [
        pltpu.make_async_copy(note_refs[n], note_outs[n].at[hi, lo, z, c], own_sem.at[n])
        for n in range(extra)
    ]
    notes = [
        Spread(mover, note_refs[n], note_outs[n], pl.ds(0, note_refs[n].shape[0]), n % 2 == 0)
        for n in range(extra)
    ]
    for own, note in zip(owns, notes):
        own.start()
        note.begin()

    def steps(axis):
        return [(s - 1, grid.peer(here, axis, s)) for s in range(1, grid.sizes[axis])]

    def add(into, terms, first, second):
        def body(t, _):
            i, j = t // second, t % second
            total = terms[0](i, j)[...].astype(jnp.float32)
            for term in terms[1:]:
                total = total + term(i, j)[...].astype(jnp.float32)
            target = into(i, j)
            target[...] = total.astype(target.dtype)
            return 0

        lax.fori_loop(0, first * second, body, 0)

    high, low, depth, pair = grid.sizes
    swaps, ones, twos, lines = [], [], [], []
    for n, start, size in chunks:
        rows = pl.ds(start, size)
        g_ref, pair_buf = g_refs[n], pair_bufs[n]
        swaps.append(
            [push(g_ref.at[:, :, :, spot[3], rows], pair_buf.at[:, :, :, rows], spot) for _, spot in steps(3)]
        )
    for own, note in zip(owns, notes):
        own.wait()
        note.first()
    for k, (n, start, size) in enumerate(chunks):
        rows = pl.ds(start, size)
        g_ref, pair_buf, acc, buf_one = g_refs[n], pair_bufs[n], accs[n], one_bufs[n]
        arrive(swaps[k])
        terms = [lambda i, j: g_ref.at[i // low, i % low, j, c, rows]]
        if pair > 1:
            terms.append(lambda i, j: pair_buf.at[i // low, i % low, j, rows])
        add(lambda i, j: acc.at[i // low, i % low, j, rows], terms, high * low, depth)
        if k % 2 == 0:
            ones.append(
                [push(acc.at[spot[0], :, :, rows], buf_one.at[s, 0:low, :, rows], spot) for s, spot in steps(0)]
            )
        else:
            ones.append(
                [push(acc.at[:, spot[1], :, rows], buf_one.at[s, 0:high, :, rows], spot) for s, spot in steps(1)]
            )
    for note in notes:
        note.second()
    for k, (n, start, size) in enumerate(chunks):
        rows = pl.ds(start, size)
        acc, buf_one, buf_two = accs[n], one_bufs[n], two_bufs[n]
        arrive(ones[k])
        even = k % 2 == 0
        mine = (lambda i, j: acc.at[hi, i, j, rows]) if even else (lambda i, j: acc.at[i, lo, j, rows])
        terms = [mine] + [
            (lambda i, j, s=s: buf_one.at[s, i, j, rows]) for s, _ in steps(0 if even else 1)
        ]
        add(mine, terms, low if even else high, depth)
        if even:
            twos.append(
                [push(acc.at[hi, spot[1], :, rows], buf_two.at[s, :, rows], spot) for s, spot in steps(1)]
            )
        else:
            twos.append(
                [push(acc.at[spot[0], lo, :, rows], buf_two.at[s, :, rows], spot) for s, spot in steps(0)]
            )
    for note in notes:
        note.third()
    for k, (n, start, size) in enumerate(chunks):
        rows = pl.ds(start, size)
        acc, buf_two, buf_z = accs[n], two_bufs[n], z_bufs[n]
        arrive(twos[k])
        mine = lambda i, j: acc.at[hi, lo, j, rows]
        terms = [mine] + [
            (lambda i, j, s=s: buf_two.at[s, j, rows]) for s, _ in steps(1 if k % 2 == 0 else 0)
        ]
        add(mine, terms, 1, depth)
        lines.append(
            [push(acc.at[hi, lo, spot[2], rows], buf_z.at[s, rows], spot) for s, spot in steps(2)]
        )
    for k, (n, start, size) in enumerate(chunks):
        rows = pl.ds(start, size)
        acc, buf_z = accs[n], z_bufs[n]
        arrive(lines[k])
        total = acc[hi, lo, z, rows].astype(jnp.float32)
        for s in range(depth - 1):
            total = total + buf_z[s, rows].astype(jnp.float32)
        out_refs[n][rows, :] = total
    for note in notes:
        note.end()
    mover.drain()


def scatter_sum(grid, arrays, notes):
    high, low, depth, pair = grid.sizes
    chunks = chunk_rows(arrays)
    copies = len(chunks) * (high + low + depth + pair - 4) + Spread.copies(grid) * len(notes)
    kind = arrays[0].dtype
    tails = [array.shape[-2:] for array in arrays]
    side = max(high, low)
    shapes = [
        (high, low, depth), (high, low, depth), (max(side - 1, 1), side, depth),
        (max(side - 1, 1), depth), (max(depth - 1, 1),),
    ]
    vmem = pl.BlockSpec(memory_space=pltpu.VMEM)
    return pl.pallas_call(
        partial(scatter_kernel, grid, chunks, len(arrays), len(notes)),
        out_shape=[jax.ShapeDtypeStruct(grid.sizes + note.shape, note.dtype) for note in notes]
        + [jax.ShapeDtypeStruct(tail, jnp.float32) for tail in tails],
        in_specs=[vmem] * (len(notes) + len(arrays)),
        out_specs=[vmem] * (len(notes) + len(arrays)),
        scratch_shapes=[pltpu.VMEM(shape + tail, kind) for shape in shapes for tail in tails]
        + [pltpu.SemaphoreType.DMA((copies,)), pltpu.SemaphoreType.DMA((copies,)), pltpu.SemaphoreType.DMA((len(notes),))],
        compiler_params=pltpu.CompilerParams(
            collective_id=1, has_side_effects=True, vmem_limit_bytes=48 * 1024 * 1024
        ),
    )(*notes, *arrays)


def padded_rows(extent):
    return -(-extent // LANES)


def pack(pieces, lead):
    parts = []
    for piece in pieces:
        extent = piece.shape[-1]
        rows = padded_rows(extent)
        gap = rows * LANES - extent
        if gap:
            piece = jnp.pad(piece, [(0, 0)] * len(lead) + [(0, gap)])
        parts.append(piece.reshape(lead + (rows, LANES)))
    if len(parts) == 1:
        return parts[0]
    return jnp.concatenate(parts, axis=-2)


def dot(left, right, contract=(1, 0)):
    return lax.dot_general(
        left, right, (((contract[0],), (contract[1],)), ((), ())), preferred_element_type=jnp.float32
    )


def block_kernel(
    count_ref, x_ref, cond_ref, cot_ref, w_ada, attn_ref, mlp_ref, bias_ref,
    out_ref, gx_ref, gcond_ref, act_ref, dmod_ref, g_attn, g_mlp, gbias_ref,
    line, w_qkv, w_proj, w_one, w_two, g_qkv, g_proj, g_one, g_two,
    mod, norm_one, inv_one, h_one, qkv, probs, mixed, branch, norm_two, inv_two, h_two,
    pre, act, mlp, wide, back, dx, small, dqkv, dmod,
):
    slots, length, width = x_ref.shape
    hidden = w_one.shape[1]
    rows_all = slots * length
    heads = probs.shape[1]
    head_dim = width // heads
    score_scale = head_dim ** (-0.5)
    f32, b16 = jnp.float32, jnp.bfloat16
    tile = 256 if hidden % 256 == 0 else hidden
    count = count_ref[0]
    o_query, o_value = 6 * width, 7 * width
    o_proj, o_one, o_two = 8 * width, 9 * width, 9 * width + hidden
    lane = lax.broadcasted_iota(jnp.int32, (length, 2 * head_dim), 1)
    lower = lane < head_dim

    def slot_loop(body):
        def step(s, _):
            body(s, pl.ds(pl.multiple_of(s * length, length), length))
            return 0

        lax.fori_loop(0, slots, step, 0)

    def part(s, k):
        return mod[pl.ds(s, 1), k * width : (k + 1) * width]

    def only(pair_block, first):
        return jnp.where(lower if first else jnp.logical_not(lower), pair_block, jnp.zeros_like(pair_block))

    def column_sum(values):
        return jnp.sum(values, axis=0, keepdims=True)

    def load_matrix(flat_ref, top, matrix):
        height, across = matrix.shape[0], matrix.shape[1] // LANES
        total = height * across

        def widen(t, _):
            at = pl.multiple_of(t * LANES, LANES)
            line[pl.ds(at, LANES), :] = flat_ref[pl.ds(top + at, LANES), :].astype(f32)
            return 0

        lax.fori_loop(0, total // LANES, widen, 0)
        for j in range(across):
            matrix[:, j * LANES : (j + 1) * LANES] = line[pl.ds(j, height, stride=across), :].astype(b16)

    def store_matrix(matrix, flat_ref, top):
        height, across = matrix.shape[0], matrix.shape[1] // LANES
        total = height * across
        for j in range(across):
            line[pl.ds(j, height, stride=across), :] = matrix[:, j * LANES : (j + 1) * LANES].astype(f32)

        def narrow(t, _):
            at = pl.multiple_of(t * LANES, LANES)
            flat_ref[pl.ds(top + at, LANES), :] = line[pl.ds(at, LANES), :].astype(b16)
            return 0

        lax.fori_loop(0, total // LANES, narrow, 0)

    proj_top, two_top = 3 * width * width // LANES, width * hidden // LANES
    load_matrix(attn_ref, 0, w_qkv)
    load_matrix(attn_ref, proj_top, w_proj)
    load_matrix(mlp_ref, 0, w_one)
    load_matrix(mlp_ref, two_top, w_two)
    cond = cond_ref[...]
    cond_act = (cond * jax.nn.sigmoid(cond)).astype(b16)
    mod[...] = dot(cond_act, w_ada[...]) + bias_ref[:, : 6 * width]

    def norm_first(s, rows):
        normed, inverse = layer_norm(x_ref[s])
        norm_one[rows, :] = normed
        inv_one[rows, :] = inverse
        h_one[rows, :] = (normed * (1.0 + part(s, 1)) + part(s, 0)).astype(b16)

    slot_loop(norm_first)
    for k, offset in enumerate((o_query, None, o_value)):
        cols = slice(k * width, (k + 1) * width)
        value = dot(h_one[...], w_qkv[:, cols])
        if offset is not None:
            value = value + bias_ref[:, offset : offset + width]
        qkv[:, cols] = value.astype(b16)

    def attend(s, rows):
        for pair in range(heads // 2):
            at = pair * 2 * head_dim
            query = qkv[rows, at : at + 2 * head_dim]
            key = qkv[rows, width + at : width + at + 2 * head_dim]
            value = qkv[rows, 2 * width + at : 2 * width + at + 2 * head_dim]
            halves = []
            for h in range(2):
                scores = dot(only(query, h == 0), key, (1, 1)) * score_scale
                total = jnp.log(jnp.sum(jnp.exp(scores), axis=-1, keepdims=True))
                prob = jnp.exp(scores - total)
                probs[s, 2 * pair + h] = prob
                halves.append(dot(prob.astype(b16), value))
            mixed[rows, at : at + 2 * head_dim] = jnp.where(lower, halves[0], halves[1]).astype(b16)

    slot_loop(attend)
    branch[...] = dot(mixed[...], w_proj[...]) + bias_ref[:, o_proj : o_proj + width]

    def norm_second(s, rows):
        after = x_ref[s] + part(s, 2) * branch[rows, :]
        dx[rows, :] = after
        normed, inverse = layer_norm(after)
        norm_two[rows, :] = normed
        inv_two[rows, :] = inverse
        h_two[rows, :] = (normed * (1.0 + part(s, 4)) + part(s, 3)).astype(b16)

    slot_loop(norm_second)

    def up(t, _):
        cols = pl.ds(pl.multiple_of(t * tile, tile), tile)
        shift = bias_ref[:, pl.ds(pl.multiple_of(o_one + t * tile, LANES), tile)]
        value = dot(h_two[...], w_one[:, cols]) + shift
        pre[:, cols] = value
        act[:, cols] = gelu_value(value).astype(b16)
        return 0

    lax.fori_loop(0, hidden // tile, up, 0)
    mlp[...] = dot(act[...], w_two[...]) + bias_ref[:, o_two : o_two + width]

    gbias_ref[...] = jnp.zeros_like(gbias_ref)

    def finish(s, rows):
        live = s < count
        value = mlp[rows, :]
        out_ref[s] = jnp.where(live, dx[rows, :] + part(s, 5) * value, 0.0)
        grad = jnp.where(live, cot_ref[s], 0.0)
        dmod[pl.ds(s, 1), 5 * width :] = column_sum(grad * value)
        full = grad * part(s, 5)
        gbias_ref[:, o_two : o_two + width] += column_sum(full)
        small[rows, :] = full.astype(b16)

    slot_loop(finish)

    def down(t, _):
        cols = pl.ds(pl.multiple_of(t * tile, tile), tile)
        full = dot(small[...], w_two[cols, :], (1, 1)) * gelu_slope(pre[:, cols])
        gbias_ref[:, pl.ds(pl.multiple_of(o_one + t * tile, LANES), tile)] = column_sum(full)
        grad = full.astype(b16)
        wide[:, cols] = grad
        g_two[cols, :] = dot(act[:, cols], small[...], (0, 0)).astype(g_two.dtype)
        g_one[:, cols] = dot(h_two[...], grad, (0, 0)).astype(g_one.dtype)
        return 0

    lax.fori_loop(0, hidden // tile, down, 0)
    back[...] = dot(wide[...], w_one[...], (1, 1))

    def mlp_back(s, rows):
        grad_two = back[rows, :]
        normed = norm_two[rows, :]
        dmod[pl.ds(s, 1), 4 * width : 5 * width] = column_sum(grad_two * normed)
        dmod[pl.ds(s, 1), 3 * width : 4 * width] = column_sum(grad_two)
        after = jnp.where(s < count, cot_ref[s], 0.0) + norm_backward(
            grad_two * (1.0 + part(s, 4)), normed, inv_two[rows, :]
        )
        dx[rows, :] = after
        dmod[pl.ds(s, 1), 2 * width : 3 * width] = column_sum(after * branch[rows, :])
        full = after * part(s, 2)
        gbias_ref[:, o_proj : o_proj + width] += column_sum(full)
        small[rows, :] = full.astype(b16)

    slot_loop(mlp_back)
    g_proj[...] = dot(mixed[...], small[...], (0, 0)).astype(g_proj.dtype)
    mixed[...] = dot(small[...], w_proj[...], (1, 1)).astype(b16)

    def attend_back(s, rows):
        for pair in range(heads // 2):
            at = pair * 2 * head_dim
            span = slice(at, at + 2 * head_dim)
            query = qkv[rows, span]
            key = qkv[rows, width + at : width + at + 2 * head_dim]
            value = qkv[rows, 2 * width + at : 2 * width + at + 2 * head_dim]
            grad = mixed[rows, span]
            d_query, d_key, d_value = [], [], []
            for h in range(2):
                prob = probs[s, 2 * pair + h]
                d_prob = dot(only(grad, h == 0), value, (1, 1))
                d_value.append(dot(prob.astype(b16), grad, (0, 0)))
                delta = jnp.sum(prob * d_prob, axis=-1, keepdims=True)
                d_score = (prob * (d_prob - delta) * score_scale).astype(b16)
                d_query.append(dot(d_score, key))
                d_key.append(dot(d_score, query, (0, 0)))
            d_query = jnp.where(lower, d_query[0], d_query[1]).astype(b16)
            d_key = jnp.where(lower, d_key[0], d_key[1]).astype(b16)
            d_value = jnp.where(lower, d_value[0], d_value[1]).astype(b16)
            dqkv[rows, span] = d_query
            dqkv[rows, width + at : width + at + 2 * head_dim] = d_key
            dqkv[rows, 2 * width + at : 2 * width + at + 2 * head_dim] = d_value
            gbias_ref[:, o_query + at : o_query + at + 2 * head_dim] += column_sum(d_query.astype(f32))
            gbias_ref[:, o_value + at : o_value + at + 2 * head_dim] += column_sum(d_value.astype(f32))

    slot_loop(attend_back)
    for k in range(3):
        cols = slice(k * width, (k + 1) * width)
        g_qkv[:, cols] = dot(h_one[...], dqkv[:, cols], (0, 0)).astype(g_qkv.dtype)
    back[...] = dot(dqkv[...], w_qkv[...], (1, 1))

    def attn_back(s, rows):
        grad_one = back[rows, :]
        normed = norm_one[rows, :]
        dmod[pl.ds(s, 1), width : 2 * width] = column_sum(grad_one * normed)
        dmod[pl.ds(s, 1), :width] = column_sum(grad_one)
        gx_ref[s] = dx[rows, :] + norm_backward(
            grad_one * (1.0 + part(s, 1)), normed, inv_one[rows, :]
        )

    slot_loop(attn_back)
    gbias_ref[:, : 6 * width] = column_sum(dmod[...])
    grad_mod = dmod[...].astype(b16)
    store_matrix(g_qkv, g_attn, 0)
    store_matrix(g_proj, g_attn, proj_top)
    store_matrix(g_one, g_mlp, 0)
    store_matrix(g_two, g_mlp, two_top)
    act_ref[...] = cond_act
    dmod_ref[...] = grad_mod
    gcond_ref[...] = dot(grad_mod, w_ada[...], (1, 1)) * silu_slope(cond)


def run_block(counts, latents, conditioning, cotangent, weights, biases):
    slots, length, width = latents.shape
    w_ada, attn, mlp = weights
    hidden = mlp.size // (2 * width)
    rows = slots * length
    f32, b16 = jnp.float32, jnp.bfloat16
    outs = [
        (latents.shape, f32), (latents.shape, f32), (conditioning.shape, f32),
        (conditioning.shape, b16), ((slots, 6 * width), b16),
        (attn.shape, b16), (mlp.shape, b16), (biases.shape, f32),
    ]
    matrices = [(width, 3 * width), (width, width), (width, hidden), (hidden, width)]
    scratch = [((max(h * w for h, w in matrices) // LANES, LANES), f32)]
    scratch += [(shape, b16) for shape in matrices + matrices]
    scratch += [
        ((slots, 6 * width), f32), ((rows, width), f32), ((rows, 1), f32), ((rows, width), b16),
        ((rows, 3 * width), b16), ((slots, HEADS, length, length), f32), ((rows, width), b16),
        ((rows, width), f32), ((rows, width), f32), ((rows, 1), f32), ((rows, width), b16),
        ((rows, hidden), f32), ((rows, hidden), b16), ((rows, width), f32), ((rows, hidden), b16),
        ((rows, width), f32), ((rows, width), f32), ((rows, width), b16), ((rows, 3 * width), b16),
        ((slots, 6 * width), f32),
    ]
    vmem = pl.BlockSpec(memory_space=pltpu.VMEM)
    return pl.pallas_call(
        block_kernel,
        out_shape=[jax.ShapeDtypeStruct(shape, kind) for shape, kind in outs],
        in_specs=[pl.BlockSpec(memory_space=pltpu.SMEM)] + [vmem] * 7,
        out_specs=[vmem] * len(outs),
        scratch_shapes=[pltpu.VMEM(shape, kind) for shape, kind in scratch],
        compiler_params=pltpu.CompilerParams(vmem_limit_bytes=60 * 1024 * 1024),
    )(counts, latents, conditioning, cotangent, *weights, biases)


LAG = 3


class Share:
    def __init__(self, mover, ref, start, size, low_first):
        self.mover, self.ref, self.rows, self.low_first = mover, ref, pl.ds(start, size), low_first
        self.swap = []

    def begin(self):
        hi, lo, z, c = self.mover.here
        self.pending = self.mover.pushes(self.ref.at[hi, lo, z, c, self.rows], 2)

    def first(self):
        hi, lo, z, c = self.mover.here
        arrive(self.pending)
        part = self.ref.at[hi, lo, :, c, self.rows]
        self.pending = self.mover.pushes(part, 1 if self.low_first else 0)
        self.swap += self.mover.pushes(part, 3)

    def second(self):
        hi, lo, z, c = self.mover.here
        arrive(self.pending)
        ref, rows = self.ref, self.rows
        if self.low_first:
            self.pending = self.mover.pushes(ref.at[hi, :, :, c, rows], 0)
            others = [ref.at[hi, spot[1], :, c, rows] for spot in self.mover.spots(1)]
        else:
            self.pending = self.mover.pushes(ref.at[:, lo, :, c, rows], 1)
            others = [ref.at[spot[0], lo, :, c, rows] for spot in self.mover.spots(0)]
        for other in others:
            self.swap += self.mover.pushes(other, 3)

    def third(self):
        hi, lo, z, c = self.mover.here
        arrive(self.pending)
        ref, rows = self.ref, self.rows
        if self.low_first:
            others = [ref.at[spot[0], :, :, c, rows] for spot in self.mover.spots(0)]
        else:
            others = [ref.at[:, spot[1], :, c, rows] for spot in self.mover.spots(1)]
        for other in others:
            self.swap += self.mover.pushes(other, 3)

    def end(self):
        arrive(self.swap)


class Reduce:
    def __init__(self, mover, bufs, start, size, even):
        self.mover, self.even = mover, even
        self.grad, self.pair, self.acc, self.one_buf, self.two_buf, self.line_buf, self.total = bufs
        self.start, self.size, self.rows = start, size, pl.ds(start, size)

    def steps(self, axis):
        grid, here = self.mover.grid, self.mover.here
        return [(s - 1, grid.peer(here, axis, s)) for s in range(1, grid.sizes[axis])]

    def begin(self):
        self.pending = [
            self.mover.push(self.grad.at[:, :, :, spot[3], self.rows], self.pair.at[:, :, :, self.rows], spot)
            for _, spot in self.steps(3)
        ]

    def add(self, into, terms, first, second):
        def body(i, _):
            for j in range(second):
                total = terms[0](i, j)[...]
                for term in terms[1:]:
                    total = total + term(i, j)[...]
                into(i, j)[...] = total
            return 0

        lax.fori_loop(0, first, body, 0)

    def one(self):
        high, low, depth, pair = self.mover.grid.sizes
        c, rows = self.mover.here[3], self.rows
        grad, pair_buf, acc, buf, push = self.grad, self.pair, self.acc, self.one_buf, self.mover.push
        arrive(self.pending)
        terms = [lambda i, j: grad.at[i // low, i % low, j, c, rows]]
        if pair > 1:
            terms.append(lambda i, j: pair_buf.at[i // low, i % low, j, rows])
        self.add(lambda i, j: acc.at[i // low, i % low, j, rows], terms, high * low, depth)
        if self.even:
            self.pending = [
                push(acc.at[spot[0], :, :, rows], buf.at[s, 0:low, :, rows], spot) for s, spot in self.steps(0)
            ]
        else:
            self.pending = [
                push(acc.at[:, spot[1], :, rows], buf.at[s, 0:high, :, rows], spot) for s, spot in self.steps(1)
            ]

    def two(self):
        high, low, depth, pair = self.mover.grid.sizes
        hi, lo, z, c = self.mover.here
        rows, acc, one, buf, push = self.rows, self.acc, self.one_buf, self.two_buf, self.mover.push
        arrive(self.pending)
        mine = (lambda i, j: acc.at[hi, i, j, rows]) if self.even else (lambda i, j: acc.at[i, lo, j, rows])
        terms = [mine] + [
            (lambda i, j, s=s: one.at[s, i, j, rows]) for s, _ in self.steps(0 if self.even else 1)
        ]
        self.add(mine, terms, low if self.even else high, depth)
        if self.even:
            self.pending = [
                push(acc.at[hi, spot[1], :, rows], buf.at[s, :, rows], spot) for s, spot in self.steps(1)
            ]
        else:
            self.pending = [
                push(acc.at[spot[0], lo, :, rows], buf.at[s, :, rows], spot) for s, spot in self.steps(0)
            ]

    def three(self):
        depth = self.mover.grid.sizes[2]
        hi, lo, z, c = self.mover.here
        rows, acc, two, buf, push = self.rows, self.acc, self.two_buf, self.line_buf, self.mover.push
        arrive(self.pending)
        mine = lambda i, j: acc.at[hi, lo, j, rows]
        terms = [mine] + [
            (lambda i, j, s=s: two.at[s, j, rows]) for s, _ in self.steps(1 if self.even else 0)
        ]
        self.add(mine, terms, 1, depth)
        self.pending = [
            push(acc.at[hi, lo, spot[2], rows], buf.at[s, rows], spot) for s, spot in self.steps(2)
        ]

    def finish(self):
        depth = self.mover.grid.sizes[2]
        hi, lo, z, c = self.mover.here
        arrive(self.pending)
        total = self.acc[hi, lo, z, self.rows].astype(jnp.float32)
        for s in range(depth - 1):
            total = total + self.line_buf[s, self.rows].astype(jnp.float32)
        self.total[self.rows, :] = total


class Sizes:
    def __init__(self, grid, latents, shards):
        ada, attn, mlp, bias = (shard.shape[0] for shard in shards)
        self.slots, self.length, width = latents.shape
        self.width, self.bias = width, bias
        self.hidden = mlp * grid.count // (2 * width)
        self.parts = self.hidden // width
        self.ada_rows, self.qkv_rows = ada // (6 * width), attn // (3 * width)
        self.attn_rows, self.one_rows, self.mlp_rows = attn // width, mlp // self.hidden, mlp // width
        self.qkv_devices, self.one_devices = 3 * width * width // attn, width * self.hidden // mlp
        self.lead = 2 * SUBLANES - (2 * self.ada_rows) % (2 * SUBLANES)
        self.head_rows = self.lead + 2 * self.ada_rows
        self.tail_rows = 4 * self.ada_rows
        group = grid.depth * grid.pair
        exact = (
            self.hidden == self.parts * width, ada == self.ada_rows * 6 * width, attn == self.qkv_rows * 3 * width,
            mlp == self.one_rows * self.hidden, mlp == self.mlp_rows * width,
            self.qkv_devices * attn == 3 * width * width, self.one_devices * mlp == width * self.hidden,
        )
        whole = (
            self.qkv_rows % SUBLANES, (2 * self.one_rows) % SUBLANES, self.one_rows % 8, self.tail_rows % SUBLANES,
            self.qkv_devices % group, self.one_devices % group, width % LANES, (4 * self.slots) % SUBLANES,
            (2 * self.slots + 4 + self.parts) % SUBLANES, self.parts % grid.pair, self.mlp_rows % SUBLANES,
            (self.length % LANES), (2 * self.width // HEADS) % LANES,
        )
        per_tile = width // self.mlp_rows if width % self.mlp_rows == 0 else 0
        self.fits = (
            all(exact) and not any(whole) and grid.pair == 2 and self.slots < self.lead and bias <= 2 * LANES
            and bias <= width and per_tile > 0 and per_tile % grid.pair == 0 and group % per_tile == 0
            and grid.count * bias == (9 + self.parts + 1) * width and grid.high * grid.low * group == grid.count
        )


def fused_kernel(
    grid, sizes, count_ref, x_hbm, cond_ref, cot_hbm, ada_hbm, attn_hbm, mlp_hbm, bias_ref,
    out_ref, gx_ref, gcond_ref, g_ada_out, g_attn_out, g_mlp_out, g_bias_out,
    all_ada, all_attn, all_mlp, note_a, note_b, grad_attn, grad_mlp,
    pair_attn, pair_mlp, acc_attn, acc_mlp, one_attn, one_mlp, two_attn, two_mlp, line_attn, line_mlp,
    sum_attn, sum_mlp, swap_out, swap_in, back_in,
    x_ref, cot_ref, ada_ref, attn_ref, mlp_ref, line, unit, local_rows, pick_head, pick_tail, spread, bias_rows,
    mod, norm_one, inv_one, h_one, qkv, probs, mixed, branch, norm_two, inv_two, h_two,
    slope, act, mlp, wide, back, dx, small, dqkv, dmod, gbias,
    send_sem, recv_sem, own_sem,
):
    mover = Mover(grid, send_sem, recv_sem)
    here = mover.here
    hi, lo, z, c = here
    high, low, depth, pair = grid.sizes
    me = ((hi * low + lo) * depth + z) * pair + c
    slots, length, width, hidden = sizes.slots, sizes.length, sizes.width, sizes.hidden
    rows_all = slots * length
    heads = probs.shape[1]
    head_dim = width // heads
    score_scale = head_dim ** (-0.5)
    f32, b16 = jnp.float32, jnp.bfloat16
    count = count_ref[0]
    parts, tiles = sizes.parts, width // LANES
    ada_rows, lead, head_rows, tail_rows = sizes.ada_rows, sizes.lead, sizes.head_rows, sizes.tail_rows
    group = depth * pair

    x_in = pltpu.make_async_copy(x_hbm, x_ref, own_sem.at[0])
    cot_in = pltpu.make_async_copy(cot_hbm, cot_ref, own_sem.at[1])
    shards_in = [
        pltpu.make_async_copy(a, b, own_sem.at[2 + n])
        for n, (a, b) in enumerate(((ada_hbm, ada_ref), (attn_hbm, attn_ref), (mlp_hbm, mlp_ref)))
    ]
    for copy in shards_in:
        copy.start()
    x_in.start()
    cot_in.start()

    def strided(start, rows, stride):
        return line[pl.ds(start, rows, stride=stride), :]

    def lanes(t):
        return slice(t * LANES, (t + 1) * LANES)

    def column_sum(values):
        return jnp.sum(values, axis=0, keepdims=True)

    cond = cond_ref[...]
    cond_act = (cond * jax.nn.sigmoid(cond)).astype(b16)
    shards_in[0].wait()
    line[0 : ada_ref.shape[0], :] = ada_ref[...].astype(f32)
    unit[0:lead, :] = jnp.zeros((lead, width), f32)
    for k in range(6):
        for t in range(tiles):
            unit[lead + ada_rows * k : lead + ada_rows * (k + 1), lanes(t)] = strided(
                tiles * k + t, ada_rows, 6 * tiles
            )
    unit[0:1, 0 : sizes.bias] = bias_ref[...].astype(f32)
    unit[1 : 1 + slots, :] = cond_act.astype(f32)
    all_ada[hi, lo, z, c] = unit[0 : head_rows + tail_rows, :].astype(b16)

    def cut_rows(ref, start, size):
        return [(ref, start + at, min(SUBLANES, size - at)) for at in range(0, size, SUBLANES)]

    pieces = cut_rows(all_ada, 0, head_rows), cut_rows(all_attn, 0, sizes.attn_rows)
    pieces += cut_rows(all_ada, head_rows, tail_rows), cut_rows(all_mlp, 0, sizes.mlp_rows)
    ends = [sum(len(piece) for piece in pieces[: k + 1]) for k in range(len(pieces))]
    shares = [
        Share(mover, ref, start, size, k % 2 == 0)
        for k, (ref, start, size) in enumerate(entry for piece in pieces for entry in piece)
    ]
    agenda, begun = [], ends[1]
    for t in range(len(shares) + 3 * LAG):
        while begun < min(len(shares), t + 2 + LAG):
            agenda.append((begun, "begin"))
            begun += 1
        for k, name in enumerate(("first", "second", "third", "end")):
            if 0 <= t - k * LAG < len(shares):
                agenda.append((t - k * LAG, name))

    def until(share, name):
        while (share, name) in agenda:
            k, step = agenda.pop(0)
            getattr(shares[k], step)()

    grid.barrier(here)
    for share in shares[: ends[0]]:
        share.begin()

    shards_in[1].wait()
    line[0 : attn_ref.shape[0], :] = attn_ref[...].astype(f32)

    @pl.when(me < sizes.qkv_devices)
    def _():
        rows = sizes.qkv_rows
        for k in range(3):
            for t in range(tiles):
                unit[rows * k : rows * (k + 1), lanes(t)] = strided(tiles * k + t, rows, 3 * tiles)

    @pl.when(me >= sizes.qkv_devices)
    def _():
        for t in range(tiles):
            unit[0 : sizes.attn_rows, lanes(t)] = strided(t, sizes.attn_rows, tiles)

    all_attn[hi, lo, z, c] = unit[0 : sizes.attn_rows, :].astype(b16)
    for share in shares[ends[0] : ends[1]]:
        share.begin()

    one_rows, per_core = sizes.one_rows, parts // pair
    shards_in[2].wait()
    line[0 : mlp_ref.shape[0], :] = mlp_ref[...].astype(f32)

    @pl.when(me < sizes.one_devices)
    def _():
        for k in range(parts):
            for t in range(tiles):
                local_rows[one_rows * k : one_rows * (k + 1), lanes(t)] = strided(
                    tiles * k + t, one_rows, parts * tiles
                )
        for k in range(per_core):
            unit[pl.ds(pl.multiple_of(2 * one_rows * k + one_rows * c, 8), one_rows), :] = local_rows[
                pl.ds(pl.multiple_of(one_rows * (per_core * c + k), 8), one_rows), :
            ]

    @pl.when(me >= sizes.one_devices)
    def _():
        for t in range(tiles):
            unit[0 : sizes.mlp_rows, lanes(t)] = strided(t, sizes.mlp_rows, tiles)
        local_rows[...] = jnp.zeros_like(local_rows)

    cut = one_rows * per_core
    swap_out[...] = local_rows[pl.ds(pl.multiple_of(cut * (1 - c), 8), cut), :].astype(b16)
    partner = grid.peer(here, 3, 1)
    swap = mover.push(swap_out, swap_in, partner)

    def picks(total, span, skip, target):
        at = lax.broadcasted_iota(jnp.int32, (1, total), 1)
        device, row = at // span, at % span - skip
        entry = jnp.where(row >= 0, device * ada_rows + row % ada_rows, -1)
        source = lax.broadcasted_iota(jnp.int32, (width, total), 0)
        target[...] = jnp.where(source == entry, 1.0, 0.0).astype(b16)

    def owner_mask(total, span, skip, blocks):
        at = lax.broadcasted_iota(jnp.int32, (blocks * slots, total), 1)
        block = lax.broadcasted_iota(jnp.int32, (blocks * slots, total), 0) // slots
        row = at % span - skip
        return jnp.logical_and(row >= 0, row // ada_rows == block)

    def spread_cond(pick, total, span, skip, blocks):
        wide_cond = dot(cond_act, pick[...])
        stacked = jnp.concatenate([wide_cond] * blocks, axis=0)
        return jnp.where(owner_mask(total, span, skip, blocks), stacked, 0.0).astype(b16)

    head_total, tail_total = grid.count * head_rows, grid.count * tail_rows

    def norm_first(s):
        rows = slice(s * length, (s + 1) * length)
        normed, inverse = layer_norm(x_ref[s])
        norm_one[rows, :] = normed
        inv_one[rows, :] = inverse

    def part(s, k):
        return mod[k * slots + s : k * slots + s + 1, :]

    until(ends[0] - 1, "first")
    picks(head_total, head_rows, lead, pick_head)
    head_cond = spread_cond(pick_head, head_total, head_rows, lead, 2)
    swap.wait_recv()

    @pl.when(me < sizes.one_devices)
    def _():
        local_rows[0:cut, :] = swap_in[...].astype(f32)
        for k in range(per_core):
            unit[pl.ds(pl.multiple_of(2 * one_rows * k + one_rows * (1 - c), 8), one_rows), :] = local_rows[
                one_rows * k : one_rows * (k + 1), :
            ]

    all_mlp[hi, lo, z, c] = unit[0 : sizes.mlp_rows, :].astype(b16)
    x_in.wait()
    for s in range(slots):
        until(min(ends[0] + s, ends[1] - 1), "first")
        norm_first(s)
    picks(tail_total, tail_rows, 0, pick_tail)
    until(ends[0] - 1, "third")
    tail_cond = spread_cond(pick_tail, tail_total, tail_rows, 0, 4)
    until(ends[0] - 1, "end")

    def rows_of(ref, start, size):
        return ref[:, :, :, :, start : start + size, :].reshape(grid.count * size, width)

    mod[0 : 2 * slots, :] = dot(head_cond, rows_of(all_ada, 0, head_rows))

    bias_rows[...] = jnp.zeros_like(bias_rows)
    lane = lax.broadcasted_iota(jnp.int32, (1, width), 1)
    for d in range(grid.count):
        values = all_ada[d // (low * group), d // group % low, d // pair % depth, d % pair, 0:SUBLANES, :].astype(f32)[0:1]
        row, shift = divmod(d * sizes.bias, width)
        turned = pltpu.roll(values, shift, 1) if shift else values
        end = shift + sizes.bias
        bias_rows[row : row + 1, :] += jnp.where(jnp.logical_and(lane >= shift, lane < end), turned, 0.0)
        if end > width:
            bias_rows[row + 1 : row + 2, :] += jnp.where(lane < end - width, turned, 0.0)

    def add_mod_bias(first, last):
        for k in range(first, last):
            span = slice(k * slots, (k + 1) * slots)
            mod[span, :] = mod[span, :] + bias_rows[k : k + 1, :]

    add_mod_bias(0, 2)

    def modulate_first(s):
        rows = slice(s * length, (s + 1) * length)
        h_one[rows, :] = (norm_one[rows, :] * (1.0 + part(s, 1)) + part(s, 0)).astype(b16)

    for s in range(slots):
        modulate_first(s)
    until(ends[1] - 1, "end")

    def devices(ref, first, last, rows):
        pieces = []
        for g in range(first // group, last // group):
            piece = ref[g // low, g % low, :, :, rows, :]
            pieces.append(piece.reshape(group * piece.shape[2], width))
        return pieces[0] if len(pieces) == 1 else jnp.concatenate(pieces, axis=0)

    def qkv_weight(k):
        return devices(all_attn, 0, sizes.qkv_devices, slice(sizes.qkv_rows * k, sizes.qkv_rows * (k + 1)))

    def proj_weight():
        return devices(all_attn, sizes.qkv_devices, grid.count, slice(0, sizes.attn_rows))

    tall = 2 * one_rows

    def one_weight(t):
        core, k = t // per_core, t % per_core
        pieces = [
            all_mlp[g // low, g % low, :, core, tall * k : tall * (k + 1), :].reshape(depth * tall, width)
            for g in range(sizes.one_devices // group)
        ]
        return pieces[0] if len(pieces) == 1 else jnp.concatenate(pieces, axis=0)

    per_tile = width // sizes.mlp_rows

    def two_place(t):
        first = sizes.one_devices + per_tile * t
        g, at = first // group, first % group // pair
        return g // low, g % low, slice(at, at + per_tile // pair)

    def two_weight(t):
        a, b, zs = two_place(t)
        return all_mlp[a, b, zs, :, :, :].reshape(width, width)

    cut_head = 2 * head_dim
    upper = lax.broadcasted_iota(jnp.int32, (length, cut_head), 1) >= head_dim

    def both(block):
        zero = jnp.zeros_like(block)
        return jnp.concatenate([jnp.where(upper, zero, block), jnp.where(upper, block, zero)], axis=0)

    for k, row in enumerate((6, None, 7)):
        value = dot(h_one[...], qkv_weight(k))
        if row is not None:
            value = value + bias_rows[row : row + 1, :]
        qkv[:, k * width : (k + 1) * width] = value.astype(b16)

    def attend(s):
        rows = slice(s * length, (s + 1) * length)
        for p in range(heads // 2):
            at = p * cut_head
            query = qkv[rows, at : at + cut_head]
            key = qkv[rows, width + at : width + at + cut_head]
            value = qkv[rows, 2 * width + at : 2 * width + at + cut_head]
            scores = dot(both(query), key, (1, 1)) * score_scale
            total = jnp.log(jnp.sum(jnp.exp(scores), axis=-1, keepdims=True))
            prob = jnp.exp(scores - total)
            probs[s, 2 * p] = prob[:length]
            probs[s, 2 * p + 1] = prob[length:]
            prob = prob.astype(b16)
            side = jnp.concatenate([prob[:length], prob[length:]], axis=1)
            mixed[rows, at : at + cut_head] = dot(side, both(value)).astype(b16)

    for s in range(slots):
        attend(s)
        if s + 1 < slots:
            until(min(ends[1] + s, ends[2] - 1), "end")
    branch[...] = dot(mixed[...], proj_weight()) + bias_rows[8:9, :]
    until(ends[2] - 1, "end")
    mod[2 * slots :, :] = dot(tail_cond, rows_of(all_ada, head_rows, tail_rows))
    add_mod_bias(2, 6)

    def norm_second(s):
        rows = slice(s * length, (s + 1) * length)
        after = x_ref[s] + part(s, 2) * branch[rows, :]
        dx[rows, :] = after
        normed, inverse = layer_norm(after)
        norm_two[rows, :] = normed
        inv_two[rows, :] = inverse
        h_two[rows, :] = (normed * (1.0 + part(s, 4)) + part(s, 3)).astype(b16)

    for s in range(slots):
        norm_second(s)

    note_rows = note_a.shape[4]
    own_lane = lax.broadcasted_iota(jnp.int32, (SUBLANES, width), 1)
    own_row = lax.broadcasted_iota(jnp.int32, (SUBLANES, width), 0)
    own_pick = jnp.where(own_lane == own_row + me * ada_rows, 1.0, 0.0).astype(b16)
    columns = dot(own_pick, rows_of(all_ada, 0, head_rows), (1, 1)).astype(b16)
    note_total = grid.count * note_rows
    at = lax.broadcasted_iota(jnp.int32, (1, note_total), 1)
    wanted = at // note_rows * head_rows + 1 + at % note_rows % slots
    source = lax.broadcasted_iota(jnp.int32, (head_total, note_total), 0)
    spread[...] = dot(columns, jnp.where(source == wanted, 1.0, 0.0).astype(b16)).astype(b16)

    def up(t):
        cols = slice(t * width, (t + 1) * width)
        pre = dot(h_two[...], one_weight(t)) + bias_rows[9 + t : 10 + t, :]
        square = pre * pre
        tanh_part = jnp.tanh(ROOT_TWO_OVER_PI * (pre + GELU_COEF * pre * square))
        half = 0.5 * (1.0 + tanh_part)
        act[:, cols] = (pre * half).astype(b16)
        slope[:, cols] = half + 0.5 * pre * (1.0 - tanh_part * tanh_part) * ROOT_TWO_OVER_PI * (
            1.0 + 3.0 * GELU_COEF * square
        )

    for k in range(per_core):
        until(ends[2] - 1 + -(-tall * (k + 1) // SUBLANES), "end")
        for core in range(pair):
            up(core * per_core + k)
    until(ends[3] - 1, "end")
    two_all = jnp.concatenate([two_weight(t) for t in range(parts)], axis=0)
    mlp[...] = dot(act[...], two_all) + bias_rows[9 + parts : 10 + parts, :]

    gbias[...] = jnp.zeros_like(gbias)
    last = gbias.shape[0] - 1
    cot_in.wait()

    def finish(s):
        rows = slice(s * length, (s + 1) * length)
        live = s < count
        value = mlp[rows, :]
        out_ref[s] = jnp.where(live, dx[rows, :] + part(s, 5) * value, 0.0)
        grad = jnp.where(live, cot_ref[s], 0.0)
        cot_ref[s] = grad
        dmod[5 * slots + s : 5 * slots + s + 1, :] = column_sum(grad * value)
        full = grad * part(s, 5)
        gbias[last : last + 1, :] += column_sum(full)
        small[rows, :] = full.astype(b16)

    for s in range(slots):
        finish(s)

    bufs_mlp = (grad_mlp, pair_mlp, acc_mlp, one_mlp, two_mlp, line_mlp, sum_mlp)
    bufs_attn = (grad_attn, pair_attn, acc_attn, one_attn, two_attn, line_attn, sum_attn)
    early = [(bufs_mlp, start, size) for _, start, size in cut_rows(all_mlp, 0, sizes.mlp_rows)]
    late = [(bufs_attn, start, size) for _, start, size in cut_rows(all_attn, 0, sizes.attn_rows)]
    reduces = [Reduce(mover, bufs, start, size, k % 2 == 0) for k, (bufs, start, size) in enumerate(early + late)]
    n_early, n_all = len(early), len(early) + len(late)
    note_first = Share(mover, note_a, 0, note_rows, True)
    note_last = Share(mover, note_b, 0, note_rows, False)

    def run(name, first, last):
        for reduce in reduces[first:last]:
            getattr(reduce, name)()

    def mlp_grads(t):
        cols = slice(t * width, (t + 1) * width)
        a, b, zs = two_place(t)
        grad_mlp[a, b, zs, :, :, :] = (
            dot(act[:, cols], small[...], (0, 0)).astype(b16).reshape(per_tile // pair, pair, sizes.mlp_rows, width)
        )

    def mlp_down(t):
        cols = slice(t * width, (t + 1) * width)
        full = dot(small[...], two_weight(t), (1, 1)) * slope[:, cols]
        gbias[3 + t : 4 + t, :] = column_sum(full)
        grad = full.astype(b16)
        wide[:, cols] = grad
        core, k = t // per_core, t % per_core
        whole = dot(h_two[...], grad, (0, 0)).astype(b16)
        for g in range(sizes.one_devices // group):
            grad_mlp[g // low, g % low, :, core, tall * k : tall * (k + 1), :] = whole[
                g * depth * tall : (g + 1) * depth * tall
            ].reshape(depth, tall, width)

    for t in range(parts):
        mlp_grads(t)
    sent = 0
    for k in range(per_core):
        for core in range(pair):
            mlp_down(core * per_core + k)
        ready = n_early if k + 1 == per_core else tall * (k + 1) // SUBLANES
        run("begin", sent, ready)
        sent = ready
    third = -(-n_early // 3)
    marks = [min(n_early, third * k) for k in range(4)]
    run("one", 0, marks[1])
    one_all = jnp.concatenate([one_weight(t) for t in range(parts)], axis=1)
    back[...] = dot(wide[...], one_all, (1, 1))
    run("one", marks[1], marks[2])

    def mlp_back(s):
        rows = slice(s * length, (s + 1) * length)
        grad_two = back[rows, :]
        normed = norm_two[rows, :]
        dmod[4 * slots + s : 4 * slots + s + 1, :] = column_sum(grad_two * normed)
        dmod[3 * slots + s : 3 * slots + s + 1, :] = column_sum(grad_two)
        after = cot_ref[s] + norm_backward(grad_two * (1.0 + part(s, 4)), normed, inv_two[rows, :])
        dx[rows, :] = after
        dmod[2 * slots + s : 2 * slots + s + 1, :] = column_sum(after * branch[rows, :])
        full = after * part(s, 2)
        gbias[2:3, :] += column_sum(full)
        small[rows, :] = full.astype(b16)

    for s in range(slots):
        mlp_back(s)
    note_a[hi, lo, z, c] = dmod[2 * slots :, :].astype(b16)
    run("two", 0, marks[1])
    note_first.begin()
    run("one", marks[2], marks[3])
    whole = dot(mixed[...], small[...], (0, 0)).astype(b16)
    for g in range(sizes.qkv_devices // group, grid.count // group):
        base = (g * group - sizes.qkv_devices) * sizes.attn_rows
        grad_attn[g // low, g % low] = whole[base : base + group * sizes.attn_rows].reshape(
            depth, pair, sizes.attn_rows, width
        )
    mixed[...] = dot(small[...], proj_weight(), (1, 1)).astype(b16)

    def attend_back(s):
        rows = slice(s * length, (s + 1) * length)
        for p in range(heads // 2):
            at = p * cut_head
            span = slice(at, at + cut_head)
            query = qkv[rows, span]
            key = qkv[rows, width + at : width + at + cut_head]
            value = qkv[rows, 2 * width + at : 2 * width + at + cut_head]
            grad = both(mixed[rows, span])
            prob = jnp.concatenate([probs[s, 2 * p], probs[s, 2 * p + 1]], axis=0)
            d_prob = dot(grad, value, (1, 1))
            d_value = dot(prob.astype(b16), grad, (0, 0)).astype(b16)
            delta = jnp.sum(prob * d_prob, axis=-1, keepdims=True)
            d_score = (prob * (d_prob - delta) * score_scale).astype(b16)
            side = jnp.concatenate([d_score[:length], d_score[length:]], axis=1)
            d_query = dot(side, both(key)).astype(b16)
            d_key = dot(d_score, both(query), (0, 0)).astype(b16)
            dqkv[rows, span] = d_query
            dqkv[rows, width + at : width + at + cut_head] = d_key
            dqkv[rows, 2 * width + at : 2 * width + at + cut_head] = d_value
            gbias[0:1, span] += column_sum(d_query.astype(f32))
            gbias[1:2, span] += column_sum(d_value.astype(f32))

    between = [
        lambda: (run("two", marks[1], marks[2]), note_first.first()),
        lambda: (run("three", 0, marks[1]), run("two", marks[2], marks[3])),
        lambda: (run("three", marks[1], marks[2]), note_first.second()),
        lambda: run("finish", 0, marks[1]),
    ]
    for s in range(slots):
        attend_back(s)
        if between:
            between.pop(0)()
    for action in between:
        action()
    for k in range(3):
        cols = slice(k * width, (k + 1) * width)
        whole = dot(h_one[...], dqkv[:, cols], (0, 0)).astype(b16)
        for g in range(sizes.qkv_devices // group):
            base = g * group * sizes.qkv_rows
            grad_attn[g // low, g % low, :, :, sizes.qkv_rows * k : sizes.qkv_rows * (k + 1), :] = whole[
                base : base + group * sizes.qkv_rows
            ].reshape(depth, pair, sizes.qkv_rows, width)
    run("begin", n_early, n_all)
    run("three", marks[2], marks[3])
    note_first.third()
    back[...] = dot(dqkv[:, 0:width], qkv_weight(0), (1, 1)) + (
        dot(dqkv[:, width : 2 * width], qkv_weight(1), (1, 1)) + dot(dqkv[:, 2 * width :], qkv_weight(2), (1, 1))
    )
    run("one", n_early, n_all)

    def attn_back(s):
        rows = slice(s * length, (s + 1) * length)
        grad_one = back[rows, :]
        normed = norm_one[rows, :]
        dmod[slots + s : slots + s + 1, :] = column_sum(grad_one * normed)
        dmod[s : s + 1, :] = column_sum(grad_one)
        gx_ref[s] = dx[rows, :] + norm_backward(grad_one * (1.0 + part(s, 1)), normed, inv_one[rows, :])

    for s in range(slots):
        attn_back(s)
    note_b[hi, lo, z, c] = jnp.concatenate([dmod[0 : 2 * slots, :], gbias[...]], axis=0).astype(b16)
    note_last.begin()
    run("finish", marks[1], marks[3])
    home = [
        mover.push(
            sum_mlp.at[pl.ds(pl.multiple_of(tall * k + one_rows * (1 - c), 8), one_rows)], back_in.at[k], partner
        )
        for k in range(per_core)
    ]
    run("two", n_early, n_all)
    note_last.first()
    note_first.end()

    def gather_entries(first, blocks, start, rows, total, span, skip, pick):
        grad_mod = dmod[first * slots : (first + blocks) * slots, :].astype(b16)
        values = dot(grad_mod, rows_of(all_ada, start, rows), (1, 1))
        values = jnp.where(owner_mask(total, span, skip, blocks), values, 0.0)
        merged = values[0:slots]
        for k in range(1, blocks):
            merged = merged + values[k * slots : (k + 1) * slots]
        upper_part = merged.astype(b16)
        lower_part = (merged - upper_part.astype(f32)).astype(b16)
        return dot(upper_part, pick[...], (1, 1)) + dot(lower_part, pick[...], (1, 1))

    grad_act = gather_entries(0, 2, 0, head_rows, head_total, head_rows, lead, pick_head)
    grad_act = grad_act + gather_entries(2, 4, head_rows, tail_rows, tail_total, tail_rows, 0, pick_tail)
    gcond_ref[...] = grad_act * silu_slope(cond)
    run("three", n_early, n_all)
    note_last.second()

    def from_notes(note, blocks, extra):
        kept = []
        entry = lax.broadcasted_iota(jnp.int32, (SUBLANES, note_total), 1) % note_rows
        for k in range(blocks):
            kept.append(jnp.where(entry // slots == k, spread[...].astype(f32), 0.0))
        line_at = lax.broadcasted_iota(jnp.int32, (SUBLANES, note_total), 0)
        wanted = jnp.where(entry < blocks * slots, entry // slots, entry - blocks * slots + blocks)
        kept.append(jnp.where(wanted == line_at, 1.0, 0.0))
        left = jnp.concatenate(kept, axis=0).astype(b16)
        return dot(left, rows_of(note, 0, note_rows))

    def store_ada(source, first, blocks):
        for k in range(blocks):
            for t in range(tiles):
                g_ada_out[pl.ds(tiles * (first + k) + t, ada_rows, stride=6 * tiles), :] = source[
                    k * SUBLANES : k * SUBLANES + ada_rows, lanes(t)
                ]

    early = from_notes(note_a, 4, 0)
    store_ada(early, 2, 4)
    arrive(home)
    for core in range(pair):
        @pl.when(jnp.logical_and(me < sizes.one_devices, c == core))
        def _():
            for k in range(per_core):
                for t in range(tiles):
                    own_at, far_at = per_core * core + k, per_core * (1 - core) + k
                    base = tall * k + one_rows * core
                    g_mlp_out[pl.ds(tiles * own_at + t, one_rows, stride=parts * tiles), :] = sum_mlp[
                        base : base + one_rows, lanes(t)
                    ]
                    g_mlp_out[pl.ds(tiles * far_at + t, one_rows, stride=parts * tiles), :] = back_in[k, :, lanes(t)]

    @pl.when(me >= sizes.one_devices)
    def _():
        for t in range(tiles):
            g_mlp_out[pl.ds(t, sizes.mlp_rows, stride=tiles), :] = sum_mlp[:, lanes(t)]

    note_last.third()
    run("finish", n_early, n_all)
    note_last.end()
    late = from_notes(note_b, 2, gbias.shape[0])
    store_ada(late, 0, 2)
    bias_rows[0:2, :] = late[2 * SUBLANES : 2 * SUBLANES + 2]
    bias_rows[2:6, :] = early[4 * SUBLANES : 4 * SUBLANES + 4]
    bias_rows[6 : 6 + gbias.shape[0], :] = late[2 * SUBLANES + 2 : 2 * SUBLANES + 2 + gbias.shape[0]]
    begin = me * sizes.bias
    row, shift = begin // width, begin % width
    pair_rows = jnp.concatenate(
        [bias_rows[pl.ds(row, 1), :], bias_rows[pl.ds(row + 1, 1), :]], axis=1
    )
    turned = pltpu.roll(pair_rows, 2 * width - shift, 1)
    for t in range(g_bias_out.shape[0]):
        g_bias_out[t : t + 1, :] = turned[:, lanes(t)]

    @pl.when(me < sizes.qkv_devices)
    def _():
        rows = sizes.qkv_rows
        for k in range(3):
            for t in range(tiles):
                g_attn_out[pl.ds(tiles * k + t, rows, stride=3 * tiles), :] = sum_attn[rows * k : rows * (k + 1), lanes(t)]

    @pl.when(me >= sizes.qkv_devices)
    def _():
        for t in range(tiles):
            g_attn_out[pl.ds(t, sizes.attn_rows, stride=tiles), :] = sum_attn[:, lanes(t)]

    mover.drain()
    assert len(mover.started) == send_sem.shape[0]


def run_fused(grid, sizes, counts, latents, conditioning, cotangent, shards, bias):
    slots, length, width, hidden = sizes.slots, sizes.length, sizes.width, sizes.hidden
    high, low, depth, pair = grid.sizes
    f32, b16 = jnp.float32, jnp.bfloat16
    rows = slots * length
    ada, attn, mlp = (shard.reshape(-1, LANES) for shard in shards)
    attn_rows, mlp_rows, one_rows = sizes.attn_rows, sizes.mlp_rows, sizes.one_rows
    ada_all = sizes.head_rows + sizes.tail_rows
    note_rows = 4 * slots
    extra = 4 + sizes.parts
    per_core = sizes.parts // pair
    side = max(high, low)
    tails = [(attn_rows, width), (mlp_rows, width)]
    leads = [
        (high, low, depth), (high, low, depth), (max(side - 1, 1), side, depth),
        (max(side - 1, 1), depth), (max(depth - 1, 1),),
    ]
    scratch = [(grid.sizes + (n, width), b16) for n in (ada_all, attn_rows, mlp_rows, note_rows, note_rows)]
    scratch += [(grid.sizes + tail, b16) for tail in tails]
    scratch += [(lead + tail, b16) for lead in leads for tail in tails]
    scratch += [(tail, f32) for tail in tails]
    cut = per_core * one_rows
    scratch += [((cut, width), b16), ((cut, width), b16), ((per_core, one_rows, width), f32)]
    scratch += [(latents.shape, f32)] * 2 + [(array.shape, b16) for array in (ada, attn, mlp)]
    scratch += [
        ((max(ada.shape[0], attn.shape[0], mlp.shape[0]), LANES), f32), ((max(mlp_rows, attn_rows, ada_all), width), f32),
        ((sizes.parts * one_rows, width), f32),
        ((width, grid.count * sizes.head_rows), b16), ((width, grid.count * sizes.tail_rows), b16),
        ((SUBLANES, grid.count * note_rows), b16), ((-(-(7 + extra) // 8) * 8, width), f32),
    ]
    scratch += [
        ((6 * slots, width), f32), ((rows, width), f32), ((rows, 1), f32), ((rows, width), b16),
        ((rows, 3 * width), b16), ((slots, HEADS, length, length), f32), ((rows, width), b16),
        ((rows, width), f32), ((rows, width), f32), ((rows, 1), f32), ((rows, width), b16),
        ((rows, hidden), f32), ((rows, hidden), b16), ((rows, width), f32), ((rows, hidden), b16),
        ((rows, width), f32), ((rows, width), f32), ((rows, width), b16), ((rows, 3 * width), b16),
        ((6 * slots, width), f32), ((extra, width), f32),
    ]
    ceil = lambda n: -(-n // SUBLANES)
    gathers = ceil(sizes.head_rows) + ceil(sizes.tail_rows) + ceil(attn_rows) + ceil(mlp_rows) + 2
    copies = gathers * Spread.copies(grid) + (ceil(attn_rows) + ceil(mlp_rows)) * (high + low + depth + pair - 4)
    copies += 1 + per_core
    vmem, anywhere = pl.BlockSpec(memory_space=pltpu.VMEM), pl.BlockSpec(memory_space=pl.ANY)
    far = pl.BlockSpec(memory_space=pltpu.HBM)
    outs = [
        (latents.shape, f32), (latents.shape, f32), (conditioning.shape, f32),
        (ada.shape, f32), (attn.shape, f32), (mlp.shape, f32), ((-(-bias.shape[1] // LANES), LANES), f32),
    ]
    pinned = lambda array: pltpu.with_memory_space_constraint(array, pltpu.HBM)
    results = pl.pallas_call(
        partial(fused_kernel, grid, sizes),
        out_shape=[jax.ShapeDtypeStruct(shape, kind) for shape, kind in outs],
        in_specs=[pl.BlockSpec(memory_space=pltpu.SMEM), far, vmem, far, far, far, far, vmem],
        out_specs=[vmem] * len(outs),
        scratch_shapes=[pltpu.VMEM(shape, kind) for shape, kind in scratch]
        + [pltpu.SemaphoreType.DMA((copies,)), pltpu.SemaphoreType.DMA((copies,)), pltpu.SemaphoreType.DMA((5,))],
        compiler_params=pltpu.CompilerParams(
            collective_id=2, has_side_effects=True, vmem_limit_bytes=50 * 1024 * 1024
        ),
    )(counts, pinned(latents), conditioning, pinned(cotangent), pinned(ada), pinned(attn), pinned(mlp), bias)
    return pl.pallas_call(
        hand_on,
        out_shape=[jax.ShapeDtypeStruct(shape, kind) for shape, kind in outs],
        in_specs=[anywhere] * len(outs),
        out_specs=[far] * len(outs),
        scratch_shapes=[pltpu.SemaphoreType.DMA((len(outs),))],
        compiler_params=pltpu.CompilerParams(vmem_limit_bytes=4 * 1024 * 1024),
    )(*results)


def hand_on(*refs):
    ins, outs, sem = refs[: len(refs) // 2], refs[len(refs) // 2 : -1], refs[-1]
    copies = [pltpu.make_async_copy(a, b, sem.at[n]) for n, (a, b) in enumerate(zip(ins, outs))]
    for copy in copies:
        copy.start()
    for copy in copies:
        copy.wait()


def local(
    grid, latents, conditioning, counts, cotangent, ada_weights, attn_weights, mlp_weights, flat_biases
):
    model_width = latents.shape[-1]
    slots = latents.shape[0]
    shards = (ada_weights, attn_weights, mlp_weights, flat_biases)
    sizes = Sizes(grid, latents, shards)
    if sizes.fits:
        outs = run_fused(
            grid, sizes, counts, latents, conditioning, cotangent, shards[:3], flat_biases[None]
        )
        return tuple(outs[:3]) + tuple(
            total.reshape(-1)[: shard.shape[0]] for total, shard in zip(outs[3:], shards)
        )
    whole_ada, whole_attn, whole_mlp, whole_bias = gather_all(
        grid, [pack([shard], ()) for shard in shards]
    )
    bias_flat = whole_bias.reshape(grid.count, -1)[:, : flat_biases.shape[0]].reshape(-1)
    weights = (
        whole_ada.reshape(model_width, 6 * model_width),
        whole_attn.reshape(-1, LANES),
        whole_mlp.reshape(-1, LANES),
    )
    biases = bias_flat.astype(jnp.float32)[None]
    output, grad_latents, grad_conditioning, cond_act, grad_mod, g_attn, g_mlp, g_bias = (
        run_block(counts, latents, conditioning, cotangent, weights, biases)
    )

    gap = padded_rows(flat_biases.shape[0]) * LANES - flat_biases.shape[0]
    bias_lines = jnp.pad(
        g_bias.astype(jnp.bfloat16).reshape(grid.count, -1), ((0, 0), (0, gap))
    )
    all_mod, all_act, *sums = scatter_sum(
        grid,
        [flat.reshape(grid.sizes + (-1, LANES)) for flat in (g_attn, g_mlp, bias_lines)],
        [grad_mod, cond_act],
    )
    all_mod = all_mod.reshape(grid.count * slots, -1)
    all_act = all_act.reshape(grid.count * slots, -1)
    grads = [own_rows(all_act, all_mod, ada_weights.shape[0])]
    grads += [total.reshape(-1)[: shard.shape[0]] for total, shard in zip(sums, shards[1:])]
    return (output, grad_latents, grad_conditioning) + tuple(grads)


def own_rows(left, right, extent):
    wide = right.shape[1]
    start = lax.axis_index(AXES) * extent
    rows = min(-(-extent // wide) + (1 if extent % wide else 0), left.shape[1])
    top = jnp.minimum(start // wide, left.shape[1] - rows)
    part = lax.dynamic_slice_in_dim(left, top, rows, 1)
    whole = dot(part, right, (0, 0)).reshape(-1)
    if rows * wide == extent:
        return whole
    return lax.dynamic_slice_in_dim(whole, start - top * wide, extent, 0)


def solution(mesh):
    in_specs = (
        P(("dp", "fsdp"), None, None),
        P(("dp", "fsdp"), None),
        P(("dp", "fsdp")),
        P(("dp", "fsdp"), None, None),
        P(("dp", "fsdp")),
        P(("dp", "fsdp")),
        P(("dp", "fsdp")),
        P(("dp", "fsdp")),
    )
    out_specs = (
        P(("dp", "fsdp"), None, None),
        P(("dp", "fsdp"), None, None),
        P(("dp", "fsdp"), None),
        P(("dp", "fsdp")),
        P(("dp", "fsdp")),
        P(("dp", "fsdp")),
        P(("dp", "fsdp")),
    )
    return jax.shard_map(partial(local, Grid(mesh)), mesh=mesh, in_specs=in_specs, out_specs=out_specs, check_vma=False)
```

```python
from functools import partial
import math

import jax
import jax.numpy as jnp
from jax import lax
from jax.experimental import pallas as pl
from jax.experimental.pallas import tpu as pltpu
from jax.sharding import PartitionSpec as P

FF = 1536
HEADS = 6


EPSILON = 1e-06
GELU_COEF = 0.044715
ROOT_TWO_OVER_PI = 0.7978845608028654


def layer_norm(values):
    centre = values - jnp.mean(values, axis=-1, keepdims=True)
    inverse = lax.rsqrt(jnp.mean(centre * centre, axis=-1, keepdims=True) + EPSILON)
    return (centre * inverse, inverse)


def norm_backward(grad_norm, normed, inverse):
    first = jnp.mean(grad_norm, axis=-1, keepdims=True)
    second = jnp.mean(grad_norm * normed, axis=-1, keepdims=True)
    return (grad_norm - first - normed * second) * inverse


def gelu_value(pre_act):
    inner = ROOT_TWO_OVER_PI * (pre_act + GELU_COEF * pre_act * pre_act * pre_act)
    return 0.5 * pre_act * (1.0 + jnp.tanh(inner))


def gelu_slope(pre_act):
    tanh_part = jnp.tanh(ROOT_TWO_OVER_PI * (pre_act + GELU_COEF * pre_act * pre_act * pre_act))
    return 0.5 * (1.0 + tanh_part) + 0.5 * pre_act * (
        1.0 - tanh_part * tanh_part
    ) * ROOT_TWO_OVER_PI * (1.0 + 3.0 * GELU_COEF * pre_act * pre_act)


def silu_slope(values):
    sigma = jax.nn.sigmoid(values)
    return sigma * (1.0 + values * (1.0 - sigma))


LANES = 128
SUBLANES = 16
AXES = ("dp", "fsdp")
MESH = pl.DeviceIdType.MESH


class Grid:
    def __init__(self, mesh):
        dp, fsdp = mesh.shape["dp"], mesh.shape["fsdp"]
        side = math.isqrt(dp)
        self.high = side if side * side == dp else 1
        self.low = dp // self.high
        self.pair = 2 if fsdp % 2 == 0 else 1
        self.depth = fsdp // self.pair
        self.count = dp * fsdp
        self.sizes = (self.high, self.low, self.depth, self.pair)

    def here(self):
        a, f = lax.axis_index("dp"), lax.axis_index("fsdp")
        return [a // self.low, a % self.low, f // self.pair, f % self.pair]

    def peer(self, here, axis, step):
        spot = list(here)
        spot[axis] = lax.rem(here[axis] + step, self.sizes[axis])
        return spot

    def ident(self, spot):
        return (spot[0] * self.low + spot[1], spot[2] * self.pair + spot[3])

    def greet(self, here):
        sem = pltpu.get_barrier_semaphore()
        total = 0
        for axis in range(4):
            for step in range(1, self.sizes[axis]):
                pl.semaphore_signal(
                    sem, inc=1, device_id=self.ident(self.peer(here, axis, step)), device_id_type=MESH
                )
                total += 1
        return lambda: pl.semaphore_wait(sem, total)

    def barrier(self, here):
        self.greet(here)()


def chunk_rows(arrays):
    chunks = []
    for n, array in enumerate(arrays):
        rows = array.shape[-2]
        if rows % (2 * SUBLANES) == 0:
            chunks += [(n, 0, rows // 2), (n, rows // 2, rows // 2)]
        else:
            chunks.append((n, 0, rows))
    return chunks


class Mover:
    def __init__(self, grid, send_sem, recv_sem):
        self.grid, self.here = grid, grid.here()
        self.send_sem, self.recv_sem = send_sem, recv_sem
        self.started = []

    def push(self, src, dst, spot):
        k = len(self.started)
        copy = pltpu.make_async_remote_copy(
            src_ref=src, dst_ref=dst, send_sem=self.send_sem.at[k], recv_sem=self.recv_sem.at[k],
            device_id=self.grid.ident(spot), device_id_type=MESH,
        )
        copy.start()
        self.started.append(copy)
        return copy

    def spots(self, axis):
        return [self.grid.peer(self.here, axis, s) for s in range(1, self.grid.sizes[axis])]

    def pushes(self, ref, axis):
        return [self.push(ref, ref, spot) for spot in self.spots(axis)]

    def drain(self):
        for copy in self.started:
            copy.wait_send()


def arrive(copies):
    for copy in copies:
        copy.wait_recv()


class Spread:
    def __init__(self, mover, in_ref, out_ref, rows, low_first):
        self.mover, self.in_ref, self.out_ref, self.rows = mover, in_ref, out_ref, rows
        self.low_first = low_first
        self.swap = []

    def begin(self):
        hi, lo, z, c = self.mover.here
        src, dst = self.in_ref.at[self.rows], self.out_ref.at[hi, lo, z, c, self.rows]
        self.pending = [self.mover.push(src, dst, spot) for spot in self.mover.spots(2)]

    def first(self):
        hi, lo, z, c = self.mover.here
        arrive(self.pending)
        part = self.out_ref.at[hi, lo, :, c, self.rows]
        self.pending = self.mover.pushes(part, 1 if self.low_first else 0)
        self.swap += self.mover.pushes(part, 3)

    def second(self):
        hi, lo, z, c = self.mover.here
        arrive(self.pending)
        out, rows = self.out_ref, self.rows
        if self.low_first:
            self.pending = self.mover.pushes(out.at[hi, :, :, c, rows], 0)
            others = [out.at[hi, spot[1], :, c, rows] for spot in self.mover.spots(1)]
        else:
            self.pending = self.mover.pushes(out.at[:, lo, :, c, rows], 1)
            others = [out.at[spot[0], lo, :, c, rows] for spot in self.mover.spots(0)]
        for other in others:
            self.swap += self.mover.pushes(other, 3)

    def third(self):
        hi, lo, z, c = self.mover.here
        arrive(self.pending)
        out, rows = self.out_ref, self.rows
        if self.low_first:
            others = [out.at[spot[0], :, :, c, rows] for spot in self.mover.spots(0)]
        else:
            others = [out.at[:, spot[1], :, c, rows] for spot in self.mover.spots(1)]
        for other in others:
            self.swap += self.mover.pushes(other, 3)

    def end(self):
        arrive(self.swap)

    @staticmethod
    def copies(grid):
        high, low, depth, pair = grid.sizes
        return depth - 1 + (high + low - 2) + (pair - 1) * (1 + high + low - 2)


def gather_kernel(grid, chunks, arrays, *refs):
    in_refs, out_refs = refs[:arrays], refs[arrays : 2 * arrays]
    send_sem, recv_sem, own_sem = refs[2 * arrays :]
    mover = Mover(grid, send_sem, recv_sem)
    hi, lo, z, c = mover.here
    grid.barrier(mover.here)
    own = [
        pltpu.make_async_copy(in_refs[n], out_refs[n].at[hi, lo, z, c], own_sem.at[n])
        for n in range(arrays)
    ]
    for copy in own:
        copy.start()
    spreads = [
        Spread(mover, in_refs[n], out_refs[n], pl.ds(start, size), k % 2 == 0)
        for k, (n, start, size) in enumerate(chunks)
    ]
    for spread in spreads:
        spread.begin()
    for copy in own:
        copy.wait()
    for spread in spreads:
        spread.first()
    for spread in spreads:
        spread.second()
    for spread in spreads:
        spread.third()
    for spread in spreads:
        spread.end()
    mover.drain()


def gather_all(grid, arrays):
    chunks = chunk_rows(arrays)
    copies = Spread.copies(grid) * len(chunks)
    vmem = pl.BlockSpec(memory_space=pltpu.VMEM)
    return pl.pallas_call(
        partial(gather_kernel, grid, chunks, len(arrays)),
        out_shape=[jax.ShapeDtypeStruct(grid.sizes + array.shape, array.dtype) for array in arrays],
        in_specs=[vmem] * len(arrays),
        out_specs=[vmem] * len(arrays),
        scratch_shapes=[
            pltpu.SemaphoreType.DMA((copies,)),
            pltpu.SemaphoreType.DMA((copies,)),
            pltpu.SemaphoreType.DMA((len(arrays),)),
        ],
        compiler_params=pltpu.CompilerParams(
            collective_id=0, has_side_effects=True, vmem_limit_bytes=48 * 1024 * 1024
        ),
    )(*arrays)


def scatter_kernel(grid, chunks, arrays, extra, *refs):
    note_refs, refs = refs[:extra], refs[extra:]
    g_refs, refs = refs[:arrays], refs[arrays:]
    note_outs, refs = refs[:extra], refs[extra:]
    out_refs, refs = refs[:arrays], refs[arrays:]
    pair_bufs, refs = refs[:arrays], refs[arrays:]
    accs, refs = refs[:arrays], refs[arrays:]
    one_bufs, refs = refs[:arrays], refs[arrays:]
    two_bufs, refs = refs[:arrays], refs[arrays:]
    z_bufs, (send_sem, recv_sem, own_sem) = refs[:arrays], refs[arrays:]
    mover = Mover(grid, send_sem, recv_sem)
    here, push = mover.here, mover.push
    hi, lo, z, c = here
    grid.barrier(here)
    owns = [
        pltpu.make_async_copy(note_refs[n], note_outs[n].at[hi, lo, z, c], own_sem.at[n])
        for n in range(extra)
    ]
    notes = [
        Spread(mover, note_refs[n], note_outs[n], pl.ds(0, note_refs[n].shape[0]), n % 2 == 0)
        for n in range(extra)
    ]
    for own, note in zip(owns, notes):
        own.start()
        note.begin()

    def steps(axis):
        return [(s - 1, grid.peer(here, axis, s)) for s in range(1, grid.sizes[axis])]

    def add(into, terms, first, second):
        def body(t, _):
            i, j = t // second, t % second
            total = terms[0](i, j)[...].astype(jnp.float32)
            for term in terms[1:]:
                total = total + term(i, j)[...].astype(jnp.float32)
            target = into(i, j)
            target[...] = total.astype(target.dtype)
            return 0

        lax.fori_loop(0, first * second, body, 0)

    high, low, depth, pair = grid.sizes
    swaps, ones, twos, lines = [], [], [], []
    for n, start, size in chunks:
        rows = pl.ds(start, size)
        g_ref, pair_buf = g_refs[n], pair_bufs[n]
        swaps.append(
            [push(g_ref.at[:, :, :, spot[3], rows], pair_buf.at[:, :, :, rows], spot) for _, spot in steps(3)]
        )
    for own, note in zip(owns, notes):
        own.wait()
        note.first()
    for k, (n, start, size) in enumerate(chunks):
        rows = pl.ds(start, size)
        g_ref, pair_buf, acc, buf_one = g_refs[n], pair_bufs[n], accs[n], one_bufs[n]
        arrive(swaps[k])
        terms = [lambda i, j: g_ref.at[i // low, i % low, j, c, rows]]
        if pair > 1:
            terms.append(lambda i, j: pair_buf.at[i // low, i % low, j, rows])
        add(lambda i, j: acc.at[i // low, i % low, j, rows], terms, high * low, depth)
        if k % 2 == 0:
            ones.append(
                [push(acc.at[spot[0], :, :, rows], buf_one.at[s, 0:low, :, rows], spot) for s, spot in steps(0)]
            )
        else:
            ones.append(
                [push(acc.at[:, spot[1], :, rows], buf_one.at[s, 0:high, :, rows], spot) for s, spot in steps(1)]
            )
    for note in notes:
        note.second()
    for k, (n, start, size) in enumerate(chunks):
        rows = pl.ds(start, size)
        acc, buf_one, buf_two = accs[n], one_bufs[n], two_bufs[n]
        arrive(ones[k])
        even = k % 2 == 0
        mine = (lambda i, j: acc.at[hi, i, j, rows]) if even else (lambda i, j: acc.at[i, lo, j, rows])
        terms = [mine] + [
            (lambda i, j, s=s: buf_one.at[s, i, j, rows]) for s, _ in steps(0 if even else 1)
        ]
        add(mine, terms, low if even else high, depth)
        if even:
            twos.append(
                [push(acc.at[hi, spot[1], :, rows], buf_two.at[s, :, rows], spot) for s, spot in steps(1)]
            )
        else:
            twos.append(
                [push(acc.at[spot[0], lo, :, rows], buf_two.at[s, :, rows], spot) for s, spot in steps(0)]
            )
    for note in notes:
        note.third()
    for k, (n, start, size) in enumerate(chunks):
        rows = pl.ds(start, size)
        acc, buf_two, buf_z = accs[n], two_bufs[n], z_bufs[n]
        arrive(twos[k])
        mine = lambda i, j: acc.at[hi, lo, j, rows]
        terms = [mine] + [
            (lambda i, j, s=s: buf_two.at[s, j, rows]) for s, _ in steps(1 if k % 2 == 0 else 0)
        ]
        add(mine, terms, 1, depth)
        lines.append(
            [push(acc.at[hi, lo, spot[2], rows], buf_z.at[s, rows], spot) for s, spot in steps(2)]
        )
    for k, (n, start, size) in enumerate(chunks):
        rows = pl.ds(start, size)
        acc, buf_z = accs[n], z_bufs[n]
        arrive(lines[k])
        total = acc[hi, lo, z, rows].astype(jnp.float32)
        for s in range(depth - 1):
            total = total + buf_z[s, rows].astype(jnp.float32)
        out_refs[n][rows, :] = total
    for note in notes:
        note.end()
    mover.drain()


def scatter_sum(grid, arrays, notes):
    high, low, depth, pair = grid.sizes
    chunks = chunk_rows(arrays)
    copies = len(chunks) * (high + low + depth + pair - 4) + Spread.copies(grid) * len(notes)
    kind = arrays[0].dtype
    tails = [array.shape[-2:] for array in arrays]
    side = max(high, low)
    shapes = [
        (high, low, depth), (high, low, depth), (max(side - 1, 1), side, depth),
        (max(side - 1, 1), depth), (max(depth - 1, 1),),
    ]
    vmem = pl.BlockSpec(memory_space=pltpu.VMEM)
    return pl.pallas_call(
        partial(scatter_kernel, grid, chunks, len(arrays), len(notes)),
        out_shape=[jax.ShapeDtypeStruct(grid.sizes + note.shape, note.dtype) for note in notes]
        + [jax.ShapeDtypeStruct(tail, jnp.float32) for tail in tails],
        in_specs=[vmem] * (len(notes) + len(arrays)),
        out_specs=[vmem] * (len(notes) + len(arrays)),
        scratch_shapes=[pltpu.VMEM(shape + tail, kind) for shape in shapes for tail in tails]
        + [pltpu.SemaphoreType.DMA((copies,)), pltpu.SemaphoreType.DMA((copies,)), pltpu.SemaphoreType.DMA((len(notes),))],
        compiler_params=pltpu.CompilerParams(
            collective_id=1, has_side_effects=True, vmem_limit_bytes=48 * 1024 * 1024
        ),
    )(*notes, *arrays)


def padded_rows(extent):
    return -(-extent // LANES)


def pack(pieces, lead):
    parts = []
    for piece in pieces:
        extent = piece.shape[-1]
        rows = padded_rows(extent)
        gap = rows * LANES - extent
        if gap:
            piece = jnp.pad(piece, [(0, 0)] * len(lead) + [(0, gap)])
        parts.append(piece.reshape(lead + (rows, LANES)))
    if len(parts) == 1:
        return parts[0]
    return jnp.concatenate(parts, axis=-2)


def dot(left, right, contract=(1, 0)):
    return lax.dot_general(
        left, right, (((contract[0],), (contract[1],)), ((), ())), preferred_element_type=jnp.float32
    )


def block_kernel(
    count_ref, x_ref, cond_ref, cot_ref, w_ada, attn_ref, mlp_ref, bias_ref,
    out_ref, gx_ref, gcond_ref, act_ref, dmod_ref, g_attn, g_mlp, gbias_ref,
    line, w_qkv, w_proj, w_one, w_two, g_qkv, g_proj, g_one, g_two,
    mod, norm_one, inv_one, h_one, qkv, probs, mixed, branch, norm_two, inv_two, h_two,
    pre, act, mlp, wide, back, dx, small, dqkv, dmod,
):
    slots, length, width = x_ref.shape
    hidden = w_one.shape[1]
    rows_all = slots * length
    heads = probs.shape[1]
    head_dim = width // heads
    score_scale = head_dim ** (-0.5)
    f32, b16 = jnp.float32, jnp.bfloat16
    tile = 256 if hidden % 256 == 0 else hidden
    count = count_ref[0]
    o_query, o_value = 6 * width, 7 * width
    o_proj, o_one, o_two = 8 * width, 9 * width, 9 * width + hidden
    lane = lax.broadcasted_iota(jnp.int32, (length, 2 * head_dim), 1)
    lower = lane < head_dim

    def slot_loop(body):
        def step(s, _):
            body(s, pl.ds(pl.multiple_of(s * length, length), length))
            return 0

        lax.fori_loop(0, slots, step, 0)

    def part(s, k):
        return mod[pl.ds(s, 1), k * width : (k + 1) * width]

    def only(pair_block, first):
        return jnp.where(lower if first else jnp.logical_not(lower), pair_block, jnp.zeros_like(pair_block))

    def column_sum(values):
        return jnp.sum(values, axis=0, keepdims=True)

    def load_matrix(flat_ref, top, matrix):
        height, across = matrix.shape[0], matrix.shape[1] // LANES
        total = height * across

        def widen(t, _):
            at = pl.multiple_of(t * LANES, LANES)
            line[pl.ds(at, LANES), :] = flat_ref[pl.ds(top + at, LANES), :].astype(f32)
            return 0

        lax.fori_loop(0, total // LANES, widen, 0)
        for j in range(across):
            matrix[:, j * LANES : (j + 1) * LANES] = line[pl.ds(j, height, stride=across), :].astype(b16)

    def store_matrix(matrix, flat_ref, top):
        height, across = matrix.shape[0], matrix.shape[1] // LANES
        total = height * across
        for j in range(across):
            line[pl.ds(j, height, stride=across), :] = matrix[:, j * LANES : (j + 1) * LANES].astype(f32)

        def narrow(t, _):
            at = pl.multiple_of(t * LANES, LANES)
            flat_ref[pl.ds(top + at, LANES), :] = line[pl.ds(at, LANES), :].astype(b16)
            return 0

        lax.fori_loop(0, total // LANES, narrow, 0)

    proj_top, two_top = 3 * width * width // LANES, width * hidden // LANES
    load_matrix(attn_ref, 0, w_qkv)
    load_matrix(attn_ref, proj_top, w_proj)
    load_matrix(mlp_ref, 0, w_one)
    load_matrix(mlp_ref, two_top, w_two)
    cond = cond_ref[...]
    cond_act = (cond * jax.nn.sigmoid(cond)).astype(b16)
    mod[...] = dot(cond_act, w_ada[...]) + bias_ref[:, : 6 * width]

    def norm_first(s, rows):
        normed, inverse = layer_norm(x_ref[s])
        norm_one[rows, :] = normed
        inv_one[rows, :] = inverse
        h_one[rows, :] = (normed * (1.0 + part(s, 1)) + part(s, 0)).astype(b16)

    slot_loop(norm_first)
    for k, offset in enumerate((o_query, None, o_value)):
        cols = slice(k * width, (k + 1) * width)
        value = dot(h_one[...], w_qkv[:, cols])
        if offset is not None:
            value = value + bias_ref[:, offset : offset + width]
        qkv[:, cols] = value.astype(b16)

    def attend(s, rows):
        for pair in range(heads // 2):
            at = pair * 2 * head_dim
            query = qkv[rows, at : at + 2 * head_dim]
            key = qkv[rows, width + at : width + at + 2 * head_dim]
            value = qkv[rows, 2 * width + at : 2 * width + at + 2 * head_dim]
            halves = []
            for h in range(2):
                scores = dot(only(query, h == 0), key, (1, 1)) * score_scale
                total = jnp.log(jnp.sum(jnp.exp(scores), axis=-1, keepdims=True))
                prob = jnp.exp(scores - total)
                probs[s, 2 * pair + h] = prob
                halves.append(dot(prob.astype(b16), value))
            mixed[rows, at : at + 2 * head_dim] = jnp.where(lower, halves[0], halves[1]).astype(b16)

    slot_loop(attend)
    branch[...] = dot(mixed[...], w_proj[...]) + bias_ref[:, o_proj : o_proj + width]

    def norm_second(s, rows):
        after = x_ref[s] + part(s, 2) * branch[rows, :]
        dx[rows, :] = after
        normed, inverse = layer_norm(after)
        norm_two[rows, :] = normed
        inv_two[rows, :] = inverse
        h_two[rows, :] = (normed * (1.0 + part(s, 4)) + part(s, 3)).astype(b16)

    slot_loop(norm_second)

    def up(t, _):
        cols = pl.ds(pl.multiple_of(t * tile, tile), tile)
        shift = bias_ref[:, pl.ds(pl.multiple_of(o_one + t * tile, LANES), tile)]
        value = dot(h_two[...], w_one[:, cols]) + shift
        pre[:, cols] = value
        act[:, cols] = gelu_value(value).astype(b16)
        return 0

    lax.fori_loop(0, hidden // tile, up, 0)
    mlp[...] = dot(act[...], w_two[...]) + bias_ref[:, o_two : o_two + width]

    gbias_ref[...] = jnp.zeros_like(gbias_ref)

    def finish(s, rows):
        live = s < count
        value = mlp[rows, :]
        out_ref[s] = jnp.where(live, dx[rows, :] + part(s, 5) * value, 0.0)
        grad = jnp.where(live, cot_ref[s], 0.0)
        dmod[pl.ds(s, 1), 5 * width :] = column_sum(grad * value)
        full = grad * part(s, 5)
        gbias_ref[:, o_two : o_two + width] += column_sum(full)
        small[rows, :] = full.astype(b16)

    slot_loop(finish)

    def down(t, _):
        cols = pl.ds(pl.multiple_of(t * tile, tile), tile)
        full = dot(small[...], w_two[cols, :], (1, 1)) * gelu_slope(pre[:, cols])
        gbias_ref[:, pl.ds(pl.multiple_of(o_one + t * tile, LANES), tile)] = column_sum(full)
        grad = full.astype(b16)
        wide[:, cols] = grad
        g_two[cols, :] = dot(act[:, cols], small[...], (0, 0)).astype(g_two.dtype)
        g_one[:, cols] = dot(h_two[...], grad, (0, 0)).astype(g_one.dtype)
        return 0

    lax.fori_loop(0, hidden // tile, down, 0)
    back[...] = dot(wide[...], w_one[...], (1, 1))

    def mlp_back(s, rows):
        grad_two = back[rows, :]
        normed = norm_two[rows, :]
        dmod[pl.ds(s, 1), 4 * width : 5 * width] = column_sum(grad_two * normed)
        dmod[pl.ds(s, 1), 3 * width : 4 * width] = column_sum(grad_two)
        after = jnp.where(s < count, cot_ref[s], 0.0) + norm_backward(
            grad_two * (1.0 + part(s, 4)), normed, inv_two[rows, :]
        )
        dx[rows, :] = after
        dmod[pl.ds(s, 1), 2 * width : 3 * width] = column_sum(after * branch[rows, :])
        full = after * part(s, 2)
        gbias_ref[:, o_proj : o_proj + width] += column_sum(full)
        small[rows, :] = full.astype(b16)

    slot_loop(mlp_back)
    g_proj[...] = dot(mixed[...], small[...], (0, 0)).astype(g_proj.dtype)
    mixed[...] = dot(small[...], w_proj[...], (1, 1)).astype(b16)

    def attend_back(s, rows):
        for pair in range(heads // 2):
            at = pair * 2 * head_dim
            span = slice(at, at + 2 * head_dim)
            query = qkv[rows, span]
            key = qkv[rows, width + at : width + at + 2 * head_dim]
            value = qkv[rows, 2 * width + at : 2 * width + at + 2 * head_dim]
            grad = mixed[rows, span]
            d_query, d_key, d_value = [], [], []
            for h in range(2):
                prob = probs[s, 2 * pair + h]
                d_prob = dot(only(grad, h == 0), value, (1, 1))
                d_value.append(dot(prob.astype(b16), grad, (0, 0)))
                delta = jnp.sum(prob * d_prob, axis=-1, keepdims=True)
                d_score = (prob * (d_prob - delta) * score_scale).astype(b16)
                d_query.append(dot(d_score, key))
                d_key.append(dot(d_score, query, (0, 0)))
            d_query = jnp.where(lower, d_query[0], d_query[1]).astype(b16)
            d_key = jnp.where(lower, d_key[0], d_key[1]).astype(b16)
            d_value = jnp.where(lower, d_value[0], d_value[1]).astype(b16)
            dqkv[rows, span] = d_query
            dqkv[rows, width + at : width + at + 2 * head_dim] = d_key
            dqkv[rows, 2 * width + at : 2 * width + at + 2 * head_dim] = d_value
            gbias_ref[:, o_query + at : o_query + at + 2 * head_dim] += column_sum(d_query.astype(f32))
            gbias_ref[:, o_value + at : o_value + at + 2 * head_dim] += column_sum(d_value.astype(f32))

    slot_loop(attend_back)
    for k in range(3):
        cols = slice(k * width, (k + 1) * width)
        g_qkv[:, cols] = dot(h_one[...], dqkv[:, cols], (0, 0)).astype(g_qkv.dtype)
    back[...] = dot(dqkv[...], w_qkv[...], (1, 1))

    def attn_back(s, rows):
        grad_one = back[rows, :]
        normed = norm_one[rows, :]
        dmod[pl.ds(s, 1), width : 2 * width] = column_sum(grad_one * normed)
        dmod[pl.ds(s, 1), :width] = column_sum(grad_one)
        gx_ref[s] = dx[rows, :] + norm_backward(
            grad_one * (1.0 + part(s, 1)), normed, inv_one[rows, :]
        )

    slot_loop(attn_back)
    gbias_ref[:, : 6 * width] = column_sum(dmod[...])
    grad_mod = dmod[...].astype(b16)
    store_matrix(g_qkv, g_attn, 0)
    store_matrix(g_proj, g_attn, proj_top)
    store_matrix(g_one, g_mlp, 0)
    store_matrix(g_two, g_mlp, two_top)
    act_ref[...] = cond_act
    dmod_ref[...] = grad_mod
    gcond_ref[...] = dot(grad_mod, w_ada[...], (1, 1)) * silu_slope(cond)


def run_block(counts, latents, conditioning, cotangent, weights, biases):
    slots, length, width = latents.shape
    w_ada, attn, mlp = weights
    hidden = mlp.size // (2 * width)
    rows = slots * length
    f32, b16 = jnp.float32, jnp.bfloat16
    outs = [
        (latents.shape, f32), (latents.shape, f32), (conditioning.shape, f32),
        (conditioning.shape, b16), ((slots, 6 * width), b16),
        (attn.shape, b16), (mlp.shape, b16), (biases.shape, f32),
    ]
    matrices = [(width, 3 * width), (width, width), (width, hidden), (hidden, width)]
    scratch = [((max(h * w for h, w in matrices) // LANES, LANES), f32)]
    scratch += [(shape, b16) for shape in matrices + matrices]
    scratch += [
        ((slots, 6 * width), f32), ((rows, width), f32), ((rows, 1), f32), ((rows, width), b16),
        ((rows, 3 * width), b16), ((slots, HEADS, length, length), f32), ((rows, width), b16),
        ((rows, width), f32), ((rows, width), f32), ((rows, 1), f32), ((rows, width), b16),
        ((rows, hidden), f32), ((rows, hidden), b16), ((rows, width), f32), ((rows, hidden), b16),
        ((rows, width), f32), ((rows, width), f32), ((rows, width), b16), ((rows, 3 * width), b16),
        ((slots, 6 * width), f32),
    ]
    vmem = pl.BlockSpec(memory_space=pltpu.VMEM)
    return pl.pallas_call(
        block_kernel,
        out_shape=[jax.ShapeDtypeStruct(shape, kind) for shape, kind in outs],
        in_specs=[pl.BlockSpec(memory_space=pltpu.SMEM)] + [vmem] * 7,
        out_specs=[vmem] * len(outs),
        scratch_shapes=[pltpu.VMEM(shape, kind) for shape, kind in scratch],
        compiler_params=pltpu.CompilerParams(vmem_limit_bytes=60 * 1024 * 1024),
    )(counts, latents, conditioning, cotangent, *weights, biases)


LAG = 3


class Share:
    def __init__(self, mover, ref, start, size, axes):
        self.mover, self.ref, self.rows, self.axes = mover, ref, pl.ds(start, size), axes
        self.spot, self.stage, self.swap = list(mover.here[:3]), 0, []

    def at(self, spot):
        return self.ref.at[spot[0], spot[1], spot[2], self.mover.here[3], self.rows]

    def begin(self):
        self.pending = self.mover.pushes(self.at(self.spot), self.axes[self.stage])

    def absorb(self):
        arrive(self.pending)
        axis, spot = self.axes[self.stage], list(self.spot)
        self.spot[axis] = slice(None)
        if self.stage == 0:
            news = [self.spot]
        else:
            news = [spot[:axis] + [peer[axis]] + spot[axis + 1 :] for peer in self.mover.spots(axis)]
        news = [list(new) for new in news]
        self.stage += 1
        if self.stage < 3:
            self.begin()
        for new in news:
            self.swap += self.mover.pushes(self.at(new), 3)

    first = second = third = absorb

    def end(self):
        arrive(self.swap)

    @staticmethod
    def copies(grid, axes):
        one, two, three = (grid.sizes[axis] - 1 for axis in axes)
        return one + two + three + (grid.pair - 1) * (1 + two + three)


def axis_order(k):
    if k % 6 in (4, 5):
        return (1, 2, 0) if k % 2 == 0 else (0, 2, 1)
    return (2, 1, 0) if k % 2 == 0 else (2, 0, 1)


class Reduce:
    def __init__(self, mover, bufs, start, size, even):
        self.mover, self.even = mover, even
        self.grad, self.pair, self.acc, self.one_buf, self.two_buf, self.line_buf, self.total = bufs
        self.start, self.size, self.rows = start, size, pl.ds(start, size)

    def steps(self, axis):
        grid, here = self.mover.grid, self.mover.here
        return [(s - 1, grid.peer(here, axis, s)) for s in range(1, grid.sizes[axis])]

    def begin(self):
        self.pending = [
            self.mover.push(self.grad.at[:, :, :, spot[3], self.rows], self.pair.at[:, :, :, self.rows], spot)
            for _, spot in self.steps(3)
        ]

    def add(self, into, terms, first, second):
        def body(i, _):
            for j in range(second):
                total = terms[0](i, j)[...]
                for term in terms[1:]:
                    total = total + term(i, j)[...]
                into(i, j)[...] = total
            return 0

        lax.fori_loop(0, first, body, 0)

    def one(self):
        high, low, depth, pair = self.mover.grid.sizes
        c, rows = self.mover.here[3], self.rows
        grad, pair_buf, acc, buf, push = self.grad, self.pair, self.acc, self.one_buf, self.mover.push
        arrive(self.pending)
        terms = [lambda i, j: grad.at[i // low, i % low, j, c, rows]]
        if pair > 1:
            terms.append(lambda i, j: pair_buf.at[i // low, i % low, j, rows])
        self.add(lambda i, j: acc.at[i // low, i % low, j, rows], terms, high * low, depth)
        if self.even:
            self.pending = [
                push(acc.at[spot[0], :, :, rows], buf.at[s, 0:low, :, rows], spot) for s, spot in self.steps(0)
            ]
        else:
            self.pending = [
                push(acc.at[:, spot[1], :, rows], buf.at[s, 0:high, :, rows], spot) for s, spot in self.steps(1)
            ]

    def two(self):
        high, low, depth, pair = self.mover.grid.sizes
        hi, lo, z, c = self.mover.here
        rows, acc, one, buf, push = self.rows, self.acc, self.one_buf, self.two_buf, self.mover.push
        arrive(self.pending)
        mine = (lambda i, j: acc.at[hi, i, j, rows]) if self.even else (lambda i, j: acc.at[i, lo, j, rows])
        terms = [mine] + [
            (lambda i, j, s=s: one.at[s, i, j, rows]) for s, _ in self.steps(0 if self.even else 1)
        ]
        self.add(mine, terms, low if self.even else high, depth)
        if self.even:
            self.pending = [
                push(acc.at[hi, spot[1], :, rows], buf.at[s, :, rows], spot) for s, spot in self.steps(1)
            ]
        else:
            self.pending = [
                push(acc.at[spot[0], lo, :, rows], buf.at[s, :, rows], spot) for s, spot in self.steps(0)
            ]

    def three(self):
        depth = self.mover.grid.sizes[2]
        hi, lo, z, c = self.mover.here
        rows, acc, two, buf, push = self.rows, self.acc, self.two_buf, self.line_buf, self.mover.push
        arrive(self.pending)
        mine = lambda i, j: acc.at[hi, lo, j, rows]
        terms = [mine] + [
            (lambda i, j, s=s: two.at[s, j, rows]) for s, _ in self.steps(1 if self.even else 0)
        ]
        self.add(mine, terms, 1, depth)
        self.pending = [
            push(acc.at[hi, lo, spot[2], rows], buf.at[s, rows], spot) for s, spot in self.steps(2)
        ]

    def finish(self):
        depth = self.mover.grid.sizes[2]
        hi, lo, z, c = self.mover.here
        arrive(self.pending)
        total = self.acc[hi, lo, z, self.rows].astype(jnp.float32)
        for s in range(depth - 1):
            total = total + self.line_buf[s, self.rows].astype(jnp.float32)
        self.total[self.rows, :] = total


class Sizes:
    def __init__(self, grid, latents, shards):
        ada, attn, mlp, bias = (shard.shape[0] for shard in shards)
        self.slots, self.length, width = latents.shape
        self.width, self.bias = width, bias
        self.hidden = mlp * grid.count // (2 * width)
        self.parts = self.hidden // width
        self.ada_rows, self.qkv_rows = ada // (6 * width), attn // (3 * width)
        self.attn_rows, self.one_rows, self.mlp_rows = attn // width, mlp // self.hidden, mlp // width
        self.qkv_devices, self.one_devices = 3 * width * width // attn, width * self.hidden // mlp
        self.lead = 2 * SUBLANES - (2 * self.ada_rows) % (2 * SUBLANES)
        self.head_rows = self.lead + 2 * self.ada_rows
        self.tail_rows = 4 * self.ada_rows
        group = grid.depth * grid.pair
        exact = (
            self.hidden == self.parts * width, ada == self.ada_rows * 6 * width, attn == self.qkv_rows * 3 * width,
            mlp == self.one_rows * self.hidden, mlp == self.mlp_rows * width,
            self.qkv_devices * attn == 3 * width * width, self.one_devices * mlp == width * self.hidden,
        )
        whole = (
            self.qkv_rows % SUBLANES, (2 * self.one_rows) % SUBLANES, self.one_rows % 8, self.tail_rows % SUBLANES,
            self.qkv_devices % group, self.one_devices % group, width % LANES, (4 * self.slots) % SUBLANES,
            (2 * self.slots + 4 + self.parts) % SUBLANES, self.parts % grid.pair, self.mlp_rows % SUBLANES,
            (self.length % LANES), (2 * self.width // HEADS) % LANES,
        )
        per_tile = width // self.mlp_rows if width % self.mlp_rows == 0 else 0
        self.fits = (
            all(exact) and not any(whole) and grid.pair == 2 and self.slots < self.lead and bias <= 2 * LANES
            and bias <= width and per_tile > 0 and per_tile % grid.pair == 0 and group % per_tile == 0
            and grid.count * bias == (9 + self.parts + 1) * width and grid.high * grid.low * group == grid.count
        )


def fused_kernel(
    grid, sizes, count_ref, x_hbm, cond_ref, cot_hbm, ada_hbm, attn_hbm, mlp_hbm, bias_ref,
    out_ref, gx_ref, gcond_ref, g_ada_out, g_attn_out, g_mlp_out, g_bias_out,
    all_ada, all_attn, all_mlp, note_a, note_b, grad_attn, grad_mlp,
    pair_attn, pair_mlp, acc_attn, acc_mlp, one_attn, one_mlp, two_attn, two_mlp, line_attn, line_mlp,
    sum_attn, sum_mlp, swap_out, swap_in, back_in,
    x_ref, cot_ref, ada_ref, attn_ref, mlp_ref, line, unit, local_rows, pick_head, pick_tail, spread, bias_rows,
    mod, norm_one, inv_one, h_one, qkv, probs, mixed, branch, norm_two, inv_two, h_two,
    slope, act, mlp, wide, back, dx, small, dqkv, dmod, gbias,
    send_sem, recv_sem, own_sem,
):
    mover = Mover(grid, send_sem, recv_sem)
    here = mover.here
    hi, lo, z, c = here
    high, low, depth, pair = grid.sizes
    me = ((hi * low + lo) * depth + z) * pair + c
    slots, length, width, hidden = sizes.slots, sizes.length, sizes.width, sizes.hidden
    rows_all = slots * length
    heads = probs.shape[1]
    head_dim = width // heads
    score_scale = head_dim ** (-0.5)
    f32, b16 = jnp.float32, jnp.bfloat16
    count = count_ref[0]
    parts, tiles = sizes.parts, width // LANES
    ada_rows, lead, head_rows, tail_rows = sizes.ada_rows, sizes.lead, sizes.head_rows, sizes.tail_rows
    group = depth * pair

    met = grid.greet(here)
    x_in = pltpu.make_async_copy(x_hbm, x_ref, own_sem.at[0])
    cot_in = pltpu.make_async_copy(cot_hbm, cot_ref, own_sem.at[1])
    shards_in = [
        pltpu.make_async_copy(a, b, own_sem.at[2 + n])
        for n, (a, b) in enumerate(((ada_hbm, ada_ref), (attn_hbm, attn_ref), (mlp_hbm, mlp_ref)))
    ]
    for copy in shards_in:
        copy.start()
    x_in.start()
    cot_in.start()

    def strided(start, rows, stride):
        return line[pl.ds(start, rows, stride=stride), :]

    def lanes(t):
        return slice(t * LANES, (t + 1) * LANES)

    def column_sum(values):
        return jnp.sum(values, axis=0, keepdims=True)

    cond = cond_ref[...]
    cond_act = (cond * jax.nn.sigmoid(cond)).astype(b16)
    shards_in[0].wait()
    line[0 : ada_ref.shape[0], :] = ada_ref[...].astype(f32)
    unit[0:lead, :] = jnp.zeros((lead, width), f32)
    for k in range(6):
        for t in range(tiles):
            unit[lead + ada_rows * k : lead + ada_rows * (k + 1), lanes(t)] = strided(
                tiles * k + t, ada_rows, 6 * tiles
            )
    unit[0:1, 0 : sizes.bias] = bias_ref[...].astype(f32)
    unit[1 : 1 + slots, :] = cond_act.astype(f32)
    all_ada[hi, lo, z, c] = unit[0 : head_rows + tail_rows, :].astype(b16)

    def cut_rows(ref, start, size):
        return [(ref, start + at, min(SUBLANES, size - at)) for at in range(0, size, SUBLANES)]

    pieces = cut_rows(all_ada, 0, head_rows), cut_rows(all_attn, 0, sizes.attn_rows)
    pieces += cut_rows(all_ada, head_rows, tail_rows), cut_rows(all_mlp, 0, sizes.mlp_rows)
    ends = [sum(len(piece) for piece in pieces[: k + 1]) for k in range(len(pieces))]
    shares = [
        Share(mover, ref, start, size, axis_order(k))
        for k, (ref, start, size) in enumerate(entry for piece in pieces for entry in piece)
    ]
    agenda, begun = [], ends[1]
    for t in range(len(shares) + 3 * LAG):
        while begun < min(len(shares), t + 2 + LAG):
            agenda.append((begun, "begin"))
            begun += 1
        for k, name in enumerate(("first", "second", "third", "end")):
            if 0 <= t - k * LAG < len(shares):
                agenda.append((t - k * LAG, name))

    def until(share, name):
        while (share, name) in agenda:
            k, step = agenda.pop(0)
            getattr(shares[k], step)()

    met()
    for share in shares[: ends[0]]:
        share.begin()

    shards_in[1].wait()
    line[0 : attn_ref.shape[0], :] = attn_ref[...].astype(f32)

    @pl.when(me < sizes.qkv_devices)
    def _():
        rows = sizes.qkv_rows
        for k in range(3):
            for t in range(tiles):
                unit[rows * k : rows * (k + 1), lanes(t)] = strided(tiles * k + t, rows, 3 * tiles)

    @pl.when(me >= sizes.qkv_devices)
    def _():
        for t in range(tiles):
            unit[0 : sizes.attn_rows, lanes(t)] = strided(t, sizes.attn_rows, tiles)

    all_attn[hi, lo, z, c] = unit[0 : sizes.attn_rows, :].astype(b16)
    for share in shares[ends[0] : ends[1]]:
        share.begin()

    one_rows, per_core = sizes.one_rows, parts // pair
    shards_in[2].wait()
    line[0 : mlp_ref.shape[0], :] = mlp_ref[...].astype(f32)

    @pl.when(me < sizes.one_devices)
    def _():
        for k in range(parts):
            for t in range(tiles):
                local_rows[one_rows * k : one_rows * (k + 1), lanes(t)] = strided(
                    tiles * k + t, one_rows, parts * tiles
                )
        for k in range(per_core):
            unit[pl.ds(pl.multiple_of(2 * one_rows * k + one_rows * c, 8), one_rows), :] = local_rows[
                pl.ds(pl.multiple_of(one_rows * (per_core * c + k), 8), one_rows), :
            ]

    @pl.when(me >= sizes.one_devices)
    def _():
        for t in range(tiles):
            unit[0 : sizes.mlp_rows, lanes(t)] = strided(t, sizes.mlp_rows, tiles)
        local_rows[...] = jnp.zeros_like(local_rows)

    cut = one_rows * per_core
    swap_out[...] = local_rows[pl.ds(pl.multiple_of(cut * (1 - c), 8), cut), :].astype(b16)
    partner = grid.peer(here, 3, 1)
    swap = mover.push(swap_out, swap_in, partner)

    def picks(total, span, skip, target):
        at = lax.broadcasted_iota(jnp.int32, (1, total), 1)
        device, row = at // span, at % span - skip
        entry = jnp.where(row >= 0, device * ada_rows + row % ada_rows, -1)
        source = lax.broadcasted_iota(jnp.int32, (width, total), 0)
        target[...] = jnp.where(source == entry, 1.0, 0.0).astype(b16)

    def owner_mask(total, span, skip, blocks):
        at = lax.broadcasted_iota(jnp.int32, (blocks * slots, total), 1)
        block = lax.broadcasted_iota(jnp.int32, (blocks * slots, total), 0) // slots
        row = at % span - skip
        return jnp.logical_and(row >= 0, row // ada_rows == block)

    def spread_cond(pick, total, span, skip, blocks):
        wide_cond = dot(cond_act, pick[...])
        stacked = jnp.concatenate([wide_cond] * blocks, axis=0)
        return jnp.where(owner_mask(total, span, skip, blocks), stacked, 0.0).astype(b16)

    head_total, tail_total = grid.count * head_rows, grid.count * tail_rows

    def norm_first(s):
        rows = slice(s * length, (s + 1) * length)
        normed, inverse = layer_norm(x_ref[s])
        norm_one[rows, :] = normed
        inv_one[rows, :] = inverse

    def part(s, k):
        return mod[k * slots + s : k * slots + s + 1, :]

    picks(head_total, head_rows, lead, pick_head)
    swap.wait_recv()

    @pl.when(me < sizes.one_devices)
    def _():
        local_rows[0:cut, :] = swap_in[...].astype(f32)
        for k in range(per_core):
            unit[pl.ds(pl.multiple_of(2 * one_rows * k + one_rows * (1 - c), 8), one_rows), :] = local_rows[
                one_rows * k : one_rows * (k + 1), :
            ]

    all_mlp[hi, lo, z, c] = unit[0 : sizes.mlp_rows, :].astype(b16)
    x_in.wait()
    until(ends[0] - 1, "first")
    for s in range(slots):
        norm_first(s)
        until(min(ends[0] + s, ends[1] - 1), "first")
    head_cond = spread_cond(pick_head, head_total, head_rows, lead, 2)
    picks(tail_total, tail_rows, 0, pick_tail)
    until(ends[0] - 1, "third")
    tail_cond = spread_cond(pick_tail, tail_total, tail_rows, 0, 4)
    until(ends[0] - 1, "end")

    def rows_of(ref, start, size):
        return ref[:, :, :, :, start : start + size, :].reshape(grid.count * size, width)

    mod[0 : 2 * slots, :] = dot(head_cond, rows_of(all_ada, 0, head_rows))

    bias_rows[...] = jnp.zeros_like(bias_rows)
    lane = lax.broadcasted_iota(jnp.int32, (1, width), 1)
    for d in range(grid.count):
        values = all_ada[d // (low * group), d // group % low, d // pair % depth, d % pair, 0:SUBLANES, :].astype(f32)[0:1]
        row, shift = divmod(d * sizes.bias, width)
        turned = pltpu.roll(values, shift, 1) if shift else values
        end = shift + sizes.bias
        bias_rows[row : row + 1, :] += jnp.where(jnp.logical_and(lane >= shift, lane < end), turned, 0.0)
        if end > width:
            bias_rows[row + 1 : row + 2, :] += jnp.where(lane < end - width, turned, 0.0)

    def add_mod_bias(first, last):
        for k in range(first, last):
            span = slice(k * slots, (k + 1) * slots)
            mod[span, :] = mod[span, :] + bias_rows[k : k + 1, :]

    add_mod_bias(0, 2)

    def modulate_first(s):
        rows = slice(s * length, (s + 1) * length)
        h_one[rows, :] = (norm_one[rows, :] * (1.0 + part(s, 1)) + part(s, 0)).astype(b16)

    for s in range(slots):
        modulate_first(s)
    until(ends[1] - 1, "end")

    def devices(ref, first, last, rows):
        pieces = []
        for g in range(first // group, last // group):
            piece = ref[g // low, g % low, :, :, rows, :]
            pieces.append(piece.reshape(group * piece.shape[2], width))
        return pieces[0] if len(pieces) == 1 else jnp.concatenate(pieces, axis=0)

    def qkv_weight(k):
        return devices(all_attn, 0, sizes.qkv_devices, slice(sizes.qkv_rows * k, sizes.qkv_rows * (k + 1)))

    def proj_weight():
        return devices(all_attn, sizes.qkv_devices, grid.count, slice(0, sizes.attn_rows))

    tall = 2 * one_rows

    def one_weight(t):
        core, k = t // per_core, t % per_core
        pieces = [
            all_mlp[g // low, g % low, :, core, tall * k : tall * (k + 1), :].reshape(depth * tall, width)
            for g in range(sizes.one_devices // group)
        ]
        return pieces[0] if len(pieces) == 1 else jnp.concatenate(pieces, axis=0)

    per_tile = width // sizes.mlp_rows

    def two_place(t):
        first = sizes.one_devices + per_tile * t
        g, at = first // group, first % group // pair
        return g // low, g % low, slice(at, at + per_tile // pair)

    def two_weight(t):
        a, b, zs = two_place(t)
        return all_mlp[a, b, zs, :, :, :].reshape(width, width)

    cut_head = 2 * head_dim
    upper = lax.broadcasted_iota(jnp.int32, (length, cut_head), 1) >= head_dim

    def both(block):
        zero = jnp.zeros_like(block)
        return jnp.concatenate([jnp.where(upper, zero, block), jnp.where(upper, block, zero)], axis=0)

    for k, row in enumerate((6, None, 7)):
        value = dot(h_one[...], qkv_weight(k))
        if row is not None:
            value = value + bias_rows[row : row + 1, :]
        qkv[:, k * width : (k + 1) * width] = value.astype(b16)

    def attend(s):
        rows = slice(s * length, (s + 1) * length)
        for p in range(heads // 2):
            at = p * cut_head
            query = qkv[rows, at : at + cut_head]
            key = qkv[rows, width + at : width + at + cut_head]
            value = qkv[rows, 2 * width + at : 2 * width + at + cut_head]
            scores = dot(both(query), key, (1, 1)) * score_scale
            total = jnp.log(jnp.sum(jnp.exp(scores), axis=-1, keepdims=True))
            prob = jnp.exp(scores - total)
            probs[s, 2 * p] = prob[:length]
            probs[s, 2 * p + 1] = prob[length:]
            prob = prob.astype(b16)
            side = jnp.concatenate([prob[:length], prob[length:]], axis=1)
            mixed[rows, at : at + cut_head] = dot(side, both(value)).astype(b16)

    for s in range(slots):
        attend(s)
        if s + 1 < slots:
            until(min(ends[1] + s, ends[2] - 1), "end")
    branch[...] = dot(mixed[...], proj_weight()) + bias_rows[8:9, :]
    until(ends[2] - 1, "end")
    mod[2 * slots :, :] = dot(tail_cond, rows_of(all_ada, head_rows, tail_rows))
    add_mod_bias(2, 6)

    def norm_second(s):
        rows = slice(s * length, (s + 1) * length)
        after = x_ref[s] + part(s, 2) * branch[rows, :]
        dx[rows, :] = after
        normed, inverse = layer_norm(after)
        norm_two[rows, :] = normed
        inv_two[rows, :] = inverse
        h_two[rows, :] = (normed * (1.0 + part(s, 4)) + part(s, 3)).astype(b16)

    for s in range(slots):
        norm_second(s)

    note_rows = note_a.shape[4]
    own_lane = lax.broadcasted_iota(jnp.int32, (SUBLANES, width), 1)
    own_row = lax.broadcasted_iota(jnp.int32, (SUBLANES, width), 0)
    own_pick = jnp.where(own_lane == own_row + me * ada_rows, 1.0, 0.0).astype(b16)
    columns = dot(own_pick, rows_of(all_ada, 0, head_rows), (1, 1)).astype(b16)
    note_total = grid.count * note_rows
    at = lax.broadcasted_iota(jnp.int32, (1, note_total), 1)
    wanted = at // note_rows * head_rows + 1 + at % note_rows % slots
    source = lax.broadcasted_iota(jnp.int32, (head_total, note_total), 0)
    spread[...] = dot(columns, jnp.where(source == wanted, 1.0, 0.0).astype(b16)).astype(b16)

    def up(t):
        cols = slice(t * width, (t + 1) * width)
        pre = dot(h_two[...], one_weight(t)) + bias_rows[9 + t : 10 + t, :]
        square = pre * pre
        tanh_part = jnp.tanh(ROOT_TWO_OVER_PI * (pre + GELU_COEF * pre * square))
        half = 0.5 * (1.0 + tanh_part)
        act[:, cols] = (pre * half).astype(b16)
        slope[:, cols] = half + 0.5 * pre * (1.0 - tanh_part * tanh_part) * ROOT_TWO_OVER_PI * (
            1.0 + 3.0 * GELU_COEF * square
        )

    for k in range(per_core):
        until(ends[2] - 1 + -(-tall * (k + 1) // SUBLANES), "end")
        for core in range(pair):
            up(core * per_core + k)
    until(ends[3] - 1, "end")
    two_all = jnp.concatenate([two_weight(t) for t in range(parts)], axis=0)
    mlp[...] = dot(act[...], two_all) + bias_rows[9 + parts : 10 + parts, :]

    gbias[...] = jnp.zeros_like(gbias)
    last = gbias.shape[0] - 1
    cot_in.wait()

    def finish(s):
        rows = slice(s * length, (s + 1) * length)
        live = s < count
        value = mlp[rows, :]
        out_ref[s] = jnp.where(live, dx[rows, :] + part(s, 5) * value, 0.0)
        grad = jnp.where(live, cot_ref[s], 0.0)
        cot_ref[s] = grad
        dmod[5 * slots + s : 5 * slots + s + 1, :] = column_sum(grad * value)
        full = grad * part(s, 5)
        gbias[last : last + 1, :] += column_sum(full)
        small[rows, :] = full.astype(b16)

    for s in range(slots):
        finish(s)

    bufs_mlp = (grad_mlp, pair_mlp, acc_mlp, one_mlp, two_mlp, line_mlp, sum_mlp)
    bufs_attn = (grad_attn, pair_attn, acc_attn, one_attn, two_attn, line_attn, sum_attn)
    early = [(bufs_mlp, start, size) for _, start, size in cut_rows(all_mlp, 0, sizes.mlp_rows)]
    late = [(bufs_attn, start, size) for _, start, size in cut_rows(all_attn, 0, sizes.attn_rows)]
    reduces = [Reduce(mover, bufs, start, size, k % 2 == 0) for k, (bufs, start, size) in enumerate(early + late)]
    n_early, n_all = len(early), len(early) + len(late)
    note_first = Share(mover, note_a, 0, note_rows, axis_order(0))
    note_last = Share(mover, note_b, 0, note_rows, axis_order(1))

    def run(name, first, last):
        for reduce in reduces[first:last]:
            getattr(reduce, name)()

    def mlp_grads(t):
        cols = slice(t * width, (t + 1) * width)
        a, b, zs = two_place(t)
        grad_mlp[a, b, zs, :, :, :] = (
            dot(act[:, cols], small[...], (0, 0)).astype(b16).reshape(per_tile // pair, pair, sizes.mlp_rows, width)
        )

    def mlp_down(t):
        cols = slice(t * width, (t + 1) * width)
        full = dot(small[...], two_weight(t), (1, 1)) * slope[:, cols]
        gbias[3 + t : 4 + t, :] = column_sum(full)
        grad = full.astype(b16)
        wide[:, cols] = grad
        core, k = t // per_core, t % per_core
        whole = dot(h_two[...], grad, (0, 0)).astype(b16)
        for g in range(sizes.one_devices // group):
            grad_mlp[g // low, g % low, :, core, tall * k : tall * (k + 1), :] = whole[
                g * depth * tall : (g + 1) * depth * tall
            ].reshape(depth, tall, width)

    for t in range(parts):
        mlp_grads(t)
    sent = 0
    for k in range(per_core):
        for core in range(pair):
            mlp_down(core * per_core + k)
        ready = n_early if k + 1 == per_core else tall * (k + 1) // SUBLANES
        run("begin", sent, ready)
        sent = ready
    third = -(-n_early // 3)
    marks = [min(n_early, third * k) for k in range(4)]
    run("one", 0, marks[1])
    one_all = jnp.concatenate([one_weight(t) for t in range(parts)], axis=1)
    back[...] = dot(wide[...], one_all, (1, 1))
    run("one", marks[1], marks[2])

    def mlp_back(s):
        rows = slice(s * length, (s + 1) * length)
        grad_two = back[rows, :]
        normed = norm_two[rows, :]
        dmod[4 * slots + s : 4 * slots + s + 1, :] = column_sum(grad_two * normed)
        dmod[3 * slots + s : 3 * slots + s + 1, :] = column_sum(grad_two)
        after = cot_ref[s] + norm_backward(grad_two * (1.0 + part(s, 4)), normed, inv_two[rows, :])
        dx[rows, :] = after
        dmod[2 * slots + s : 2 * slots + s + 1, :] = column_sum(after * branch[rows, :])
        full = after * part(s, 2)
        gbias[2:3, :] += column_sum(full)
        small[rows, :] = full.astype(b16)

    for s in range(slots):
        mlp_back(s)
    note_a[hi, lo, z, c] = dmod[2 * slots :, :].astype(b16)
    note_first.begin()
    whole = dot(mixed[...], small[...], (0, 0)).astype(b16)
    for g in range(sizes.qkv_devices // group, grid.count // group):
        base = (g * group - sizes.qkv_devices) * sizes.attn_rows
        grad_attn[g // low, g % low] = whole[base : base + group * sizes.attn_rows].reshape(
            depth, pair, sizes.attn_rows, width
        )
    mixed[...] = dot(small[...], proj_weight(), (1, 1)).astype(b16)

    def attend_back(s):
        rows = slice(s * length, (s + 1) * length)
        for p in range(heads // 2):
            at = p * cut_head
            span = slice(at, at + cut_head)
            query = qkv[rows, span]
            key = qkv[rows, width + at : width + at + cut_head]
            value = qkv[rows, 2 * width + at : 2 * width + at + cut_head]
            grad = both(mixed[rows, span])
            prob = jnp.concatenate([probs[s, 2 * p], probs[s, 2 * p + 1]], axis=0)
            d_prob = dot(grad, value, (1, 1))
            d_value = dot(prob.astype(b16), grad, (0, 0)).astype(b16)
            delta = jnp.sum(prob * d_prob, axis=-1, keepdims=True)
            d_score = (prob * (d_prob - delta) * score_scale).astype(b16)
            side = jnp.concatenate([d_score[:length], d_score[length:]], axis=1)
            d_query = dot(side, both(key)).astype(b16)
            d_key = dot(d_score, both(query), (0, 0)).astype(b16)
            dqkv[rows, span] = d_query
            dqkv[rows, width + at : width + at + cut_head] = d_key
            dqkv[rows, 2 * width + at : 2 * width + at + cut_head] = d_value
            gbias[0:1, span] += column_sum(d_query.astype(f32))
            gbias[1:2, span] += column_sum(d_value.astype(f32))

    between = {
        min(1, slots - 1): lambda: (run("two", 0, marks[1]), run("one", marks[2], marks[3])),
        min(2, slots - 1): note_first.first,
    }
    for s in range(slots):
        attend_back(s)
        if s in between:
            between[s]()
    run("two", marks[1], marks[2])
    for k in range(3):
        cols = slice(k * width, (k + 1) * width)
        whole = dot(h_one[...], dqkv[:, cols], (0, 0)).astype(b16)
        for g in range(sizes.qkv_devices // group):
            base = g * group * sizes.qkv_rows
            grad_attn[g // low, g % low, :, :, sizes.qkv_rows * k : sizes.qkv_rows * (k + 1), :] = whole[
                base : base + group * sizes.qkv_rows
            ].reshape(depth, pair, sizes.qkv_rows, width)
    run("begin", n_early, n_all)
    run("three", 0, marks[1])
    back[...] = dot(dqkv[:, 0:width], qkv_weight(0), (1, 1)) + (
        dot(dqkv[:, width : 2 * width], qkv_weight(1), (1, 1)) + dot(dqkv[:, 2 * width :], qkv_weight(2), (1, 1))
    )
    run("one", n_early, n_all)

    def attn_back(s):
        rows = slice(s * length, (s + 1) * length)
        grad_one = back[rows, :]
        normed = norm_one[rows, :]
        dmod[slots + s : slots + s + 1, :] = column_sum(grad_one * normed)
        dmod[s : s + 1, :] = column_sum(grad_one)
        gx_ref[s] = dx[rows, :] + norm_backward(grad_one * (1.0 + part(s, 1)), normed, inv_one[rows, :])

    for s in range(slots):
        attn_back(s)
    note_b[hi, lo, z, c] = jnp.concatenate([dmod[0 : 2 * slots, :], gbias[...]], axis=0).astype(b16)
    note_last.begin()
    run("two", marks[2], marks[3])
    run("three", marks[1], marks[2])
    note_first.second()
    run("finish", 0, marks[1])

    def gather_entries(first, blocks, start, rows, total, span, skip, pick):
        grad_mod = dmod[first * slots : (first + blocks) * slots, :].astype(b16)
        values = dot(grad_mod, rows_of(all_ada, start, rows), (1, 1))
        values = jnp.where(owner_mask(total, span, skip, blocks), values, 0.0)
        merged = values[0:slots]
        for k in range(1, blocks):
            merged = merged + values[k * slots : (k + 1) * slots]
        upper_part = merged.astype(b16)
        lower_part = (merged - upper_part.astype(f32)).astype(b16)
        return dot(upper_part, pick[...], (1, 1)) + dot(lower_part, pick[...], (1, 1))

    grad_act = gather_entries(2, 4, head_rows, tail_rows, tail_total, tail_rows, 0, pick_tail)
    note_last.first()
    run("three", marks[2], marks[3])
    run("finish", marks[1], marks[2])
    run("two", n_early, n_all - 1)
    note_first.third()
    grad_act = grad_act + gather_entries(0, 2, 0, head_rows, head_total, head_rows, lead, pick_head)
    gcond_ref[...] = grad_act * silu_slope(cond)
    run("two", n_all - 1, n_all)
    note_last.second()
    run("finish", marks[2], marks[3])
    home = [
        mover.push(
            sum_mlp.at[pl.ds(pl.multiple_of(tall * k + one_rows * (1 - c), 8), one_rows)], back_in.at[k], partner
        )
        for k in range(per_core)
    ]
    note_first.end()
    run("three", n_early, n_all - 1)
    def from_notes(note, blocks, extra):
        kept = []
        entry = lax.broadcasted_iota(jnp.int32, (SUBLANES, note_total), 1) % note_rows
        for k in range(blocks):
            kept.append(jnp.where(entry // slots == k, spread[...].astype(f32), 0.0))
        line_at = lax.broadcasted_iota(jnp.int32, (SUBLANES, note_total), 0)
        wanted = jnp.where(entry < blocks * slots, entry // slots, entry - blocks * slots + blocks)
        kept.append(jnp.where(wanted == line_at, 1.0, 0.0))
        left = jnp.concatenate(kept, axis=0).astype(b16)
        return dot(left, rows_of(note, 0, note_rows))

    def store_ada(source, first, blocks):
        for k in range(blocks):
            for t in range(tiles):
                g_ada_out[pl.ds(tiles * (first + k) + t, ada_rows, stride=6 * tiles), :] = source[
                    k * SUBLANES : k * SUBLANES + ada_rows, lanes(t)
                ]

    early = from_notes(note_a, 4, 0)
    store_ada(early, 2, 4)
    run("three", n_all - 1, n_all)
    note_last.third()
    arrive(home)
    for core in range(pair):
        @pl.when(jnp.logical_and(me < sizes.one_devices, c == core))
        def _():
            for k in range(per_core):
                for t in range(tiles):
                    own_at, far_at = per_core * core + k, per_core * (1 - core) + k
                    base = tall * k + one_rows * core
                    g_mlp_out[pl.ds(tiles * own_at + t, one_rows, stride=parts * tiles), :] = sum_mlp[
                        base : base + one_rows, lanes(t)
                    ]
                    g_mlp_out[pl.ds(tiles * far_at + t, one_rows, stride=parts * tiles), :] = back_in[k, :, lanes(t)]

    @pl.when(me >= sizes.one_devices)
    def _():
        for t in range(tiles):
            g_mlp_out[pl.ds(t, sizes.mlp_rows, stride=tiles), :] = sum_mlp[:, lanes(t)]

    note_last.end()
    late = from_notes(note_b, 2, gbias.shape[0])
    store_ada(late, 0, 2)
    bias_rows[0:2, :] = late[2 * SUBLANES : 2 * SUBLANES + 2]
    bias_rows[2:6, :] = early[4 * SUBLANES : 4 * SUBLANES + 4]
    bias_rows[6 : 6 + gbias.shape[0], :] = late[2 * SUBLANES + 2 : 2 * SUBLANES + 2 + gbias.shape[0]]
    begin = me * sizes.bias
    row, shift = begin // width, begin % width
    pair_rows = jnp.concatenate(
        [bias_rows[pl.ds(row, 1), :], bias_rows[pl.ds(row + 1, 1), :]], axis=1
    )
    turned = pltpu.roll(pair_rows, 2 * width - shift, 1)
    for t in range(g_bias_out.shape[0]):
        g_bias_out[t : t + 1, :] = turned[:, lanes(t)]

    run("finish", n_early, n_all)

    @pl.when(me < sizes.qkv_devices)
    def _():
        rows = sizes.qkv_rows
        for k in range(3):
            for t in range(tiles):
                g_attn_out[pl.ds(tiles * k + t, rows, stride=3 * tiles), :] = sum_attn[rows * k : rows * (k + 1), lanes(t)]

    @pl.when(me >= sizes.qkv_devices)
    def _():
        for t in range(tiles):
            g_attn_out[pl.ds(t, sizes.attn_rows, stride=tiles), :] = sum_attn[:, lanes(t)]

    mover.drain()
    assert len(mover.started) == send_sem.shape[0]


def run_fused(grid, sizes, counts, latents, conditioning, cotangent, shards, bias):
    slots, length, width, hidden = sizes.slots, sizes.length, sizes.width, sizes.hidden
    high, low, depth, pair = grid.sizes
    f32, b16 = jnp.float32, jnp.bfloat16
    rows = slots * length
    ada, attn, mlp = (shard.reshape(-1, LANES) for shard in shards)
    attn_rows, mlp_rows, one_rows = sizes.attn_rows, sizes.mlp_rows, sizes.one_rows
    ada_all = sizes.head_rows + sizes.tail_rows
    note_rows = 4 * slots
    extra = 4 + sizes.parts
    per_core = sizes.parts // pair
    side = max(high, low)
    tails = [(attn_rows, width), (mlp_rows, width)]
    leads = [
        (high, low, depth), (high, low, depth), (max(side - 1, 1), side, depth),
        (max(side - 1, 1), depth), (max(depth - 1, 1),),
    ]
    scratch = [(grid.sizes + (n, width), b16) for n in (ada_all, attn_rows, mlp_rows, note_rows, note_rows)]
    scratch += [(grid.sizes + tail, b16) for tail in tails]
    scratch += [(lead + tail, b16) for lead in leads for tail in tails]
    scratch += [(tail, f32) for tail in tails]
    cut = per_core * one_rows
    scratch += [((cut, width), b16), ((cut, width), b16), ((per_core, one_rows, width), f32)]
    scratch += [(latents.shape, f32)] * 2 + [(array.shape, b16) for array in (ada, attn, mlp)]
    scratch += [
        ((max(ada.shape[0], attn.shape[0], mlp.shape[0]), LANES), f32), ((max(mlp_rows, attn_rows, ada_all), width), f32),
        ((sizes.parts * one_rows, width), f32),
        ((width, grid.count * sizes.head_rows), b16), ((width, grid.count * sizes.tail_rows), b16),
        ((SUBLANES, grid.count * note_rows), b16), ((-(-(7 + extra) // 8) * 8, width), f32),
    ]
    scratch += [
        ((6 * slots, width), f32), ((rows, width), f32), ((rows, 1), f32), ((rows, width), b16),
        ((rows, 3 * width), b16), ((slots, HEADS, length, length), f32), ((rows, width), b16),
        ((rows, width), f32), ((rows, width), f32), ((rows, 1), f32), ((rows, width), b16),
        ((rows, hidden), f32), ((rows, hidden), b16), ((rows, width), f32), ((rows, hidden), b16),
        ((rows, width), f32), ((rows, width), f32), ((rows, width), b16), ((rows, 3 * width), b16),
        ((6 * slots, width), f32), ((extra, width), f32),
    ]
    ceil = lambda n: -(-n // SUBLANES)
    gathers = ceil(sizes.head_rows) + ceil(sizes.tail_rows) + ceil(attn_rows) + ceil(mlp_rows)
    copies = sum(Share.copies(grid, axis_order(k)) for k in list(range(gathers)) + [0, 1])
    copies += (ceil(attn_rows) + ceil(mlp_rows)) * (high + low + depth + pair - 4)
    copies += 1 + per_core
    vmem, anywhere = pl.BlockSpec(memory_space=pltpu.VMEM), pl.BlockSpec(memory_space=pl.ANY)
    far = pl.BlockSpec(memory_space=pltpu.HBM)
    outs = [
        (latents.shape, f32), (latents.shape, f32), (conditioning.shape, f32),
        (ada.shape, f32), (attn.shape, f32), (mlp.shape, f32), ((-(-bias.shape[1] // LANES), LANES), f32),
    ]
    pinned = lambda array: pltpu.with_memory_space_constraint(array, pltpu.HBM)
    results = pl.pallas_call(
        partial(fused_kernel, grid, sizes),
        out_shape=[jax.ShapeDtypeStruct(shape, kind) for shape, kind in outs],
        in_specs=[pl.BlockSpec(memory_space=pltpu.SMEM), far, vmem, far, far, far, far, vmem],
        out_specs=[vmem] * len(outs),
        scratch_shapes=[pltpu.VMEM(shape, kind) for shape, kind in scratch]
        + [pltpu.SemaphoreType.DMA((copies,)), pltpu.SemaphoreType.DMA((copies,)), pltpu.SemaphoreType.DMA((5,))],
        compiler_params=pltpu.CompilerParams(
            collective_id=2, has_side_effects=True, vmem_limit_bytes=50 * 1024 * 1024
        ),
    )(counts, pinned(latents), conditioning, pinned(cotangent), pinned(ada), pinned(attn), pinned(mlp), bias)
    return pl.pallas_call(
        hand_on,
        out_shape=[jax.ShapeDtypeStruct(shape, kind) for shape, kind in outs],
        in_specs=[anywhere] * len(outs),
        out_specs=[far] * len(outs),
        scratch_shapes=[pltpu.SemaphoreType.DMA((len(outs),))],
        compiler_params=pltpu.CompilerParams(vmem_limit_bytes=4 * 1024 * 1024),
    )(*results)


def hand_on(*refs):
    ins, outs, sem = refs[: len(refs) // 2], refs[len(refs) // 2 : -1], refs[-1]
    copies = [pltpu.make_async_copy(a, b, sem.at[n]) for n, (a, b) in enumerate(zip(ins, outs))]
    for copy in copies:
        copy.start()
    for copy in copies:
        copy.wait()


def local(
    grid, latents, conditioning, counts, cotangent, ada_weights, attn_weights, mlp_weights, flat_biases
):
    model_width = latents.shape[-1]
    slots = latents.shape[0]
    shards = (ada_weights, attn_weights, mlp_weights, flat_biases)
    sizes = Sizes(grid, latents, shards)
    if sizes.fits:
        outs = run_fused(
            grid, sizes, counts, latents, conditioning, cotangent, shards[:3], flat_biases[None]
        )
        return tuple(outs[:3]) + tuple(
            total.reshape(-1)[: shard.shape[0]] for total, shard in zip(outs[3:], shards)
        )
    whole_ada, whole_attn, whole_mlp, whole_bias = gather_all(
        grid, [pack([shard], ()) for shard in shards]
    )
    bias_flat = whole_bias.reshape(grid.count, -1)[:, : flat_biases.shape[0]].reshape(-1)
    weights = (
        whole_ada.reshape(model_width, 6 * model_width),
        whole_attn.reshape(-1, LANES),
        whole_mlp.reshape(-1, LANES),
    )
    biases = bias_flat.astype(jnp.float32)[None]
    output, grad_latents, grad_conditioning, cond_act, grad_mod, g_attn, g_mlp, g_bias = (
        run_block(counts, latents, conditioning, cotangent, weights, biases)
    )

    gap = padded_rows(flat_biases.shape[0]) * LANES - flat_biases.shape[0]
    bias_lines = jnp.pad(
        g_bias.astype(jnp.bfloat16).reshape(grid.count, -1), ((0, 0), (0, gap))
    )
    all_mod, all_act, *sums = scatter_sum(
        grid,
        [flat.reshape(grid.sizes + (-1, LANES)) for flat in (g_attn, g_mlp, bias_lines)],
        [grad_mod, cond_act],
    )
    all_mod = all_mod.reshape(grid.count * slots, -1)
    all_act = all_act.reshape(grid.count * slots, -1)
    grads = [own_rows(all_act, all_mod, ada_weights.shape[0])]
    grads += [total.reshape(-1)[: shard.shape[0]] for total, shard in zip(sums, shards[1:])]
    return (output, grad_latents, grad_conditioning) + tuple(grads)


def own_rows(left, right, extent):
    wide = right.shape[1]
    start = lax.axis_index(AXES) * extent
    rows = min(-(-extent // wide) + (1 if extent % wide else 0), left.shape[1])
    top = jnp.minimum(start // wide, left.shape[1] - rows)
    part = lax.dynamic_slice_in_dim(left, top, rows, 1)
    whole = dot(part, right, (0, 0)).reshape(-1)
    if rows * wide == extent:
        return whole
    return lax.dynamic_slice_in_dim(whole, start - top * wide, extent, 0)


def solution(mesh):
    in_specs = (
        P(("dp", "fsdp"), None, None),
        P(("dp", "fsdp"), None),
        P(("dp", "fsdp")),
        P(("dp", "fsdp"), None, None),
        P(("dp", "fsdp")),
        P(("dp", "fsdp")),
        P(("dp", "fsdp")),
        P(("dp", "fsdp")),
    )
    out_specs = (
        P(("dp", "fsdp"), None, None),
        P(("dp", "fsdp"), None, None),
        P(("dp", "fsdp"), None),
        P(("dp", "fsdp")),
        P(("dp", "fsdp")),
        P(("dp", "fsdp")),
        P(("dp", "fsdp")),
    )
    return jax.shard_map(partial(local, Grid(mesh)), mesh=mesh, in_specs=in_specs, out_specs=out_specs, check_vma=False)
```

```python
from functools import partial
import math

import jax
import jax.numpy as jnp
from jax import lax
from jax.experimental import pallas as pl
from jax.experimental.pallas import tpu as pltpu
from jax.sharding import PartitionSpec as P

FF = 1536
HEADS = 6


EPSILON = 1e-06
GELU_COEF = 0.044715
ROOT_TWO_OVER_PI = 0.7978845608028654


def layer_norm(values):
    centre = values - jnp.mean(values, axis=-1, keepdims=True)
    inverse = lax.rsqrt(jnp.mean(centre * centre, axis=-1, keepdims=True) + EPSILON)
    return (centre * inverse, inverse)


def norm_backward(grad_norm, normed, inverse):
    first = jnp.mean(grad_norm, axis=-1, keepdims=True)
    second = jnp.mean(grad_norm * normed, axis=-1, keepdims=True)
    return (grad_norm - first - normed * second) * inverse


def gelu_value(pre_act):
    inner = ROOT_TWO_OVER_PI * (pre_act + GELU_COEF * pre_act * pre_act * pre_act)
    return 0.5 * pre_act * (1.0 + jnp.tanh(inner))


def gelu_slope(pre_act):
    tanh_part = jnp.tanh(ROOT_TWO_OVER_PI * (pre_act + GELU_COEF * pre_act * pre_act * pre_act))
    return 0.5 * (1.0 + tanh_part) + 0.5 * pre_act * (
        1.0 - tanh_part * tanh_part
    ) * ROOT_TWO_OVER_PI * (1.0 + 3.0 * GELU_COEF * pre_act * pre_act)


def silu_slope(values):
    sigma = jax.nn.sigmoid(values)
    return sigma * (1.0 + values * (1.0 - sigma))


LANES = 128
SUBLANES = 16
AXES = ("dp", "fsdp")
MESH = pl.DeviceIdType.MESH


class Grid:
    def __init__(self, mesh):
        dp, fsdp = mesh.shape["dp"], mesh.shape["fsdp"]
        side = math.isqrt(dp)
        self.high = side if side * side == dp else 1
        self.low = dp // self.high
        self.pair = 2 if fsdp % 2 == 0 else 1
        self.depth = fsdp // self.pair
        self.count = dp * fsdp
        self.sizes = (self.high, self.low, self.depth, self.pair)

    def here(self):
        a, f = lax.axis_index("dp"), lax.axis_index("fsdp")
        return [a // self.low, a % self.low, f // self.pair, f % self.pair]

    def peer(self, here, axis, step):
        spot = list(here)
        spot[axis] = lax.rem(here[axis] + step, self.sizes[axis])
        return spot

    def ident(self, spot):
        return (spot[0] * self.low + spot[1], spot[2] * self.pair + spot[3])

    def greet(self, here):
        sem = pltpu.get_barrier_semaphore()
        total = 0
        for axis in range(4):
            for step in range(1, self.sizes[axis]):
                pl.semaphore_signal(
                    sem, inc=1, device_id=self.ident(self.peer(here, axis, step)), device_id_type=MESH
                )
                total += 1
        return lambda: pl.semaphore_wait(sem, total)

    def barrier(self, here):
        self.greet(here)()


def chunk_rows(arrays):
    chunks = []
    for n, array in enumerate(arrays):
        rows = array.shape[-2]
        if rows % (2 * SUBLANES) == 0:
            chunks += [(n, 0, rows // 2), (n, rows // 2, rows // 2)]
        else:
            chunks.append((n, 0, rows))
    return chunks


class Mover:
    def __init__(self, grid, send_sem, recv_sem):
        self.grid, self.here = grid, grid.here()
        self.send_sem, self.recv_sem = send_sem, recv_sem
        self.started = []

    def push(self, src, dst, spot):
        k = len(self.started)
        copy = pltpu.make_async_remote_copy(
            src_ref=src, dst_ref=dst, send_sem=self.send_sem.at[k], recv_sem=self.recv_sem.at[k],
            device_id=self.grid.ident(spot), device_id_type=MESH,
        )
        copy.start()
        self.started.append(copy)
        return copy

    def spots(self, axis):
        return [self.grid.peer(self.here, axis, s) for s in range(1, self.grid.sizes[axis])]

    def pushes(self, ref, axis):
        return [self.push(ref, ref, spot) for spot in self.spots(axis)]

    def drain(self):
        for copy in self.started:
            copy.wait_send()


def arrive(copies):
    for copy in copies:
        copy.wait_recv()


class Spread:
    def __init__(self, mover, in_ref, out_ref, rows, low_first):
        self.mover, self.in_ref, self.out_ref, self.rows = mover, in_ref, out_ref, rows
        self.low_first = low_first
        self.swap = []

    def begin(self):
        hi, lo, z, c = self.mover.here
        src, dst = self.in_ref.at[self.rows], self.out_ref.at[hi, lo, z, c, self.rows]
        self.pending = [self.mover.push(src, dst, spot) for spot in self.mover.spots(2)]

    def first(self):
        hi, lo, z, c = self.mover.here
        arrive(self.pending)
        part = self.out_ref.at[hi, lo, :, c, self.rows]
        self.pending = self.mover.pushes(part, 1 if self.low_first else 0)
        self.swap += self.mover.pushes(part, 3)

    def second(self):
        hi, lo, z, c = self.mover.here
        arrive(self.pending)
        out, rows = self.out_ref, self.rows
        if self.low_first:
            self.pending = self.mover.pushes(out.at[hi, :, :, c, rows], 0)
            others = [out.at[hi, spot[1], :, c, rows] for spot in self.mover.spots(1)]
        else:
            self.pending = self.mover.pushes(out.at[:, lo, :, c, rows], 1)
            others = [out.at[spot[0], lo, :, c, rows] for spot in self.mover.spots(0)]
        for other in others:
            self.swap += self.mover.pushes(other, 3)

    def third(self):
        hi, lo, z, c = self.mover.here
        arrive(self.pending)
        out, rows = self.out_ref, self.rows
        if self.low_first:
            others = [out.at[spot[0], :, :, c, rows] for spot in self.mover.spots(0)]
        else:
            others = [out.at[:, spot[1], :, c, rows] for spot in self.mover.spots(1)]
        for other in others:
            self.swap += self.mover.pushes(other, 3)

    def end(self):
        arrive(self.swap)

    @staticmethod
    def copies(grid):
        high, low, depth, pair = grid.sizes
        return depth - 1 + (high + low - 2) + (pair - 1) * (1 + high + low - 2)


def gather_kernel(grid, chunks, arrays, *refs):
    in_refs, out_refs = refs[:arrays], refs[arrays : 2 * arrays]
    send_sem, recv_sem, own_sem = refs[2 * arrays :]
    mover = Mover(grid, send_sem, recv_sem)
    hi, lo, z, c = mover.here
    grid.barrier(mover.here)
    own = [
        pltpu.make_async_copy(in_refs[n], out_refs[n].at[hi, lo, z, c], own_sem.at[n])
        for n in range(arrays)
    ]
    for copy in own:
        copy.start()
    spreads = [
        Spread(mover, in_refs[n], out_refs[n], pl.ds(start, size), k % 2 == 0)
        for k, (n, start, size) in enumerate(chunks)
    ]
    for spread in spreads:
        spread.begin()
    for copy in own:
        copy.wait()
    for spread in spreads:
        spread.first()
    for spread in spreads:
        spread.second()
    for spread in spreads:
        spread.third()
    for spread in spreads:
        spread.end()
    mover.drain()


def gather_all(grid, arrays):
    chunks = chunk_rows(arrays)
    copies = Spread.copies(grid) * len(chunks)
    vmem = pl.BlockSpec(memory_space=pltpu.VMEM)
    return pl.pallas_call(
        partial(gather_kernel, grid, chunks, len(arrays)),
        out_shape=[jax.ShapeDtypeStruct(grid.sizes + array.shape, array.dtype) for array in arrays],
        in_specs=[vmem] * len(arrays),
        out_specs=[vmem] * len(arrays),
        scratch_shapes=[
            pltpu.SemaphoreType.DMA((copies,)),
            pltpu.SemaphoreType.DMA((copies,)),
            pltpu.SemaphoreType.DMA((len(arrays),)),
        ],
        compiler_params=pltpu.CompilerParams(
            collective_id=0, has_side_effects=True, vmem_limit_bytes=48 * 1024 * 1024
        ),
    )(*arrays)


def scatter_kernel(grid, chunks, arrays, extra, *refs):
    note_refs, refs = refs[:extra], refs[extra:]
    g_refs, refs = refs[:arrays], refs[arrays:]
    note_outs, refs = refs[:extra], refs[extra:]
    out_refs, refs = refs[:arrays], refs[arrays:]
    pair_bufs, refs = refs[:arrays], refs[arrays:]
    accs, refs = refs[:arrays], refs[arrays:]
    one_bufs, refs = refs[:arrays], refs[arrays:]
    two_bufs, refs = refs[:arrays], refs[arrays:]
    z_bufs, (send_sem, recv_sem, own_sem) = refs[:arrays], refs[arrays:]
    mover = Mover(grid, send_sem, recv_sem)
    here, push = mover.here, mover.push
    hi, lo, z, c = here
    grid.barrier(here)
    owns = [
        pltpu.make_async_copy(note_refs[n], note_outs[n].at[hi, lo, z, c], own_sem.at[n])
        for n in range(extra)
    ]
    notes = [
        Spread(mover, note_refs[n], note_outs[n], pl.ds(0, note_refs[n].shape[0]), n % 2 == 0)
        for n in range(extra)
    ]
    for own, note in zip(owns, notes):
        own.start()
        note.begin()

    def steps(axis):
        return [(s - 1, grid.peer(here, axis, s)) for s in range(1, grid.sizes[axis])]

    def add(into, terms, first, second):
        def body(t, _):
            i, j = t // second, t % second
            total = terms[0](i, j)[...].astype(jnp.float32)
            for term in terms[1:]:
                total = total + term(i, j)[...].astype(jnp.float32)
            target = into(i, j)
            target[...] = total.astype(target.dtype)
            return 0

        lax.fori_loop(0, first * second, body, 0)

    high, low, depth, pair = grid.sizes
    swaps, ones, twos, lines = [], [], [], []
    for n, start, size in chunks:
        rows = pl.ds(start, size)
        g_ref, pair_buf = g_refs[n], pair_bufs[n]
        swaps.append(
            [push(g_ref.at[:, :, :, spot[3], rows], pair_buf.at[:, :, :, rows], spot) for _, spot in steps(3)]
        )
    for own, note in zip(owns, notes):
        own.wait()
        note.first()
    for k, (n, start, size) in enumerate(chunks):
        rows = pl.ds(start, size)
        g_ref, pair_buf, acc, buf_one = g_refs[n], pair_bufs[n], accs[n], one_bufs[n]
        arrive(swaps[k])
        terms = [lambda i, j: g_ref.at[i // low, i % low, j, c, rows]]
        if pair > 1:
            terms.append(lambda i, j: pair_buf.at[i // low, i % low, j, rows])
        add(lambda i, j: acc.at[i // low, i % low, j, rows], terms, high * low, depth)
        if k % 2 == 0:
            ones.append(
                [push(acc.at[spot[0], :, :, rows], buf_one.at[s, 0:low, :, rows], spot) for s, spot in steps(0)]
            )
        else:
            ones.append(
                [push(acc.at[:, spot[1], :, rows], buf_one.at[s, 0:high, :, rows], spot) for s, spot in steps(1)]
            )
    for note in notes:
        note.second()
    for k, (n, start, size) in enumerate(chunks):
        rows = pl.ds(start, size)
        acc, buf_one, buf_two = accs[n], one_bufs[n], two_bufs[n]
        arrive(ones[k])
        even = k % 2 == 0
        mine = (lambda i, j: acc.at[hi, i, j, rows]) if even else (lambda i, j: acc.at[i, lo, j, rows])
        terms = [mine] + [
            (lambda i, j, s=s: buf_one.at[s, i, j, rows]) for s, _ in steps(0 if even else 1)
        ]
        add(mine, terms, low if even else high, depth)
        if even:
            twos.append(
                [push(acc.at[hi, spot[1], :, rows], buf_two.at[s, :, rows], spot) for s, spot in steps(1)]
            )
        else:
            twos.append(
                [push(acc.at[spot[0], lo, :, rows], buf_two.at[s, :, rows], spot) for s, spot in steps(0)]
            )
    for note in notes:
        note.third()
    for k, (n, start, size) in enumerate(chunks):
        rows = pl.ds(start, size)
        acc, buf_two, buf_z = accs[n], two_bufs[n], z_bufs[n]
        arrive(twos[k])
        mine = lambda i, j: acc.at[hi, lo, j, rows]
        terms = [mine] + [
            (lambda i, j, s=s: buf_two.at[s, j, rows]) for s, _ in steps(1 if k % 2 == 0 else 0)
        ]
        add(mine, terms, 1, depth)
        lines.append(
            [push(acc.at[hi, lo, spot[2], rows], buf_z.at[s, rows], spot) for s, spot in steps(2)]
        )
    for k, (n, start, size) in enumerate(chunks):
        rows = pl.ds(start, size)
        acc, buf_z = accs[n], z_bufs[n]
        arrive(lines[k])
        total = acc[hi, lo, z, rows].astype(jnp.float32)
        for s in range(depth - 1):
            total = total + buf_z[s, rows].astype(jnp.float32)
        out_refs[n][rows, :] = total
    for note in notes:
        note.end()
    mover.drain()


def scatter_sum(grid, arrays, notes):
    high, low, depth, pair = grid.sizes
    chunks = chunk_rows(arrays)
    copies = len(chunks) * (high + low + depth + pair - 4) + Spread.copies(grid) * len(notes)
    kind = arrays[0].dtype
    tails = [array.shape[-2:] for array in arrays]
    side = max(high, low)
    shapes = [
        (high, low, depth), (high, low, depth), (max(side - 1, 1), side, depth),
        (max(side - 1, 1), depth), (max(depth - 1, 1),),
    ]
    vmem = pl.BlockSpec(memory_space=pltpu.VMEM)
    return pl.pallas_call(
        partial(scatter_kernel, grid, chunks, len(arrays), len(notes)),
        out_shape=[jax.ShapeDtypeStruct(grid.sizes + note.shape, note.dtype) for note in notes]
        + [jax.ShapeDtypeStruct(tail, jnp.float32) for tail in tails],
        in_specs=[vmem] * (len(notes) + len(arrays)),
        out_specs=[vmem] * (len(notes) + len(arrays)),
        scratch_shapes=[pltpu.VMEM(shape + tail, kind) for shape in shapes for tail in tails]
        + [pltpu.SemaphoreType.DMA((copies,)), pltpu.SemaphoreType.DMA((copies,)), pltpu.SemaphoreType.DMA((len(notes),))],
        compiler_params=pltpu.CompilerParams(
            collective_id=1, has_side_effects=True, vmem_limit_bytes=48 * 1024 * 1024
        ),
    )(*notes, *arrays)


def padded_rows(extent):
    return -(-extent // LANES)


def pack(pieces, lead):
    parts = []
    for piece in pieces:
        extent = piece.shape[-1]
        rows = padded_rows(extent)
        gap = rows * LANES - extent
        if gap:
            piece = jnp.pad(piece, [(0, 0)] * len(lead) + [(0, gap)])
        parts.append(piece.reshape(lead + (rows, LANES)))
    if len(parts) == 1:
        return parts[0]
    return jnp.concatenate(parts, axis=-2)


def dot(left, right, contract=(1, 0)):
    return lax.dot_general(
        left, right, (((contract[0],), (contract[1],)), ((), ())), preferred_element_type=jnp.float32
    )


def block_kernel(
    count_ref, x_ref, cond_ref, cot_ref, w_ada, attn_ref, mlp_ref, bias_ref,
    out_ref, gx_ref, gcond_ref, act_ref, dmod_ref, g_attn, g_mlp, gbias_ref,
    line, w_qkv, w_proj, w_one, w_two, g_qkv, g_proj, g_one, g_two,
    mod, norm_one, inv_one, h_one, qkv, probs, mixed, branch, norm_two, inv_two, h_two,
    pre, act, mlp, wide, back, dx, small, dqkv, dmod,
):
    slots, length, width = x_ref.shape
    hidden = w_one.shape[1]
    rows_all = slots * length
    heads = probs.shape[1]
    head_dim = width // heads
    score_scale = head_dim ** (-0.5)
    f32, b16 = jnp.float32, jnp.bfloat16
    tile = 256 if hidden % 256 == 0 else hidden
    count = count_ref[0]
    o_query, o_value = 6 * width, 7 * width
    o_proj, o_one, o_two = 8 * width, 9 * width, 9 * width + hidden
    lane = lax.broadcasted_iota(jnp.int32, (length, 2 * head_dim), 1)
    lower = lane < head_dim

    def slot_loop(body):
        def step(s, _):
            body(s, pl.ds(pl.multiple_of(s * length, length), length))
            return 0

        lax.fori_loop(0, slots, step, 0)

    def part(s, k):
        return mod[pl.ds(s, 1), k * width : (k + 1) * width]

    def only(pair_block, first):
        return jnp.where(lower if first else jnp.logical_not(lower), pair_block, jnp.zeros_like(pair_block))

    def column_sum(values):
        return jnp.sum(values, axis=0, keepdims=True)

    def load_matrix(flat_ref, top, matrix):
        height, across = matrix.shape[0], matrix.shape[1] // LANES
        total = height * across

        def widen(t, _):
            at = pl.multiple_of(t * LANES, LANES)
            line[pl.ds(at, LANES), :] = flat_ref[pl.ds(top + at, LANES), :].astype(f32)
            return 0

        lax.fori_loop(0, total // LANES, widen, 0)
        for j in range(across):
            matrix[:, j * LANES : (j + 1) * LANES] = line[pl.ds(j, height, stride=across), :].astype(b16)

    def store_matrix(matrix, flat_ref, top):
        height, across = matrix.shape[0], matrix.shape[1] // LANES
        total = height * across
        for j in range(across):
            line[pl.ds(j, height, stride=across), :] = matrix[:, j * LANES : (j + 1) * LANES].astype(f32)

        def narrow(t, _):
            at = pl.multiple_of(t * LANES, LANES)
            flat_ref[pl.ds(top + at, LANES), :] = line[pl.ds(at, LANES), :].astype(b16)
            return 0

        lax.fori_loop(0, total // LANES, narrow, 0)

    proj_top, two_top = 3 * width * width // LANES, width * hidden // LANES
    load_matrix(attn_ref, 0, w_qkv)
    load_matrix(attn_ref, proj_top, w_proj)
    load_matrix(mlp_ref, 0, w_one)
    load_matrix(mlp_ref, two_top, w_two)
    cond = cond_ref[...]
    cond_act = (cond * jax.nn.sigmoid(cond)).astype(b16)
    mod[...] = dot(cond_act, w_ada[...]) + bias_ref[:, : 6 * width]

    def norm_first(s, rows):
        normed, inverse = layer_norm(x_ref[s])
        norm_one[rows, :] = normed
        inv_one[rows, :] = inverse
        h_one[rows, :] = (normed * (1.0 + part(s, 1)) + part(s, 0)).astype(b16)

    slot_loop(norm_first)
    for k, offset in enumerate((o_query, None, o_value)):
        cols = slice(k * width, (k + 1) * width)
        value = dot(h_one[...], w_qkv[:, cols])
        if offset is not None:
            value = value + bias_ref[:, offset : offset + width]
        qkv[:, cols] = value.astype(b16)

    def attend(s, rows):
        for pair in range(heads // 2):
            at = pair * 2 * head_dim
            query = qkv[rows, at : at + 2 * head_dim]
            key = qkv[rows, width + at : width + at + 2 * head_dim]
            value = qkv[rows, 2 * width + at : 2 * width + at + 2 * head_dim]
            halves = []
            for h in range(2):
                scores = dot(only(query, h == 0), key, (1, 1)) * score_scale
                total = jnp.log(jnp.sum(jnp.exp(scores), axis=-1, keepdims=True))
                prob = jnp.exp(scores - total)
                probs[s, 2 * pair + h] = prob
                halves.append(dot(prob.astype(b16), value))
            mixed[rows, at : at + 2 * head_dim] = jnp.where(lower, halves[0], halves[1]).astype(b16)

    slot_loop(attend)
    branch[...] = dot(mixed[...], w_proj[...]) + bias_ref[:, o_proj : o_proj + width]

    def norm_second(s, rows):
        after = x_ref[s] + part(s, 2) * branch[rows, :]
        dx[rows, :] = after
        normed, inverse = layer_norm(after)
        norm_two[rows, :] = normed
        inv_two[rows, :] = inverse
        h_two[rows, :] = (normed * (1.0 + part(s, 4)) + part(s, 3)).astype(b16)

    slot_loop(norm_second)

    def up(t, _):
        cols = pl.ds(pl.multiple_of(t * tile, tile), tile)
        shift = bias_ref[:, pl.ds(pl.multiple_of(o_one + t * tile, LANES), tile)]
        value = dot(h_two[...], w_one[:, cols]) + shift
        pre[:, cols] = value
        act[:, cols] = gelu_value(value).astype(b16)
        return 0

    lax.fori_loop(0, hidden // tile, up, 0)
    mlp[...] = dot(act[...], w_two[...]) + bias_ref[:, o_two : o_two + width]

    gbias_ref[...] = jnp.zeros_like(gbias_ref)

    def finish(s, rows):
        live = s < count
        value = mlp[rows, :]
        out_ref[s] = jnp.where(live, dx[rows, :] + part(s, 5) * value, 0.0)
        grad = jnp.where(live, cot_ref[s], 0.0)
        dmod[pl.ds(s, 1), 5 * width :] = column_sum(grad * value)
        full = grad * part(s, 5)
        gbias_ref[:, o_two : o_two + width] += column_sum(full)
        small[rows, :] = full.astype(b16)

    slot_loop(finish)

    def down(t, _):
        cols = pl.ds(pl.multiple_of(t * tile, tile), tile)
        full = dot(small[...], w_two[cols, :], (1, 1)) * gelu_slope(pre[:, cols])
        gbias_ref[:, pl.ds(pl.multiple_of(o_one + t * tile, LANES), tile)] = column_sum(full)
        grad = full.astype(b16)
        wide[:, cols] = grad
        g_two[cols, :] = dot(act[:, cols], small[...], (0, 0)).astype(g_two.dtype)
        g_one[:, cols] = dot(h_two[...], grad, (0, 0)).astype(g_one.dtype)
        return 0

    lax.fori_loop(0, hidden // tile, down, 0)
    back[...] = dot(wide[...], w_one[...], (1, 1))

    def mlp_back(s, rows):
        grad_two = back[rows, :]
        normed = norm_two[rows, :]
        dmod[pl.ds(s, 1), 4 * width : 5 * width] = column_sum(grad_two * normed)
        dmod[pl.ds(s, 1), 3 * width : 4 * width] = column_sum(grad_two)
        after = jnp.where(s < count, cot_ref[s], 0.0) + norm_backward(
            grad_two * (1.0 + part(s, 4)), normed, inv_two[rows, :]
        )
        dx[rows, :] = after
        dmod[pl.ds(s, 1), 2 * width : 3 * width] = column_sum(after * branch[rows, :])
        full = after * part(s, 2)
        gbias_ref[:, o_proj : o_proj + width] += column_sum(full)
        small[rows, :] = full.astype(b16)

    slot_loop(mlp_back)
    g_proj[...] = dot(mixed[...], small[...], (0, 0)).astype(g_proj.dtype)
    mixed[...] = dot(small[...], w_proj[...], (1, 1)).astype(b16)

    def attend_back(s, rows):
        for pair in range(heads // 2):
            at = pair * 2 * head_dim
            span = slice(at, at + 2 * head_dim)
            query = qkv[rows, span]
            key = qkv[rows, width + at : width + at + 2 * head_dim]
            value = qkv[rows, 2 * width + at : 2 * width + at + 2 * head_dim]
            grad = mixed[rows, span]
            d_query, d_key, d_value = [], [], []
            for h in range(2):
                prob = probs[s, 2 * pair + h]
                d_prob = dot(only(grad, h == 0), value, (1, 1))
                d_value.append(dot(prob.astype(b16), grad, (0, 0)))
                delta = jnp.sum(prob * d_prob, axis=-1, keepdims=True)
                d_score = (prob * (d_prob - delta) * score_scale).astype(b16)
                d_query.append(dot(d_score, key))
                d_key.append(dot(d_score, query, (0, 0)))
            d_query = jnp.where(lower, d_query[0], d_query[1]).astype(b16)
            d_key = jnp.where(lower, d_key[0], d_key[1]).astype(b16)
            d_value = jnp.where(lower, d_value[0], d_value[1]).astype(b16)
            dqkv[rows, span] = d_query
            dqkv[rows, width + at : width + at + 2 * head_dim] = d_key
            dqkv[rows, 2 * width + at : 2 * width + at + 2 * head_dim] = d_value
            gbias_ref[:, o_query + at : o_query + at + 2 * head_dim] += column_sum(d_query.astype(f32))
            gbias_ref[:, o_value + at : o_value + at + 2 * head_dim] += column_sum(d_value.astype(f32))

    slot_loop(attend_back)
    for k in range(3):
        cols = slice(k * width, (k + 1) * width)
        g_qkv[:, cols] = dot(h_one[...], dqkv[:, cols], (0, 0)).astype(g_qkv.dtype)
    back[...] = dot(dqkv[...], w_qkv[...], (1, 1))

    def attn_back(s, rows):
        grad_one = back[rows, :]
        normed = norm_one[rows, :]
        dmod[pl.ds(s, 1), width : 2 * width] = column_sum(grad_one * normed)
        dmod[pl.ds(s, 1), :width] = column_sum(grad_one)
        gx_ref[s] = dx[rows, :] + norm_backward(
            grad_one * (1.0 + part(s, 1)), normed, inv_one[rows, :]
        )

    slot_loop(attn_back)
    gbias_ref[:, : 6 * width] = column_sum(dmod[...])
    grad_mod = dmod[...].astype(b16)
    store_matrix(g_qkv, g_attn, 0)
    store_matrix(g_proj, g_attn, proj_top)
    store_matrix(g_one, g_mlp, 0)
    store_matrix(g_two, g_mlp, two_top)
    act_ref[...] = cond_act
    dmod_ref[...] = grad_mod
    gcond_ref[...] = dot(grad_mod, w_ada[...], (1, 1)) * silu_slope(cond)


def run_block(counts, latents, conditioning, cotangent, weights, biases):
    slots, length, width = latents.shape
    w_ada, attn, mlp = weights
    hidden = mlp.size // (2 * width)
    rows = slots * length
    f32, b16 = jnp.float32, jnp.bfloat16
    outs = [
        (latents.shape, f32), (latents.shape, f32), (conditioning.shape, f32),
        (conditioning.shape, b16), ((slots, 6 * width), b16),
        (attn.shape, b16), (mlp.shape, b16), (biases.shape, f32),
    ]
    matrices = [(width, 3 * width), (width, width), (width, hidden), (hidden, width)]
    scratch = [((max(h * w for h, w in matrices) // LANES, LANES), f32)]
    scratch += [(shape, b16) for shape in matrices + matrices]
    scratch += [
        ((slots, 6 * width), f32), ((rows, width), f32), ((rows, 1), f32), ((rows, width), b16),
        ((rows, 3 * width), b16), ((slots, HEADS, length, length), f32), ((rows, width), b16),
        ((rows, width), f32), ((rows, width), f32), ((rows, 1), f32), ((rows, width), b16),
        ((rows, hidden), f32), ((rows, hidden), b16), ((rows, width), f32), ((rows, hidden), b16),
        ((rows, width), f32), ((rows, width), f32), ((rows, width), b16), ((rows, 3 * width), b16),
        ((slots, 6 * width), f32),
    ]
    vmem = pl.BlockSpec(memory_space=pltpu.VMEM)
    return pl.pallas_call(
        block_kernel,
        out_shape=[jax.ShapeDtypeStruct(shape, kind) for shape, kind in outs],
        in_specs=[pl.BlockSpec(memory_space=pltpu.SMEM)] + [vmem] * 7,
        out_specs=[vmem] * len(outs),
        scratch_shapes=[pltpu.VMEM(shape, kind) for shape, kind in scratch],
        compiler_params=pltpu.CompilerParams(vmem_limit_bytes=60 * 1024 * 1024),
    )(counts, latents, conditioning, cotangent, *weights, biases)


LAG = 3


class Share:
    def __init__(self, mover, ref, start, size, axes):
        self.mover, self.ref, self.rows, self.axes = mover, ref, pl.ds(start, size), axes
        self.spot, self.stage, self.swap = list(mover.here[:3]), 0, []

    def at(self, spot):
        return self.ref.at[spot[0], spot[1], spot[2], self.mover.here[3], self.rows]

    def begin(self):
        self.pending = self.mover.pushes(self.at(self.spot), self.axes[self.stage])

    def absorb(self):
        arrive(self.pending)
        axis, spot = self.axes[self.stage], list(self.spot)
        self.spot[axis] = slice(None)
        if self.stage == 0:
            news = [self.spot]
        else:
            news = [spot[:axis] + [peer[axis]] + spot[axis + 1 :] for peer in self.mover.spots(axis)]
        news = [list(new) for new in news]
        self.stage += 1
        if self.stage < 3:
            self.begin()
        for new in news:
            self.swap += self.mover.pushes(self.at(new), 3)

    first = second = third = absorb

    def end(self):
        arrive(self.swap)

    @staticmethod
    def copies(grid, axes):
        one, two, three = (grid.sizes[axis] - 1 for axis in axes)
        return one + two + three + (grid.pair - 1) * (1 + two + three)


def axis_order(k):
    if k % 6 in (4, 5):
        return (1, 2, 0) if k % 2 == 0 else (0, 2, 1)
    return (2, 1, 0) if k % 2 == 0 else (2, 0, 1)


class Reduce:
    def __init__(self, mover, bufs, rows, cols, axes):
        self.mover, self.axes, self.rows, self.cols = mover, axes, rows, cols
        self.grad, self.pair, self.acc, self.plane_buf, self.deep_buf, self.side_buf, self.line_buf, self.total = bufs
        self.fixed, self.stage = {}, 0

    def steps(self, axis):
        grid, here = self.mover.grid, self.mover.here
        return [(s - 1, grid.peer(here, axis, s)) for s in range(1, grid.sizes[axis])]

    def place(self, fixed):
        index = [fixed.get(axis, slice(None)) for axis in range(3)]
        return self.acc.at[index[0], index[1], index[2], self.rows, self.cols]

    def slot(self, s, spots=None):
        sizes = self.mover.grid.sizes
        left = [axis for axis in range(3) if axis not in self.fixed and axis != self.axes[self.stage]]
        at = tuple(slice(0, sizes[axis]) if spots is None else spots[axis] for axis in left)
        buf = self.line_buf if not left else self.plane_buf if len(left) == 2 else (
            self.deep_buf if left[0] == 2 else self.side_buf
        )
        return buf.at[(s,) + at + (self.rows, self.cols)]

    def begin(self):
        self.pending = [
            self.mover.push(
                self.grad.at[:, :, :, spot[3], self.rows, self.cols],
                self.pair.at[:, :, :, self.rows, self.cols], spot,
            )
            for _, spot in self.steps(3)
        ]

    def send(self):
        axis = self.axes[self.stage]
        self.pending = [
            self.mover.push(self.place({**self.fixed, axis: spot[axis]}), self.slot(s), spot)
            for s, spot in self.steps(axis)
        ]

    def absorb(self):
        arrive(self.pending)
        axis, sizes = self.axes[self.stage], self.mover.grid.sizes
        spots = [{}]
        for other in range(3):
            if other not in self.fixed and other != axis:
                spots = [{**spot, other: n} for spot in spots for n in range(sizes[other])]
        arrived = [[self.slot(s, spot) for s, _ in self.steps(axis)] for spot in spots]
        self.fixed[axis] = self.mover.here[axis]
        for spot, terms in zip(spots, arrived):
            into = self.place({**self.fixed, **spot})
            total = into[...]
            for term in terms:
                total = total + term[...]
            into[...] = total
        self.stage += 1
        self.send()

    two = three = absorb

    def one(self):
        high, low, depth, pair = self.mover.grid.sizes
        c, rows, cols, grad, other, acc = self.mover.here[3], self.rows, self.cols, self.grad, self.pair, self.acc
        arrive(self.pending)

        def body(i, _):
            for j in range(depth):
                a, b = i // low, i % low
                acc[a, b, j, rows, cols] = grad[a, b, j, c, rows, cols] + other[a, b, j, rows, cols]
            return 0

        lax.fori_loop(0, high * low, body, 0)
        self.send()

    def finish(self):
        hi, lo, z, c = self.mover.here
        arrive(self.pending)
        total = self.acc[hi, lo, z, self.rows, self.cols].astype(jnp.float32)
        for s, _ in self.steps(self.axes[self.stage]):
            total = total + self.line_buf[s, self.rows, self.cols].astype(jnp.float32)
        self.total[self.rows, self.cols] = total


def sum_order(k):
    if k % 6 in (2, 3):
        return (0, 2, 1) if k % 2 == 0 else (1, 2, 0)
    return (0, 1, 2) if k % 2 == 0 else (1, 0, 2)


class Sizes:
    def __init__(self, grid, latents, shards):
        ada, attn, mlp, bias = (shard.shape[0] for shard in shards)
        self.slots, self.length, width = latents.shape
        self.width, self.bias = width, bias
        self.hidden = mlp * grid.count // (2 * width)
        self.parts = self.hidden // width
        self.ada_rows, self.qkv_rows = ada // (6 * width), attn // (3 * width)
        self.attn_rows, self.one_rows, self.mlp_rows = attn // width, mlp // self.hidden, mlp // width
        self.qkv_devices, self.one_devices = 3 * width * width // attn, width * self.hidden // mlp
        self.lead = 2 * SUBLANES - (2 * self.ada_rows) % (2 * SUBLANES)
        self.head_rows = self.lead + 2 * self.ada_rows
        self.tail_rows = 4 * self.ada_rows
        group = grid.depth * grid.pair
        exact = (
            self.hidden == self.parts * width, ada == self.ada_rows * 6 * width, attn == self.qkv_rows * 3 * width,
            mlp == self.one_rows * self.hidden, mlp == self.mlp_rows * width,
            self.qkv_devices * attn == 3 * width * width, self.one_devices * mlp == width * self.hidden,
        )
        whole = (
            self.qkv_rows % SUBLANES, (2 * self.one_rows) % SUBLANES, self.one_rows % 8, self.tail_rows % SUBLANES,
            self.qkv_devices % group, self.one_devices % group, width % LANES, (4 * self.slots) % SUBLANES,
            (2 * self.slots + 4 + self.parts) % SUBLANES, self.parts % grid.pair, self.mlp_rows % SUBLANES,
            (self.length % LANES), (2 * self.width // HEADS) % LANES,
        )
        per_tile = width // self.mlp_rows if width % self.mlp_rows == 0 else 0
        self.fits = (
            all(exact) and not any(whole) and grid.pair == 2 and self.slots < self.lead and bias <= 2 * LANES
            and bias <= width and per_tile > 0 and per_tile % grid.pair == 0 and group % per_tile == 0
            and grid.count * bias == (9 + self.parts + 1) * width and grid.high * grid.low * group == grid.count
        )


def fused_kernel(
    grid, sizes, count_ref, x_hbm, cond_ref, cot_hbm, ada_hbm, attn_hbm, mlp_hbm, bias_ref,
    out_ref, gx_ref, gcond_ref, g_ada_out, g_attn_out, g_mlp_out, g_bias_out,
    all_ada, all_attn, all_mlp, note_a, note_b, grad_attn, grad_mlp,
    pair_attn, pair_mlp, acc_attn, acc_mlp, one_attn, one_mlp, two_attn, two_mlp, side_attn, side_mlp, line_attn, line_mlp,
    sum_attn, sum_mlp, swap_out, swap_in, back_in,
    x_ref, cot_ref, ada_ref, attn_ref, mlp_ref, line, unit, local_rows, pick_head, pick_tail, spread, bias_rows,
    mod, norm_one, inv_one, h_one, qkv, probs, mixed, branch, norm_two, inv_two, h_two,
    slope, act, mlp, wide, back, dx, small, dqkv, dmod, gbias,
    send_sem, recv_sem, own_sem,
):
    mover = Mover(grid, send_sem, recv_sem)
    here = mover.here
    hi, lo, z, c = here
    high, low, depth, pair = grid.sizes
    me = ((hi * low + lo) * depth + z) * pair + c
    slots, length, width, hidden = sizes.slots, sizes.length, sizes.width, sizes.hidden
    rows_all = slots * length
    heads = probs.shape[1]
    head_dim = width // heads
    score_scale = head_dim ** (-0.5)
    f32, b16 = jnp.float32, jnp.bfloat16
    count = count_ref[0]
    parts, tiles = sizes.parts, width // LANES
    ada_rows, lead, head_rows, tail_rows = sizes.ada_rows, sizes.lead, sizes.head_rows, sizes.tail_rows
    group = depth * pair

    met = grid.greet(here)
    x_in = pltpu.make_async_copy(x_hbm, x_ref, own_sem.at[0])
    cot_in = pltpu.make_async_copy(cot_hbm, cot_ref, own_sem.at[1])
    shards_in = [
        pltpu.make_async_copy(a, b, own_sem.at[2 + n])
        for n, (a, b) in enumerate(((ada_hbm, ada_ref), (attn_hbm, attn_ref), (mlp_hbm, mlp_ref)))
    ]
    for copy in shards_in:
        copy.start()
    x_in.start()
    cot_in.start()

    def strided(start, rows, stride):
        return line[pl.ds(start, rows, stride=stride), :]

    def lanes(t):
        return slice(t * LANES, (t + 1) * LANES)

    def column_sum(values):
        return jnp.sum(values, axis=0, keepdims=True)

    cond = cond_ref[...]
    cond_act = (cond * jax.nn.sigmoid(cond)).astype(b16)
    shards_in[0].wait()
    line[0 : ada_ref.shape[0], :] = ada_ref[...].astype(f32)
    unit[0:lead, :] = jnp.zeros((lead, width), f32)
    for k in range(6):
        for t in range(tiles):
            unit[lead + ada_rows * k : lead + ada_rows * (k + 1), lanes(t)] = strided(
                tiles * k + t, ada_rows, 6 * tiles
            )
    unit[0:1, 0 : sizes.bias] = bias_ref[...].astype(f32)
    unit[1 : 1 + slots, :] = cond_act.astype(f32)
    all_ada[hi, lo, z, c] = unit[0 : head_rows + tail_rows, :].astype(b16)

    def cut_rows(ref, start, size):
        return [(ref, start + at, min(SUBLANES, size - at)) for at in range(0, size, SUBLANES)]

    pieces = cut_rows(all_ada, 0, head_rows), cut_rows(all_attn, 0, sizes.attn_rows)
    pieces += cut_rows(all_ada, head_rows, tail_rows), cut_rows(all_mlp, 0, sizes.mlp_rows)
    ends = [sum(len(piece) for piece in pieces[: k + 1]) for k in range(len(pieces))]
    shares = [
        Share(mover, ref, start, size, axis_order(k))
        for k, (ref, start, size) in enumerate(entry for piece in pieces for entry in piece)
    ]
    agenda, begun = [], ends[1]
    for t in range(len(shares) + 3 * LAG):
        while begun < min(len(shares), t + 2 + LAG):
            agenda.append((begun, "begin"))
            begun += 1
        for k, name in enumerate(("first", "second", "third", "end")):
            if 0 <= t - k * LAG < len(shares):
                agenda.append((t - k * LAG, name))

    def until(share, name):
        while (share, name) in agenda:
            k, step = agenda.pop(0)
            getattr(shares[k], step)()

    met()
    for share in shares[: ends[0]]:
        share.begin()

    shards_in[1].wait()
    line[0 : attn_ref.shape[0], :] = attn_ref[...].astype(f32)

    @pl.when(me < sizes.qkv_devices)
    def _():
        rows = sizes.qkv_rows
        for k in range(3):
            for t in range(tiles):
                unit[rows * k : rows * (k + 1), lanes(t)] = strided(tiles * k + t, rows, 3 * tiles)

    @pl.when(me >= sizes.qkv_devices)
    def _():
        for t in range(tiles):
            unit[0 : sizes.attn_rows, lanes(t)] = strided(t, sizes.attn_rows, tiles)

    all_attn[hi, lo, z, c] = unit[0 : sizes.attn_rows, :].astype(b16)
    for share in shares[ends[0] : ends[1]]:
        share.begin()

    one_rows, per_core = sizes.one_rows, parts // pair
    shards_in[2].wait()
    line[0 : mlp_ref.shape[0], :] = mlp_ref[...].astype(f32)

    @pl.when(me < sizes.one_devices)
    def _():
        for k in range(parts):
            for t in range(tiles):
                local_rows[one_rows * k : one_rows * (k + 1), lanes(t)] = strided(
                    tiles * k + t, one_rows, parts * tiles
                )
        for k in range(per_core):
            unit[pl.ds(pl.multiple_of(2 * one_rows * k + one_rows * c, 8), one_rows), :] = local_rows[
                pl.ds(pl.multiple_of(one_rows * (per_core * c + k), 8), one_rows), :
            ]

    @pl.when(me >= sizes.one_devices)
    def _():
        for t in range(tiles):
            unit[0 : sizes.mlp_rows, lanes(t)] = strided(t, sizes.mlp_rows, tiles)
        local_rows[...] = jnp.zeros_like(local_rows)

    cut = one_rows * per_core
    swap_out[...] = local_rows[pl.ds(pl.multiple_of(cut * (1 - c), 8), cut), :].astype(b16)
    partner = grid.peer(here, 3, 1)
    swap = mover.push(swap_out, swap_in, partner)

    def picks(total, span, skip, target):
        at = lax.broadcasted_iota(jnp.int32, (1, total), 1)
        device, row = at // span, at % span - skip
        entry = jnp.where(row >= 0, device * ada_rows + row % ada_rows, -1)
        source = lax.broadcasted_iota(jnp.int32, (width, total), 0)
        target[...] = jnp.where(source == entry, 1.0, 0.0).astype(b16)

    def owner_mask(total, span, skip, blocks):
        at = lax.broadcasted_iota(jnp.int32, (blocks * slots, total), 1)
        block = lax.broadcasted_iota(jnp.int32, (blocks * slots, total), 0) // slots
        row = at % span - skip
        return jnp.logical_and(row >= 0, row // ada_rows == block)

    def spread_cond(pick, total, span, skip, blocks):
        wide_cond = dot(cond_act, pick[...])
        stacked = jnp.concatenate([wide_cond] * blocks, axis=0)
        return jnp.where(owner_mask(total, span, skip, blocks), stacked, 0.0).astype(b16)

    head_total, tail_total = grid.count * head_rows, grid.count * tail_rows

    def norm_first(s):
        rows = slice(s * length, (s + 1) * length)
        normed, inverse = layer_norm(x_ref[s])
        norm_one[rows, :] = normed
        inv_one[rows, :] = inverse

    def part(s, k):
        return mod[k * slots + s : k * slots + s + 1, :]

    picks(head_total, head_rows, lead, pick_head)
    swap.wait_recv()

    @pl.when(me < sizes.one_devices)
    def _():
        local_rows[0:cut, :] = swap_in[...].astype(f32)
        for k in range(per_core):
            unit[pl.ds(pl.multiple_of(2 * one_rows * k + one_rows * (1 - c), 8), one_rows), :] = local_rows[
                one_rows * k : one_rows * (k + 1), :
            ]

    all_mlp[hi, lo, z, c] = unit[0 : sizes.mlp_rows, :].astype(b16)
    x_in.wait()
    until(ends[0] - 1, "first")
    for s in range(slots):
        norm_first(s)
        until(min(ends[0] + s, ends[1] - 1), "first")
    head_cond = spread_cond(pick_head, head_total, head_rows, lead, 2)
    picks(tail_total, tail_rows, 0, pick_tail)
    until(ends[0] - 1, "third")
    tail_cond = spread_cond(pick_tail, tail_total, tail_rows, 0, 4)
    until(ends[0] - 1, "end")

    def rows_of(ref, start, size):
        return ref[:, :, :, :, start : start + size, :].reshape(grid.count * size, width)

    mod[0 : 2 * slots, :] = dot(head_cond, rows_of(all_ada, 0, head_rows))

    bias_rows[...] = jnp.zeros_like(bias_rows)
    lane = lax.broadcasted_iota(jnp.int32, (1, width), 1)
    for d in range(grid.count):
        values = all_ada[d // (low * group), d // group % low, d // pair % depth, d % pair, 0:SUBLANES, :].astype(f32)[0:1]
        row, shift = divmod(d * sizes.bias, width)
        turned = pltpu.roll(values, shift, 1) if shift else values
        end = shift + sizes.bias
        bias_rows[row : row + 1, :] += jnp.where(jnp.logical_and(lane >= shift, lane < end), turned, 0.0)
        if end > width:
            bias_rows[row + 1 : row + 2, :] += jnp.where(lane < end - width, turned, 0.0)

    def add_mod_bias(first, last):
        for k in range(first, last):
            span = slice(k * slots, (k + 1) * slots)
            mod[span, :] = mod[span, :] + bias_rows[k : k + 1, :]

    add_mod_bias(0, 2)

    def modulate_first(s):
        rows = slice(s * length, (s + 1) * length)
        h_one[rows, :] = (norm_one[rows, :] * (1.0 + part(s, 1)) + part(s, 0)).astype(b16)

    for s in range(slots):
        modulate_first(s)
    until(ends[1] - 1, "end")

    def devices(ref, first, last, rows):
        pieces = []
        for g in range(first // group, last // group):
            piece = ref[g // low, g % low, :, :, rows, :]
            pieces.append(piece.reshape(group * piece.shape[2], width))
        return pieces[0] if len(pieces) == 1 else jnp.concatenate(pieces, axis=0)

    def qkv_weight(k):
        return devices(all_attn, 0, sizes.qkv_devices, slice(sizes.qkv_rows * k, sizes.qkv_rows * (k + 1)))

    def proj_weight():
        return devices(all_attn, sizes.qkv_devices, grid.count, slice(0, sizes.attn_rows))

    tall = 2 * one_rows

    def one_weight(t):
        core, k = t // per_core, t % per_core
        pieces = [
            all_mlp[g // low, g % low, :, core, tall * k : tall * (k + 1), :].reshape(depth * tall, width)
            for g in range(sizes.one_devices // group)
        ]
        return pieces[0] if len(pieces) == 1 else jnp.concatenate(pieces, axis=0)

    per_tile = width // sizes.mlp_rows

    def two_place(t):
        first = sizes.one_devices + per_tile * t
        g, at = first // group, first % group // pair
        return g // low, g % low, slice(at, at + per_tile // pair)

    def two_weight(t):
        a, b, zs = two_place(t)
        return all_mlp[a, b, zs, :, :, :].reshape(width, width)

    cut_head = 2 * head_dim
    upper = lax.broadcasted_iota(jnp.int32, (length, cut_head), 1) >= head_dim

    def both(block):
        zero = jnp.zeros_like(block)
        return jnp.concatenate([jnp.where(upper, zero, block), jnp.where(upper, block, zero)], axis=0)

    for k, row in enumerate((6, None, 7)):
        value = dot(h_one[...], qkv_weight(k))
        if row is not None:
            value = value + bias_rows[row : row + 1, :]
        qkv[:, k * width : (k + 1) * width] = value.astype(b16)

    def attend(s):
        rows = slice(s * length, (s + 1) * length)
        for p in range(heads // 2):
            at = p * cut_head
            query = qkv[rows, at : at + cut_head]
            key = qkv[rows, width + at : width + at + cut_head]
            value = qkv[rows, 2 * width + at : 2 * width + at + cut_head]
            scores = dot(both(query), key, (1, 1)) * score_scale
            total = jnp.log(jnp.sum(jnp.exp(scores), axis=-1, keepdims=True))
            prob = jnp.exp(scores - total)
            probs[s, 2 * p] = prob[:length]
            probs[s, 2 * p + 1] = prob[length:]
            prob = prob.astype(b16)
            side = jnp.concatenate([prob[:length], prob[length:]], axis=1)
            mixed[rows, at : at + cut_head] = dot(side, both(value)).astype(b16)

    for s in range(slots):
        attend(s)
        if s + 1 < slots:
            until(min(ends[1] + s, ends[2] - 1), "end")
    branch[...] = dot(mixed[...], proj_weight()) + bias_rows[8:9, :]
    until(ends[2] - 1, "end")
    mod[2 * slots :, :] = dot(tail_cond, rows_of(all_ada, head_rows, tail_rows))
    add_mod_bias(2, 6)

    def norm_second(s):
        rows = slice(s * length, (s + 1) * length)
        after = x_ref[s] + part(s, 2) * branch[rows, :]
        dx[rows, :] = after
        normed, inverse = layer_norm(after)
        norm_two[rows, :] = normed
        inv_two[rows, :] = inverse
        h_two[rows, :] = (normed * (1.0 + part(s, 4)) + part(s, 3)).astype(b16)

    for s in range(slots):
        norm_second(s)

    note_rows = note_a.shape[4]
    own_lane = lax.broadcasted_iota(jnp.int32, (SUBLANES, width), 1)
    own_row = lax.broadcasted_iota(jnp.int32, (SUBLANES, width), 0)
    own_pick = jnp.where(own_lane == own_row + me * ada_rows, 1.0, 0.0).astype(b16)
    columns = dot(own_pick, rows_of(all_ada, 0, head_rows), (1, 1)).astype(b16)
    note_total = grid.count * note_rows
    at = lax.broadcasted_iota(jnp.int32, (1, note_total), 1)
    wanted = at // note_rows * head_rows + 1 + at % note_rows % slots
    source = lax.broadcasted_iota(jnp.int32, (head_total, note_total), 0)
    spread[...] = dot(columns, jnp.where(source == wanted, 1.0, 0.0).astype(b16)).astype(b16)

    def up(t):
        cols = slice(t * width, (t + 1) * width)
        pre = dot(h_two[...], one_weight(t)) + bias_rows[9 + t : 10 + t, :]
        square = pre * pre
        tanh_part = jnp.tanh(ROOT_TWO_OVER_PI * (pre + GELU_COEF * pre * square))
        half = 0.5 * (1.0 + tanh_part)
        act[:, cols] = (pre * half).astype(b16)
        slope[:, cols] = half + 0.5 * pre * (1.0 - tanh_part * tanh_part) * ROOT_TWO_OVER_PI * (
            1.0 + 3.0 * GELU_COEF * square
        )

    for k in range(per_core):
        until(ends[2] - 1 + -(-tall * (k + 1) // SUBLANES), "end")
        for core in range(pair):
            up(core * per_core + k)
    until(ends[3] - 1, "end")

    gbias[...] = jnp.zeros_like(gbias)
    last = gbias.shape[0] - 1
    cot_in.wait()

    for s in range(slots):
        grad = jnp.where(s < count, cot_ref[s], 0.0)
        cot_ref[s] = grad
        small[s * length : (s + 1) * length, :] = (grad * part(s, 5)).astype(b16)

    def finish(s):
        rows = slice(s * length, (s + 1) * length)
        value, grad = mlp[rows, :], cot_ref[s]
        out_ref[s] = jnp.where(s < count, dx[rows, :] + part(s, 5) * value, 0.0)
        dmod[5 * slots + s : 5 * slots + s + 1, :] = column_sum(grad * value)
        gbias[last : last + 1, :] += column_sum(grad * part(s, 5))


    bufs_mlp = (grad_mlp, pair_mlp, acc_mlp, one_mlp, two_mlp, side_mlp, line_mlp, sum_mlp)
    bufs_attn = (grad_attn, pair_attn, acc_attn, one_attn, two_attn, side_attn, line_attn, sum_attn)
    early = [
        Reduce(mover, bufs_mlp, pl.ds(start, size), slice(None), sum_order(k))
        for k, (_, start, size) in enumerate(cut_rows(all_mlp, 0, sizes.mlp_rows))
    ]
    late = [
        Reduce(mover, bufs_attn, slice(None), pl.ds(p * cut_head, cut_head), sum_order(p % 2))
        for p in range(heads // 2)
    ]
    reduces = early + late
    n_early, n_all = len(early), len(reduces)
    note_first = Share(mover, note_a, 0, note_rows, axis_order(1))
    note_last = Share(mover, note_b, 0, note_rows, axis_order(1))

    def run(name, first, last):
        for reduce in reduces[first:last]:
            getattr(reduce, name)()

    def mlp_grads(t):
        cols = slice(t * width, (t + 1) * width)
        a, b, zs = two_place(t)
        grad_mlp[a, b, zs, :, :, :] = (
            dot(act[:, cols], small[...], (0, 0)).astype(b16).reshape(per_tile // pair, pair, sizes.mlp_rows, width)
        )

    def mlp_down(t):
        cols = slice(t * width, (t + 1) * width)
        full = dot(small[...], two_weight(t), (1, 1)) * slope[:, cols]
        gbias[3 + t : 4 + t, :] = column_sum(full)
        grad = full.astype(b16)
        wide[:, cols] = grad
        core, k = t // per_core, t % per_core
        whole = dot(h_two[...], grad, (0, 0)).astype(b16)
        for g in range(sizes.one_devices // group):
            grad_mlp[g // low, g % low, :, core, tall * k : tall * (k + 1), :] = whole[
                g * depth * tall : (g + 1) * depth * tall
            ].reshape(depth, tall, width)

    for t in range(parts):
        mlp_grads(t)
    sent = 0
    for k in range(per_core):
        for core in range(pair):
            mlp_down(core * per_core + k)
        ready = n_early if k + 1 == per_core else tall * (k + 1) // SUBLANES
        run("begin", sent, ready)
        sent = ready
    two_all = jnp.concatenate([two_weight(t) for t in range(parts)], axis=0)
    mlp[...] = dot(act[...], two_all) + bias_rows[9 + parts : 10 + parts, :]
    for s in range(slots):
        finish(s)
    third = -(-n_early // 3)
    marks = [min(n_early, third * k) for k in range(4)]
    run("one", 0, marks[1])
    one_all = jnp.concatenate([one_weight(t) for t in range(parts)], axis=1)
    back[...] = dot(wide[...], one_all, (1, 1))
    run("one", marks[1], marks[2])

    def mlp_back(s):
        rows = slice(s * length, (s + 1) * length)
        grad_two = back[rows, :]
        normed = norm_two[rows, :]
        dmod[4 * slots + s : 4 * slots + s + 1, :] = column_sum(grad_two * normed)
        dmod[3 * slots + s : 3 * slots + s + 1, :] = column_sum(grad_two)
        after = cot_ref[s] + norm_backward(grad_two * (1.0 + part(s, 4)), normed, inv_two[rows, :])
        dx[rows, :] = after
        dmod[2 * slots + s : 2 * slots + s + 1, :] = column_sum(after * branch[rows, :])
        full = after * part(s, 2)
        gbias[2:3, :] += column_sum(full)
        small[rows, :] = full.astype(b16)

    for s in range(slots):
        mlp_back(s)
    note_a[hi, lo, z, c] = dmod[2 * slots :, :].astype(b16)
    note_first.begin()
    whole = dot(mixed[...], small[...], (0, 0)).astype(b16)
    for g in range(sizes.qkv_devices // group, grid.count // group):
        base = (g * group - sizes.qkv_devices) * sizes.attn_rows
        grad_attn[g // low, g % low] = whole[base : base + group * sizes.attn_rows].reshape(
            depth, pair, sizes.attn_rows, width
        )
    mixed[...] = dot(small[...], proj_weight(), (1, 1)).astype(b16)

    def attend_back(s, p):
        rows = slice(s * length, (s + 1) * length)
        at = p * cut_head
        span = slice(at, at + cut_head)
        query = qkv[rows, span]
        key = qkv[rows, width + at : width + at + cut_head]
        value = qkv[rows, 2 * width + at : 2 * width + at + cut_head]
        grad = both(mixed[rows, span])
        prob = jnp.concatenate([probs[s, 2 * p], probs[s, 2 * p + 1]], axis=0)
        d_prob = dot(grad, value, (1, 1))
        d_value = dot(prob.astype(b16), grad, (0, 0)).astype(b16)
        delta = jnp.sum(prob * d_prob, axis=-1, keepdims=True)
        d_score = (prob * (d_prob - delta) * score_scale).astype(b16)
        side = jnp.concatenate([d_score[:length], d_score[length:]], axis=1)
        d_query = dot(side, both(key)).astype(b16)
        d_key = dot(d_score, both(query), (0, 0)).astype(b16)
        dqkv[rows, span] = d_query
        dqkv[rows, width + at : width + at + cut_head] = d_key
        dqkv[rows, 2 * width + at : 2 * width + at + cut_head] = d_value
        gbias[0:1, span] += column_sum(d_query.astype(f32))
        gbias[1:2, span] += column_sum(d_value.astype(f32))

    between = {
        0: lambda: (run("two", 0, marks[1]), run("one", marks[2], marks[3])),
        1: lambda: (run("one", n_early, n_early + 1), note_first.first(), run("two", marks[1], marks[2])),
        2: lambda: (run("one", n_early + 1, n_early + 2), run("three", 0, marks[1])),
    }
    for p in range(heads // 2):
        for s in range(slots):
            attend_back(s, p)
        sides = [dqkv[:, k * width + p * cut_head : k * width + (p + 1) * cut_head] for k in range(3)]
        whole = dot(h_one[...], jnp.concatenate(sides, axis=1), (0, 0)).astype(b16)
        for k in range(3):
            block = whole[:, k * cut_head : (k + 1) * cut_head]
            for g in range(sizes.qkv_devices // group):
                base = g * group * sizes.qkv_rows
                grad_attn[
                    g // low, g % low, :, :, sizes.qkv_rows * k : sizes.qkv_rows * (k + 1),
                    p * cut_head : (p + 1) * cut_head,
                ] = block[base : base + group * sizes.qkv_rows].reshape(depth, pair, sizes.qkv_rows, cut_head)
        run("begin", n_early + p, n_early + p + 1)
        if p in between:
            between.pop(p)()
    for action in between.values():
        action()
    back[...] = dot(dqkv[:, 0:width], qkv_weight(0), (1, 1)) + (
        dot(dqkv[:, width : 2 * width], qkv_weight(1), (1, 1)) + dot(dqkv[:, 2 * width :], qkv_weight(2), (1, 1))
    )
    run("one", n_early + 2, n_all)

    def attn_back(s):
        rows = slice(s * length, (s + 1) * length)
        grad_one = back[rows, :]
        normed = norm_one[rows, :]
        dmod[slots + s : slots + s + 1, :] = column_sum(grad_one * normed)
        dmod[s : s + 1, :] = column_sum(grad_one)

    def input_back(s):
        rows = slice(s * length, (s + 1) * length)
        grad_one = back[rows, :]
        normed = norm_one[rows, :]
        gx_ref[s] = dx[rows, :] + norm_backward(grad_one * (1.0 + part(s, 1)), normed, inv_one[rows, :])

    for s in range(slots):
        attn_back(s)
    note_b[hi, lo, z, c] = jnp.concatenate([dmod[0 : 2 * slots, :], gbias[...]], axis=0).astype(b16)
    note_last.begin()
    for s in range(slots):
        input_back(s)
    run("two", marks[2], marks[3])
    run("three", marks[1], marks[2])
    run("two", n_early, n_early + 2)
    note_first.second()
    run("finish", 0, marks[1])

    def gather_entries(first, blocks, start, rows, total, span, skip, pick):
        grad_mod = dmod[first * slots : (first + blocks) * slots, :].astype(b16)
        values = dot(grad_mod, rows_of(all_ada, start, rows), (1, 1))
        values = jnp.where(owner_mask(total, span, skip, blocks), values, 0.0)
        merged = values[0:slots]
        for k in range(1, blocks):
            merged = merged + values[k * slots : (k + 1) * slots]
        upper_part = merged.astype(b16)
        lower_part = (merged - upper_part.astype(f32)).astype(b16)
        return dot(upper_part, pick[...], (1, 1)) + dot(lower_part, pick[...], (1, 1))

    grad_act = gather_entries(2, 4, head_rows, tail_rows, tail_total, tail_rows, 0, pick_tail)
    note_last.first()
    run("two", n_early + 2, n_all)
    run("three", marks[2], marks[3])
    run("finish", marks[1], marks[2])
    run("three", n_early, n_early + 2)
    note_first.third()
    grad_act = grad_act + gather_entries(0, 2, 0, head_rows, head_total, head_rows, lead, pick_head)
    gcond_ref[...] = grad_act * silu_slope(cond)
    note_last.second()
    run("three", n_early + 2, n_all)
    note_first.end()

    def from_notes(note, blocks, extra):
        kept = []
        entry = lax.broadcasted_iota(jnp.int32, (SUBLANES, note_total), 1) % note_rows
        for k in range(blocks):
            kept.append(jnp.where(entry // slots == k, spread[...].astype(f32), 0.0))
        line_at = lax.broadcasted_iota(jnp.int32, (SUBLANES, note_total), 0)
        wanted = jnp.where(entry < blocks * slots, entry // slots, entry - blocks * slots + blocks)
        kept.append(jnp.where(wanted == line_at, 1.0, 0.0))
        left = jnp.concatenate(kept, axis=0).astype(b16)
        return dot(left, rows_of(note, 0, note_rows))

    def store_ada(source, first, blocks):
        for k in range(blocks):
            for t in range(tiles):
                g_ada_out[pl.ds(tiles * (first + k) + t, ada_rows, stride=6 * tiles), :] = source[
                    k * SUBLANES : k * SUBLANES + ada_rows, lanes(t)
                ]

    early = from_notes(note_a, 4, 0)
    store_ada(early, 2, 4)
    note_last.third()
    run("finish", marks[2], marks[3])
    home = [
        mover.push(
            sum_mlp.at[pl.ds(pl.multiple_of(tall * k + one_rows * (1 - c), 8), one_rows)], back_in.at[k], partner
        )
        for k in range(per_core)
    ]
    arrive(home)
    for core in range(pair):
        @pl.when(jnp.logical_and(me < sizes.one_devices, c == core))
        def _():
            for k in range(per_core):
                for t in range(tiles):
                    own_at, far_at = per_core * core + k, per_core * (1 - core) + k
                    base = tall * k + one_rows * core
                    g_mlp_out[pl.ds(tiles * own_at + t, one_rows, stride=parts * tiles), :] = sum_mlp[
                        base : base + one_rows, lanes(t)
                    ]
                    g_mlp_out[pl.ds(tiles * far_at + t, one_rows, stride=parts * tiles), :] = back_in[k, :, lanes(t)]

    @pl.when(me >= sizes.one_devices)
    def _():
        for t in range(tiles):
            g_mlp_out[pl.ds(t, sizes.mlp_rows, stride=tiles), :] = sum_mlp[:, lanes(t)]

    note_last.end()
    late = from_notes(note_b, 2, gbias.shape[0])
    store_ada(late, 0, 2)
    bias_rows[0:2, :] = late[2 * SUBLANES : 2 * SUBLANES + 2]
    bias_rows[2:6, :] = early[4 * SUBLANES : 4 * SUBLANES + 4]
    bias_rows[6 : 6 + gbias.shape[0], :] = late[2 * SUBLANES + 2 : 2 * SUBLANES + 2 + gbias.shape[0]]
    begin = me * sizes.bias
    row, shift = begin // width, begin % width
    pair_rows = jnp.concatenate(
        [bias_rows[pl.ds(row, 1), :], bias_rows[pl.ds(row + 1, 1), :]], axis=1
    )
    turned = pltpu.roll(pair_rows, 2 * width - shift, 1)
    for t in range(g_bias_out.shape[0]):
        g_bias_out[t : t + 1, :] = turned[:, lanes(t)]

    run("finish", n_early, n_all)

    @pl.when(me < sizes.qkv_devices)
    def _():
        rows = sizes.qkv_rows
        for k in range(3):
            for t in range(tiles):
                g_attn_out[pl.ds(tiles * k + t, rows, stride=3 * tiles), :] = sum_attn[rows * k : rows * (k + 1), lanes(t)]

    @pl.when(me >= sizes.qkv_devices)
    def _():
        for t in range(tiles):
            g_attn_out[pl.ds(t, sizes.attn_rows, stride=tiles), :] = sum_attn[:, lanes(t)]

    mover.drain()
    assert len(mover.started) == send_sem.shape[0]


def run_fused(grid, sizes, counts, latents, conditioning, cotangent, shards, bias):
    slots, length, width, hidden = sizes.slots, sizes.length, sizes.width, sizes.hidden
    high, low, depth, pair = grid.sizes
    f32, b16 = jnp.float32, jnp.bfloat16
    rows = slots * length
    ada, attn, mlp = (shard.reshape(-1, LANES) for shard in shards)
    attn_rows, mlp_rows, one_rows = sizes.attn_rows, sizes.mlp_rows, sizes.one_rows
    ada_all = sizes.head_rows + sizes.tail_rows
    note_rows = 4 * slots
    extra = 4 + sizes.parts
    per_core = sizes.parts // pair
    side = max(high, low)
    tails = [(attn_rows, width), (mlp_rows, width)]
    leads = [
        (high, low, depth), (high, low, depth), (max(side - 1, 1), side, depth),
        (max(side - 1, 1), depth), (max(depth - 1, 1), side), (max(depth - 1, side - 1, 1),),
    ]
    scratch = [(grid.sizes + (n, width), b16) for n in (ada_all, attn_rows, mlp_rows, note_rows, note_rows)]
    scratch += [(grid.sizes + tail, b16) for tail in tails]
    scratch += [(lead + tail, b16) for lead in leads for tail in tails]
    scratch += [(tail, f32) for tail in tails]
    cut = per_core * one_rows
    scratch += [((cut, width), b16), ((cut, width), b16), ((per_core, one_rows, width), f32)]
    scratch += [(latents.shape, f32)] * 2 + [(array.shape, b16) for array in (ada, attn, mlp)]
    scratch += [
        ((max(ada.shape[0], attn.shape[0], mlp.shape[0]), LANES), f32), ((max(mlp_rows, attn_rows, ada_all), width), f32),
        ((sizes.parts * one_rows, width), f32),
        ((width, grid.count * sizes.head_rows), b16), ((width, grid.count * sizes.tail_rows), b16),
        ((SUBLANES, grid.count * note_rows), b16), ((-(-(7 + extra) // 8) * 8, width), f32),
    ]
    scratch += [
        ((6 * slots, width), f32), ((rows, width), f32), ((rows, 1), f32), ((rows, width), b16),
        ((rows, 3 * width), b16), ((slots, HEADS, length, length), f32), ((rows, width), b16),
        ((rows, width), f32), ((rows, width), f32), ((rows, 1), f32), ((rows, width), b16),
        ((rows, hidden), f32), ((rows, hidden), b16), ((rows, width), f32), ((rows, hidden), b16),
        ((rows, width), f32), ((rows, width), f32), ((rows, width), b16), ((rows, 3 * width), b16),
        ((6 * slots, width), f32), ((extra, width), f32),
    ]
    ceil = lambda n: -(-n // SUBLANES)
    gathers = ceil(sizes.head_rows) + ceil(sizes.tail_rows) + ceil(attn_rows) + ceil(mlp_rows)
    copies = sum(Share.copies(grid, axis_order(k)) for k in list(range(gathers)) + [1, 1])
    copies += (HEADS // 2 + ceil(mlp_rows)) * (high + low + depth + pair - 4)
    copies += 1 + per_core
    vmem, anywhere = pl.BlockSpec(memory_space=pltpu.VMEM), pl.BlockSpec(memory_space=pl.ANY)
    far = pl.BlockSpec(memory_space=pltpu.HBM)
    outs = [
        (latents.shape, f32), (latents.shape, f32), (conditioning.shape, f32),
        (ada.shape, f32), (attn.shape, f32), (mlp.shape, f32), ((-(-bias.shape[1] // LANES), LANES), f32),
    ]
    pinned = lambda array: pltpu.with_memory_space_constraint(array, pltpu.HBM)
    results = pl.pallas_call(
        partial(fused_kernel, grid, sizes),
        out_shape=[jax.ShapeDtypeStruct(shape, kind) for shape, kind in outs],
        in_specs=[pl.BlockSpec(memory_space=pltpu.SMEM), far, vmem, far, far, far, far, vmem],
        out_specs=[vmem] * len(outs),
        scratch_shapes=[pltpu.VMEM(shape, kind) for shape, kind in scratch]
        + [pltpu.SemaphoreType.DMA((copies,)), pltpu.SemaphoreType.DMA((copies,)), pltpu.SemaphoreType.DMA((5,))],
        compiler_params=pltpu.CompilerParams(
            collective_id=2, has_side_effects=True, vmem_limit_bytes=50 * 1024 * 1024
        ),
    )(counts, pinned(latents), conditioning, pinned(cotangent), pinned(ada), pinned(attn), pinned(mlp), bias)
    return pl.pallas_call(
        hand_on,
        out_shape=[jax.ShapeDtypeStruct(shape, kind) for shape, kind in outs],
        in_specs=[anywhere] * len(outs),
        out_specs=[far] * len(outs),
        scratch_shapes=[pltpu.SemaphoreType.DMA((len(outs),))],
        compiler_params=pltpu.CompilerParams(vmem_limit_bytes=4 * 1024 * 1024),
    )(*results)


def hand_on(*refs):
    ins, outs, sem = refs[: len(refs) // 2], refs[len(refs) // 2 : -1], refs[-1]
    copies = [pltpu.make_async_copy(a, b, sem.at[n]) for n, (a, b) in enumerate(zip(ins, outs))]
    for copy in copies:
        copy.start()
    for copy in copies:
        copy.wait()


def local(
    grid, latents, conditioning, counts, cotangent, ada_weights, attn_weights, mlp_weights, flat_biases
):
    model_width = latents.shape[-1]
    slots = latents.shape[0]
    shards = (ada_weights, attn_weights, mlp_weights, flat_biases)
    sizes = Sizes(grid, latents, shards)
    if sizes.fits:
        outs = run_fused(
            grid, sizes, counts, latents, conditioning, cotangent, shards[:3], flat_biases[None]
        )
        return tuple(outs[:3]) + tuple(
            total.reshape(-1)[: shard.shape[0]] for total, shard in zip(outs[3:], shards)
        )
    whole_ada, whole_attn, whole_mlp, whole_bias = gather_all(
        grid, [pack([shard], ()) for shard in shards]
    )
    bias_flat = whole_bias.reshape(grid.count, -1)[:, : flat_biases.shape[0]].reshape(-1)
    weights = (
        whole_ada.reshape(model_width, 6 * model_width),
        whole_attn.reshape(-1, LANES),
        whole_mlp.reshape(-1, LANES),
    )
    biases = bias_flat.astype(jnp.float32)[None]
    output, grad_latents, grad_conditioning, cond_act, grad_mod, g_attn, g_mlp, g_bias = (
        run_block(counts, latents, conditioning, cotangent, weights, biases)
    )

    gap = padded_rows(flat_biases.shape[0]) * LANES - flat_biases.shape[0]
    bias_lines = jnp.pad(
        g_bias.astype(jnp.bfloat16).reshape(grid.count, -1), ((0, 0), (0, gap))
    )
    all_mod, all_act, *sums = scatter_sum(
        grid,
        [flat.reshape(grid.sizes + (-1, LANES)) for flat in (g_attn, g_mlp, bias_lines)],
        [grad_mod, cond_act],
    )
    all_mod = all_mod.reshape(grid.count * slots, -1)
    all_act = all_act.reshape(grid.count * slots, -1)
    grads = [own_rows(all_act, all_mod, ada_weights.shape[0])]
    grads += [total.reshape(-1)[: shard.shape[0]] for total, shard in zip(sums, shards[1:])]
    return (output, grad_latents, grad_conditioning) + tuple(grads)


def own_rows(left, right, extent):
    wide = right.shape[1]
    start = lax.axis_index(AXES) * extent
    rows = min(-(-extent // wide) + (1 if extent % wide else 0), left.shape[1])
    top = jnp.minimum(start // wide, left.shape[1] - rows)
    part = lax.dynamic_slice_in_dim(left, top, rows, 1)
    whole = dot(part, right, (0, 0)).reshape(-1)
    if rows * wide == extent:
        return whole
    return lax.dynamic_slice_in_dim(whole, start - top * wide, extent, 0)


def solution(mesh):
    in_specs = (
        P(("dp", "fsdp"), None, None),
        P(("dp", "fsdp"), None),
        P(("dp", "fsdp")),
        P(("dp", "fsdp"), None, None),
        P(("dp", "fsdp")),
        P(("dp", "fsdp")),
        P(("dp", "fsdp")),
        P(("dp", "fsdp")),
    )
    out_specs = (
        P(("dp", "fsdp"), None, None),
        P(("dp", "fsdp"), None, None),
        P(("dp", "fsdp"), None),
        P(("dp", "fsdp")),
        P(("dp", "fsdp")),
        P(("dp", "fsdp")),
        P(("dp", "fsdp")),
    )
    return jax.shard_map(partial(local, Grid(mesh)), mesh=mesh, in_specs=in_specs, out_specs=out_specs, check_vma=False)
```

```python
from functools import partial
import math

import jax
import jax.numpy as jnp
from jax import lax
from jax.experimental import pallas as pl
from jax.experimental.pallas import tpu as pltpu
from jax.sharding import PartitionSpec as P

FF = 1536
HEADS = 6


EPSILON = 1e-06
GELU_COEF = 0.044715
ROOT_TWO_OVER_PI = 0.7978845608028654


def layer_norm(values):
    centre = values - jnp.mean(values, axis=-1, keepdims=True)
    inverse = lax.rsqrt(jnp.mean(centre * centre, axis=-1, keepdims=True) + EPSILON)
    return (centre * inverse, inverse)


def norm_backward(grad_norm, normed, inverse):
    first = jnp.mean(grad_norm, axis=-1, keepdims=True)
    second = jnp.mean(grad_norm * normed, axis=-1, keepdims=True)
    return (grad_norm - first - normed * second) * inverse


def gelu_value(pre_act):
    inner = ROOT_TWO_OVER_PI * (pre_act + GELU_COEF * pre_act * pre_act * pre_act)
    return 0.5 * pre_act * (1.0 + jnp.tanh(inner))


def gelu_slope(pre_act):
    tanh_part = jnp.tanh(ROOT_TWO_OVER_PI * (pre_act + GELU_COEF * pre_act * pre_act * pre_act))
    return 0.5 * (1.0 + tanh_part) + 0.5 * pre_act * (
        1.0 - tanh_part * tanh_part
    ) * ROOT_TWO_OVER_PI * (1.0 + 3.0 * GELU_COEF * pre_act * pre_act)


def silu_slope(values):
    sigma = jax.nn.sigmoid(values)
    return sigma * (1.0 + values * (1.0 - sigma))


LANES = 128
SUBLANES = 16
AXES = ("dp", "fsdp")
MESH = pl.DeviceIdType.MESH


class Grid:
    def __init__(self, mesh):
        dp, fsdp = mesh.shape["dp"], mesh.shape["fsdp"]
        side = math.isqrt(dp)
        self.high = side if side * side == dp else 1
        self.low = dp // self.high
        self.pair = 2 if fsdp % 2 == 0 else 1
        self.depth = fsdp // self.pair
        self.count = dp * fsdp
        self.sizes = (self.high, self.low, self.depth, self.pair)

    def here(self):
        a, f = lax.axis_index("dp"), lax.axis_index("fsdp")
        return [a // self.low, a % self.low, f // self.pair, f % self.pair]

    def peer(self, here, axis, step):
        spot = list(here)
        spot[axis] = lax.rem(here[axis] + step, self.sizes[axis])
        return spot

    def ident(self, spot):
        return (spot[0] * self.low + spot[1], spot[2] * self.pair + spot[3])

    def greet(self, here):
        sem = pltpu.get_barrier_semaphore()
        total = 0
        for axis in range(4):
            for step in range(1, self.sizes[axis]):
                pl.semaphore_signal(
                    sem, inc=1, device_id=self.ident(self.peer(here, axis, step)), device_id_type=MESH
                )
                total += 1
        return lambda: pl.semaphore_wait(sem, total)

    def barrier(self, here):
        self.greet(here)()


def chunk_rows(arrays):
    chunks = []
    for n, array in enumerate(arrays):
        rows = array.shape[-2]
        if rows % (2 * SUBLANES) == 0:
            chunks += [(n, 0, rows // 2), (n, rows // 2, rows // 2)]
        else:
            chunks.append((n, 0, rows))
    return chunks


class Mover:
    def __init__(self, grid, send_sem, recv_sem):
        self.grid, self.here = grid, grid.here()
        self.send_sem, self.recv_sem = send_sem, recv_sem
        self.started = []

    def push(self, src, dst, spot):
        k = len(self.started)
        copy = pltpu.make_async_remote_copy(
            src_ref=src, dst_ref=dst, send_sem=self.send_sem.at[k], recv_sem=self.recv_sem.at[k],
            device_id=self.grid.ident(spot), device_id_type=MESH,
        )
        copy.start()
        self.started.append(copy)
        return copy

    def spots(self, axis):
        return [self.grid.peer(self.here, axis, s) for s in range(1, self.grid.sizes[axis])]

    def pushes(self, ref, axis):
        return [self.push(ref, ref, spot) for spot in self.spots(axis)]

    def drain(self):
        for copy in self.started:
            copy.wait_send()


def arrive(copies):
    for copy in copies:
        copy.wait_recv()


class Spread:
    def __init__(self, mover, in_ref, out_ref, rows, low_first):
        self.mover, self.in_ref, self.out_ref, self.rows = mover, in_ref, out_ref, rows
        self.low_first = low_first
        self.swap = []

    def begin(self):
        hi, lo, z, c = self.mover.here
        src, dst = self.in_ref.at[self.rows], self.out_ref.at[hi, lo, z, c, self.rows]
        self.pending = [self.mover.push(src, dst, spot) for spot in self.mover.spots(2)]

    def first(self):
        hi, lo, z, c = self.mover.here
        arrive(self.pending)
        part = self.out_ref.at[hi, lo, :, c, self.rows]
        self.pending = self.mover.pushes(part, 1 if self.low_first else 0)
        self.swap += self.mover.pushes(part, 3)

    def second(self):
        hi, lo, z, c = self.mover.here
        arrive(self.pending)
        out, rows = self.out_ref, self.rows
        if self.low_first:
            self.pending = self.mover.pushes(out.at[hi, :, :, c, rows], 0)
            others = [out.at[hi, spot[1], :, c, rows] for spot in self.mover.spots(1)]
        else:
            self.pending = self.mover.pushes(out.at[:, lo, :, c, rows], 1)
            others = [out.at[spot[0], lo, :, c, rows] for spot in self.mover.spots(0)]
        for other in others:
            self.swap += self.mover.pushes(other, 3)

    def third(self):
        hi, lo, z, c = self.mover.here
        arrive(self.pending)
        out, rows = self.out_ref, self.rows
        if self.low_first:
            others = [out.at[spot[0], :, :, c, rows] for spot in self.mover.spots(0)]
        else:
            others = [out.at[:, spot[1], :, c, rows] for spot in self.mover.spots(1)]
        for other in others:
            self.swap += self.mover.pushes(other, 3)

    def end(self):
        arrive(self.swap)

    @staticmethod
    def copies(grid):
        high, low, depth, pair = grid.sizes
        return depth - 1 + (high + low - 2) + (pair - 1) * (1 + high + low - 2)


def gather_kernel(grid, chunks, arrays, *refs):
    in_refs, out_refs = refs[:arrays], refs[arrays : 2 * arrays]
    send_sem, recv_sem, own_sem = refs[2 * arrays :]
    mover = Mover(grid, send_sem, recv_sem)
    hi, lo, z, c = mover.here
    grid.barrier(mover.here)
    own = [
        pltpu.make_async_copy(in_refs[n], out_refs[n].at[hi, lo, z, c], own_sem.at[n])
        for n in range(arrays)
    ]
    for copy in own:
        copy.start()
    spreads = [
        Spread(mover, in_refs[n], out_refs[n], pl.ds(start, size), k % 2 == 0)
        for k, (n, start, size) in enumerate(chunks)
    ]
    for spread in spreads:
        spread.begin()
    for copy in own:
        copy.wait()
    for spread in spreads:
        spread.first()
    for spread in spreads:
        spread.second()
    for spread in spreads:
        spread.third()
    for spread in spreads:
        spread.end()
    mover.drain()


def gather_all(grid, arrays):
    chunks = chunk_rows(arrays)
    copies = Spread.copies(grid) * len(chunks)
    vmem = pl.BlockSpec(memory_space=pltpu.VMEM)
    return pl.pallas_call(
        partial(gather_kernel, grid, chunks, len(arrays)),
        out_shape=[jax.ShapeDtypeStruct(grid.sizes + array.shape, array.dtype) for array in arrays],
        in_specs=[vmem] * len(arrays),
        out_specs=[vmem] * len(arrays),
        scratch_shapes=[
            pltpu.SemaphoreType.DMA((copies,)),
            pltpu.SemaphoreType.DMA((copies,)),
            pltpu.SemaphoreType.DMA((len(arrays),)),
        ],
        compiler_params=pltpu.CompilerParams(
            collective_id=0, has_side_effects=True, vmem_limit_bytes=48 * 1024 * 1024
        ),
    )(*arrays)


def scatter_kernel(grid, chunks, arrays, extra, *refs):
    note_refs, refs = refs[:extra], refs[extra:]
    g_refs, refs = refs[:arrays], refs[arrays:]
    note_outs, refs = refs[:extra], refs[extra:]
    out_refs, refs = refs[:arrays], refs[arrays:]
    pair_bufs, refs = refs[:arrays], refs[arrays:]
    accs, refs = refs[:arrays], refs[arrays:]
    one_bufs, refs = refs[:arrays], refs[arrays:]
    two_bufs, refs = refs[:arrays], refs[arrays:]
    z_bufs, (send_sem, recv_sem, own_sem) = refs[:arrays], refs[arrays:]
    mover = Mover(grid, send_sem, recv_sem)
    here, push = mover.here, mover.push
    hi, lo, z, c = here
    grid.barrier(here)
    owns = [
        pltpu.make_async_copy(note_refs[n], note_outs[n].at[hi, lo, z, c], own_sem.at[n])
        for n in range(extra)
    ]
    notes = [
        Spread(mover, note_refs[n], note_outs[n], pl.ds(0, note_refs[n].shape[0]), n % 2 == 0)
        for n in range(extra)
    ]
    for own, note in zip(owns, notes):
        own.start()
        note.begin()

    def steps(axis):
        return [(s - 1, grid.peer(here, axis, s)) for s in range(1, grid.sizes[axis])]

    def add(into, terms, first, second):
        def body(t, _):
            i, j = t // second, t % second
            total = terms[0](i, j)[...].astype(jnp.float32)
            for term in terms[1:]:
                total = total + term(i, j)[...].astype(jnp.float32)
            target = into(i, j)
            target[...] = total.astype(target.dtype)
            return 0

        lax.fori_loop(0, first * second, body, 0)

    high, low, depth, pair = grid.sizes
    swaps, ones, twos, lines = [], [], [], []
    for n, start, size in chunks:
        rows = pl.ds(start, size)
        g_ref, pair_buf = g_refs[n], pair_bufs[n]
        swaps.append(
            [push(g_ref.at[:, :, :, spot[3], rows], pair_buf.at[:, :, :, rows], spot) for _, spot in steps(3)]
        )
    for own, note in zip(owns, notes):
        own.wait()
        note.first()
    for k, (n, start, size) in enumerate(chunks):
        rows = pl.ds(start, size)
        g_ref, pair_buf, acc, buf_one = g_refs[n], pair_bufs[n], accs[n], one_bufs[n]
        arrive(swaps[k])
        terms = [lambda i, j: g_ref.at[i // low, i % low, j, c, rows]]
        if pair > 1:
            terms.append(lambda i, j: pair_buf.at[i // low, i % low, j, rows])
        add(lambda i, j: acc.at[i // low, i % low, j, rows], terms, high * low, depth)
        if k % 2 == 0:
            ones.append(
                [push(acc.at[spot[0], :, :, rows], buf_one.at[s, 0:low, :, rows], spot) for s, spot in steps(0)]
            )
        else:
            ones.append(
                [push(acc.at[:, spot[1], :, rows], buf_one.at[s, 0:high, :, rows], spot) for s, spot in steps(1)]
            )
    for note in notes:
        note.second()
    for k, (n, start, size) in enumerate(chunks):
        rows = pl.ds(start, size)
        acc, buf_one, buf_two = accs[n], one_bufs[n], two_bufs[n]
        arrive(ones[k])
        even = k % 2 == 0
        mine = (lambda i, j: acc.at[hi, i, j, rows]) if even else (lambda i, j: acc.at[i, lo, j, rows])
        terms = [mine] + [
            (lambda i, j, s=s: buf_one.at[s, i, j, rows]) for s, _ in steps(0 if even else 1)
        ]
        add(mine, terms, low if even else high, depth)
        if even:
            twos.append(
                [push(acc.at[hi, spot[1], :, rows], buf_two.at[s, :, rows], spot) for s, spot in steps(1)]
            )
        else:
            twos.append(
                [push(acc.at[spot[0], lo, :, rows], buf_two.at[s, :, rows], spot) for s, spot in steps(0)]
            )
    for note in notes:
        note.third()
    for k, (n, start, size) in enumerate(chunks):
        rows = pl.ds(start, size)
        acc, buf_two, buf_z = accs[n], two_bufs[n], z_bufs[n]
        arrive(twos[k])
        mine = lambda i, j: acc.at[hi, lo, j, rows]
        terms = [mine] + [
            (lambda i, j, s=s: buf_two.at[s, j, rows]) for s, _ in steps(1 if k % 2 == 0 else 0)
        ]
        add(mine, terms, 1, depth)
        lines.append(
            [push(acc.at[hi, lo, spot[2], rows], buf_z.at[s, rows], spot) for s, spot in steps(2)]
        )
    for k, (n, start, size) in enumerate(chunks):
        rows = pl.ds(start, size)
        acc, buf_z = accs[n], z_bufs[n]
        arrive(lines[k])
        total = acc[hi, lo, z, rows].astype(jnp.float32)
        for s in range(depth - 1):
            total = total + buf_z[s, rows].astype(jnp.float32)
        out_refs[n][rows, :] = total
    for note in notes:
        note.end()
    mover.drain()


def scatter_sum(grid, arrays, notes):
    high, low, depth, pair = grid.sizes
    chunks = chunk_rows(arrays)
    copies = len(chunks) * (high + low + depth + pair - 4) + Spread.copies(grid) * len(notes)
    kind = arrays[0].dtype
    tails = [array.shape[-2:] for array in arrays]
    side = max(high, low)
    shapes = [
        (high, low, depth), (high, low, depth), (max(side - 1, 1), side, depth),
        (max(side - 1, 1), depth), (max(depth - 1, 1),),
    ]
    vmem = pl.BlockSpec(memory_space=pltpu.VMEM)
    return pl.pallas_call(
        partial(scatter_kernel, grid, chunks, len(arrays), len(notes)),
        out_shape=[jax.ShapeDtypeStruct(grid.sizes + note.shape, note.dtype) for note in notes]
        + [jax.ShapeDtypeStruct(tail, jnp.float32) for tail in tails],
        in_specs=[vmem] * (len(notes) + len(arrays)),
        out_specs=[vmem] * (len(notes) + len(arrays)),
        scratch_shapes=[pltpu.VMEM(shape + tail, kind) for shape in shapes for tail in tails]
        + [pltpu.SemaphoreType.DMA((copies,)), pltpu.SemaphoreType.DMA((copies,)), pltpu.SemaphoreType.DMA((len(notes),))],
        compiler_params=pltpu.CompilerParams(
            collective_id=1, has_side_effects=True, vmem_limit_bytes=48 * 1024 * 1024
        ),
    )(*notes, *arrays)


def padded_rows(extent):
    return -(-extent // LANES)


def pack(pieces, lead):
    parts = []
    for piece in pieces:
        extent = piece.shape[-1]
        rows = padded_rows(extent)
        gap = rows * LANES - extent
        if gap:
            piece = jnp.pad(piece, [(0, 0)] * len(lead) + [(0, gap)])
        parts.append(piece.reshape(lead + (rows, LANES)))
    if len(parts) == 1:
        return parts[0]
    return jnp.concatenate(parts, axis=-2)


def dot(left, right, contract=(1, 0)):
    return lax.dot_general(
        left, right, (((contract[0],), (contract[1],)), ((), ())), preferred_element_type=jnp.float32
    )


def block_kernel(
    count_ref, x_ref, cond_ref, cot_ref, w_ada, attn_ref, mlp_ref, bias_ref,
    out_ref, gx_ref, gcond_ref, act_ref, dmod_ref, g_attn, g_mlp, gbias_ref,
    line, w_qkv, w_proj, w_one, w_two, g_qkv, g_proj, g_one, g_two,
    mod, norm_one, inv_one, h_one, qkv, probs, mixed, branch, norm_two, inv_two, h_two,
    pre, act, mlp, wide, back, dx, small, dqkv, dmod,
):
    slots, length, width = x_ref.shape
    hidden = w_one.shape[1]
    rows_all = slots * length
    heads = probs.shape[1]
    head_dim = width // heads
    score_scale = head_dim ** (-0.5)
    f32, b16 = jnp.float32, jnp.bfloat16
    tile = 256 if hidden % 256 == 0 else hidden
    count = count_ref[0]
    o_query, o_value = 6 * width, 7 * width
    o_proj, o_one, o_two = 8 * width, 9 * width, 9 * width + hidden
    lane = lax.broadcasted_iota(jnp.int32, (length, 2 * head_dim), 1)
    lower = lane < head_dim

    def slot_loop(body):
        def step(s, _):
            body(s, pl.ds(pl.multiple_of(s * length, length), length))
            return 0

        lax.fori_loop(0, slots, step, 0)

    def part(s, k):
        return mod[pl.ds(s, 1), k * width : (k + 1) * width]

    def only(pair_block, first):
        return jnp.where(lower if first else jnp.logical_not(lower), pair_block, jnp.zeros_like(pair_block))

    def column_sum(values):
        return jnp.sum(values, axis=0, keepdims=True)

    def load_matrix(flat_ref, top, matrix):
        height, across = matrix.shape[0], matrix.shape[1] // LANES
        total = height * across

        def widen(t, _):
            at = pl.multiple_of(t * LANES, LANES)
            line[pl.ds(at, LANES), :] = flat_ref[pl.ds(top + at, LANES), :].astype(f32)
            return 0

        lax.fori_loop(0, total // LANES, widen, 0)
        for j in range(across):
            matrix[:, j * LANES : (j + 1) * LANES] = line[pl.ds(j, height, stride=across), :].astype(b16)

    def store_matrix(matrix, flat_ref, top):
        height, across = matrix.shape[0], matrix.shape[1] // LANES
        total = height * across
        for j in range(across):
            line[pl.ds(j, height, stride=across), :] = matrix[:, j * LANES : (j + 1) * LANES].astype(f32)

        def narrow(t, _):
            at = pl.multiple_of(t * LANES, LANES)
            flat_ref[pl.ds(top + at, LANES), :] = line[pl.ds(at, LANES), :].astype(b16)
            return 0

        lax.fori_loop(0, total // LANES, narrow, 0)

    proj_top, two_top = 3 * width * width // LANES, width * hidden // LANES
    load_matrix(attn_ref, 0, w_qkv)
    load_matrix(attn_ref, proj_top, w_proj)
    load_matrix(mlp_ref, 0, w_one)
    load_matrix(mlp_ref, two_top, w_two)
    cond = cond_ref[...]
    cond_act = (cond * jax.nn.sigmoid(cond)).astype(b16)
    mod[...] = dot(cond_act, w_ada[...]) + bias_ref[:, : 6 * width]

    def norm_first(s, rows):
        normed, inverse = layer_norm(x_ref[s])
        norm_one[rows, :] = normed
        inv_one[rows, :] = inverse
        h_one[rows, :] = (normed * (1.0 + part(s, 1)) + part(s, 0)).astype(b16)

    slot_loop(norm_first)
    for k, offset in enumerate((o_query, None, o_value)):
        cols = slice(k * width, (k + 1) * width)
        value = dot(h_one[...], w_qkv[:, cols])
        if offset is not None:
            value = value + bias_ref[:, offset : offset + width]
        qkv[:, cols] = value.astype(b16)

    def attend(s, rows):
        for pair in range(heads // 2):
            at = pair * 2 * head_dim
            query = qkv[rows, at : at + 2 * head_dim]
            key = qkv[rows, width + at : width + at + 2 * head_dim]
            value = qkv[rows, 2 * width + at : 2 * width + at + 2 * head_dim]
            halves = []
            for h in range(2):
                scores = dot(only(query, h == 0), key, (1, 1)) * score_scale
                total = jnp.log(jnp.sum(jnp.exp(scores), axis=-1, keepdims=True))
                prob = jnp.exp(scores - total)
                probs[s, 2 * pair + h] = prob
                halves.append(dot(prob.astype(b16), value))
            mixed[rows, at : at + 2 * head_dim] = jnp.where(lower, halves[0], halves[1]).astype(b16)

    slot_loop(attend)
    branch[...] = dot(mixed[...], w_proj[...]) + bias_ref[:, o_proj : o_proj + width]

    def norm_second(s, rows):
        after = x_ref[s] + part(s, 2) * branch[rows, :]
        dx[rows, :] = after
        normed, inverse = layer_norm(after)
        norm_two[rows, :] = normed
        inv_two[rows, :] = inverse
        h_two[rows, :] = (normed * (1.0 + part(s, 4)) + part(s, 3)).astype(b16)

    slot_loop(norm_second)

    def up(t, _):
        cols = pl.ds(pl.multiple_of(t * tile, tile), tile)
        shift = bias_ref[:, pl.ds(pl.multiple_of(o_one + t * tile, LANES), tile)]
        value = dot(h_two[...], w_one[:, cols]) + shift
        pre[:, cols] = value
        act[:, cols] = gelu_value(value).astype(b16)
        return 0

    lax.fori_loop(0, hidden // tile, up, 0)
    mlp[...] = dot(act[...], w_two[...]) + bias_ref[:, o_two : o_two + width]

    gbias_ref[...] = jnp.zeros_like(gbias_ref)

    def finish(s, rows):
        live = s < count
        value = mlp[rows, :]
        out_ref[s] = jnp.where(live, dx[rows, :] + part(s, 5) * value, 0.0)
        grad = jnp.where(live, cot_ref[s], 0.0)
        dmod[pl.ds(s, 1), 5 * width :] = column_sum(grad * value)
        full = grad * part(s, 5)
        gbias_ref[:, o_two : o_two + width] += column_sum(full)
        small[rows, :] = full.astype(b16)

    slot_loop(finish)

    def down(t, _):
        cols = pl.ds(pl.multiple_of(t * tile, tile), tile)
        full = dot(small[...], w_two[cols, :], (1, 1)) * gelu_slope(pre[:, cols])
        gbias_ref[:, pl.ds(pl.multiple_of(o_one + t * tile, LANES), tile)] = column_sum(full)
        grad = full.astype(b16)
        wide[:, cols] = grad
        g_two[cols, :] = dot(act[:, cols], small[...], (0, 0)).astype(g_two.dtype)
        g_one[:, cols] = dot(h_two[...], grad, (0, 0)).astype(g_one.dtype)
        return 0

    lax.fori_loop(0, hidden // tile, down, 0)
    back[...] = dot(wide[...], w_one[...], (1, 1))

    def mlp_back(s, rows):
        grad_two = back[rows, :]
        normed = norm_two[rows, :]
        dmod[pl.ds(s, 1), 4 * width : 5 * width] = column_sum(grad_two * normed)
        dmod[pl.ds(s, 1), 3 * width : 4 * width] = column_sum(grad_two)
        after = jnp.where(s < count, cot_ref[s], 0.0) + norm_backward(
            grad_two * (1.0 + part(s, 4)), normed, inv_two[rows, :]
        )
        dx[rows, :] = after
        dmod[pl.ds(s, 1), 2 * width : 3 * width] = column_sum(after * branch[rows, :])
        full = after * part(s, 2)
        gbias_ref[:, o_proj : o_proj + width] += column_sum(full)
        small[rows, :] = full.astype(b16)

    slot_loop(mlp_back)
    g_proj[...] = dot(mixed[...], small[...], (0, 0)).astype(g_proj.dtype)
    mixed[...] = dot(small[...], w_proj[...], (1, 1)).astype(b16)

    def attend_back(s, rows):
        for pair in range(heads // 2):
            at = pair * 2 * head_dim
            span = slice(at, at + 2 * head_dim)
            query = qkv[rows, span]
            key = qkv[rows, width + at : width + at + 2 * head_dim]
            value = qkv[rows, 2 * width + at : 2 * width + at + 2 * head_dim]
            grad = mixed[rows, span]
            d_query, d_key, d_value = [], [], []
            for h in range(2):
                prob = probs[s, 2 * pair + h]
                d_prob = dot(only(grad, h == 0), value, (1, 1))
                d_value.append(dot(prob.astype(b16), grad, (0, 0)))
                delta = jnp.sum(prob * d_prob, axis=-1, keepdims=True)
                d_score = (prob * (d_prob - delta) * score_scale).astype(b16)
                d_query.append(dot(d_score, key))
                d_key.append(dot(d_score, query, (0, 0)))
            d_query = jnp.where(lower, d_query[0], d_query[1]).astype(b16)
            d_key = jnp.where(lower, d_key[0], d_key[1]).astype(b16)
            d_value = jnp.where(lower, d_value[0], d_value[1]).astype(b16)
            dqkv[rows, span] = d_query
            dqkv[rows, width + at : width + at + 2 * head_dim] = d_key
            dqkv[rows, 2 * width + at : 2 * width + at + 2 * head_dim] = d_value
            gbias_ref[:, o_query + at : o_query + at + 2 * head_dim] += column_sum(d_query.astype(f32))
            gbias_ref[:, o_value + at : o_value + at + 2 * head_dim] += column_sum(d_value.astype(f32))

    slot_loop(attend_back)
    for k in range(3):
        cols = slice(k * width, (k + 1) * width)
        g_qkv[:, cols] = dot(h_one[...], dqkv[:, cols], (0, 0)).astype(g_qkv.dtype)
    back[...] = dot(dqkv[...], w_qkv[...], (1, 1))

    def attn_back(s, rows):
        grad_one = back[rows, :]
        normed = norm_one[rows, :]
        dmod[pl.ds(s, 1), width : 2 * width] = column_sum(grad_one * normed)
        dmod[pl.ds(s, 1), :width] = column_sum(grad_one)
        gx_ref[s] = dx[rows, :] + norm_backward(
            grad_one * (1.0 + part(s, 1)), normed, inv_one[rows, :]
        )

    slot_loop(attn_back)
    gbias_ref[:, : 6 * width] = column_sum(dmod[...])
    grad_mod = dmod[...].astype(b16)
    store_matrix(g_qkv, g_attn, 0)
    store_matrix(g_proj, g_attn, proj_top)
    store_matrix(g_one, g_mlp, 0)
    store_matrix(g_two, g_mlp, two_top)
    act_ref[...] = cond_act
    dmod_ref[...] = grad_mod
    gcond_ref[...] = dot(grad_mod, w_ada[...], (1, 1)) * silu_slope(cond)


def run_block(counts, latents, conditioning, cotangent, weights, biases):
    slots, length, width = latents.shape
    w_ada, attn, mlp = weights
    hidden = mlp.size // (2 * width)
    rows = slots * length
    f32, b16 = jnp.float32, jnp.bfloat16
    outs = [
        (latents.shape, f32), (latents.shape, f32), (conditioning.shape, f32),
        (conditioning.shape, b16), ((slots, 6 * width), b16),
        (attn.shape, b16), (mlp.shape, b16), (biases.shape, f32),
    ]
    matrices = [(width, 3 * width), (width, width), (width, hidden), (hidden, width)]
    scratch = [((max(h * w for h, w in matrices) // LANES, LANES), f32)]
    scratch += [(shape, b16) for shape in matrices + matrices]
    scratch += [
        ((slots, 6 * width), f32), ((rows, width), f32), ((rows, 1), f32), ((rows, width), b16),
        ((rows, 3 * width), b16), ((slots, HEADS, length, length), f32), ((rows, width), b16),
        ((rows, width), f32), ((rows, width), f32), ((rows, 1), f32), ((rows, width), b16),
        ((rows, hidden), f32), ((rows, hidden), b16), ((rows, width), f32), ((rows, hidden), b16),
        ((rows, width), f32), ((rows, width), f32), ((rows, width), b16), ((rows, 3 * width), b16),
        ((slots, 6 * width), f32),
    ]
    vmem = pl.BlockSpec(memory_space=pltpu.VMEM)
    return pl.pallas_call(
        block_kernel,
        out_shape=[jax.ShapeDtypeStruct(shape, kind) for shape, kind in outs],
        in_specs=[pl.BlockSpec(memory_space=pltpu.SMEM)] + [vmem] * 7,
        out_specs=[vmem] * len(outs),
        scratch_shapes=[pltpu.VMEM(shape, kind) for shape, kind in scratch],
        compiler_params=pltpu.CompilerParams(vmem_limit_bytes=60 * 1024 * 1024),
    )(counts, latents, conditioning, cotangent, *weights, biases)


LAG = 3


class Share:
    def __init__(self, mover, ref, start, size, axes):
        self.mover, self.ref, self.rows, self.axes = mover, ref, pl.ds(start, size), axes
        self.spot, self.stage, self.swap = list(mover.here[:3]), 0, []

    def at(self, spot):
        return self.ref.at[spot[0], spot[1], spot[2], self.mover.here[3], self.rows]

    def begin(self):
        self.pending = self.mover.pushes(self.at(self.spot), self.axes[self.stage])

    def absorb(self):
        arrive(self.pending)
        axis, spot = self.axes[self.stage], list(self.spot)
        self.spot[axis] = slice(None)
        if self.stage == 0:
            news = [self.spot]
        else:
            news = [spot[:axis] + [peer[axis]] + spot[axis + 1 :] for peer in self.mover.spots(axis)]
        news = [list(new) for new in news]
        self.stage += 1
        if self.stage < 3:
            self.begin()
        for new in news:
            self.swap += self.mover.pushes(self.at(new), 3)

    first = second = third = absorb

    def end(self):
        arrive(self.swap)

    @staticmethod
    def copies(grid, axes):
        one, two, three = (grid.sizes[axis] - 1 for axis in axes)
        return one + two + three + (grid.pair - 1) * (1 + two + three)


def axis_order(k):
    if k % 6 in (4, 5):
        return (1, 2, 0) if k % 2 == 0 else (0, 2, 1)
    return (2, 1, 0) if k % 2 == 0 else (2, 0, 1)


class Reduce:
    def __init__(self, mover, bufs, rows, cols, axes):
        self.mover, self.axes, self.rows, self.cols = mover, axes, rows, cols
        self.grad, self.pair, self.acc, self.plane_buf, self.deep_buf, self.side_buf, self.line_buf, self.total = bufs
        self.fixed, self.stage = {}, 0

    def steps(self, axis):
        grid, here = self.mover.grid, self.mover.here
        return [(s - 1, grid.peer(here, axis, s)) for s in range(1, grid.sizes[axis])]

    def place(self, fixed):
        index = [fixed.get(axis, slice(None)) for axis in range(3)]
        return self.acc.at[index[0], index[1], index[2], self.rows, self.cols]

    def slot(self, s, spots=None):
        sizes = self.mover.grid.sizes
        left = [axis for axis in range(3) if axis not in self.fixed and axis != self.axes[self.stage]]
        at = tuple(slice(0, sizes[axis]) if spots is None else spots[axis] for axis in left)
        buf = self.line_buf if not left else self.plane_buf if len(left) == 2 else (
            self.deep_buf if left[0] == 2 else self.side_buf
        )
        return buf.at[(s,) + at + (self.rows, self.cols)]

    def begin(self):
        self.pending = [
            self.mover.push(
                self.grad.at[:, :, :, spot[3], self.rows, self.cols],
                self.pair.at[:, :, :, self.rows, self.cols], spot,
            )
            for _, spot in self.steps(3)
        ]

    def send(self):
        axis = self.axes[self.stage]
        self.pending = [
            self.mover.push(self.place({**self.fixed, axis: spot[axis]}), self.slot(s), spot)
            for s, spot in self.steps(axis)
        ]

    def absorb(self):
        arrive(self.pending)
        axis, sizes = self.axes[self.stage], self.mover.grid.sizes
        spots = [{}]
        for other in range(3):
            if other not in self.fixed and other != axis:
                spots = [{**spot, other: n} for spot in spots for n in range(sizes[other])]
        arrived = [[self.slot(s, spot) for s, _ in self.steps(axis)] for spot in spots]
        self.fixed[axis] = self.mover.here[axis]
        for spot, terms in zip(spots, arrived):
            into = self.place({**self.fixed, **spot})
            total = into[...]
            for term in terms:
                total = total + term[...]
            into[...] = total
        self.stage += 1
        self.send()

    two = three = absorb

    def one(self):
        high, low, depth, pair = self.mover.grid.sizes
        c, rows, cols, grad, other, acc = self.mover.here[3], self.rows, self.cols, self.grad, self.pair, self.acc
        arrive(self.pending)

        def body(i, _):
            for j in range(depth):
                a, b = i // low, i % low
                acc[a, b, j, rows, cols] = grad[a, b, j, c, rows, cols] + other[a, b, j, rows, cols]
            return 0

        lax.fori_loop(0, high * low, body, 0)
        self.send()

    def finish(self):
        hi, lo, z, c = self.mover.here
        arrive(self.pending)
        total = self.acc[hi, lo, z, self.rows, self.cols].astype(jnp.float32)
        for s, _ in self.steps(self.axes[self.stage]):
            total = total + self.line_buf[s, self.rows, self.cols].astype(jnp.float32)
        self.total[self.rows, self.cols] = total


def sum_order(k):
    if k % 6 in (2, 3):
        return (0, 2, 1) if k % 2 == 0 else (1, 2, 0)
    return (0, 1, 2) if k % 2 == 0 else (1, 0, 2)


class Sizes:
    def __init__(self, grid, latents, shards):
        ada, attn, mlp, bias = (shard.shape[0] for shard in shards)
        self.slots, self.length, width = latents.shape
        self.width, self.bias = width, bias
        self.hidden = mlp * grid.count // (2 * width)
        self.parts = self.hidden // width
        self.ada_rows, self.qkv_rows = ada // (6 * width), attn // (3 * width)
        self.attn_rows, self.one_rows, self.mlp_rows = attn // width, mlp // self.hidden, mlp // width
        self.qkv_devices, self.one_devices = 3 * width * width // attn, width * self.hidden // mlp
        self.lead = 2 * SUBLANES - (2 * self.ada_rows) % (2 * SUBLANES)
        self.head_rows = self.lead + 2 * self.ada_rows
        self.tail_rows = 4 * self.ada_rows
        group = grid.depth * grid.pair
        exact = (
            self.hidden == self.parts * width, ada == self.ada_rows * 6 * width, attn == self.qkv_rows * 3 * width,
            mlp == self.one_rows * self.hidden, mlp == self.mlp_rows * width,
            self.qkv_devices * attn == 3 * width * width, self.one_devices * mlp == width * self.hidden,
        )
        whole = (
            self.qkv_rows % SUBLANES, (2 * self.one_rows) % SUBLANES, self.one_rows % 8, self.tail_rows % SUBLANES,
            self.qkv_devices % group, self.one_devices % group, width % LANES, (4 * self.slots) % SUBLANES,
            (2 * self.slots + 4 + self.parts) % SUBLANES, self.parts % grid.pair, self.mlp_rows % SUBLANES,
            (self.length % LANES), (2 * self.width // HEADS) % LANES,
        )
        per_tile = width // self.mlp_rows if width % self.mlp_rows == 0 else 0
        self.fits = (
            all(exact) and not any(whole) and grid.pair == 2 and self.slots < self.lead and bias <= 2 * LANES
            and bias <= width and per_tile > 0 and per_tile % grid.pair == 0 and group % per_tile == 0
            and grid.count * bias == (9 + self.parts + 1) * width and grid.high * grid.low * group == grid.count
        )


def fused_kernel(
    grid, sizes, count_ref, x_hbm, cond_hbm, cot_hbm, ada_hbm, attn_hbm, mlp_hbm, bias_hbm,
    out_ref, gx_ref, gcond_ref, g_ada_out, g_attn_out, g_mlp_out, g_bias_out,
    all_ada, all_attn, all_mlp, note_a, note_b, grad_attn, grad_mlp,
    pair_attn, pair_mlp, acc_attn, acc_mlp, one_attn, one_mlp, two_attn, two_mlp, side_attn, side_mlp, line_attn, line_mlp,
    sum_attn, sum_mlp, swap_out, swap_in, back_in,
    x_ref, cot_ref, ada_ref, attn_ref, mlp_ref, cond_ref, bias_ref, line, unit, local_rows, pick_head, pick_tail, spread, bias_rows,
    mod, norm_one, inv_one, h_one, qkv, probs, mixed, branch, norm_two, inv_two, h_two,
    slope, act, mlp, wide, back, dx, small, dqkv, dmod, gbias,
    send_sem, recv_sem, own_sem,
):
    mover = Mover(grid, send_sem, recv_sem)
    here = mover.here
    hi, lo, z, c = here
    high, low, depth, pair = grid.sizes
    me = ((hi * low + lo) * depth + z) * pair + c
    slots, length, width, hidden = sizes.slots, sizes.length, sizes.width, sizes.hidden
    rows_all = slots * length
    heads = probs.shape[1]
    head_dim = width // heads
    score_scale = head_dim ** (-0.5)
    f32, b16 = jnp.float32, jnp.bfloat16
    count = count_ref[0]
    parts, tiles = sizes.parts, width // LANES
    ada_rows, lead, head_rows, tail_rows = sizes.ada_rows, sizes.lead, sizes.head_rows, sizes.tail_rows
    group = depth * pair

    met = grid.greet(here)
    x_in = pltpu.make_async_copy(x_hbm, x_ref, own_sem.at[0])
    cot_in = pltpu.make_async_copy(cot_hbm, cot_ref, own_sem.at[1])
    shards_in = [
        pltpu.make_async_copy(a, b, own_sem.at[2 + n])
        for n, (a, b) in enumerate(
            ((ada_hbm, ada_ref), (attn_hbm, attn_ref), (mlp_hbm, mlp_ref), (cond_hbm, cond_ref), (bias_hbm, bias_ref))
        )
    ]
    for n in (3, 4, 0, 1, 2):
        shards_in[n].start()
    x_in.start()
    cot_in.start()

    def strided(start, rows, stride):
        return line[pl.ds(start, rows, stride=stride), :]

    def lanes(t):
        return slice(t * LANES, (t + 1) * LANES)

    def column_sum(values):
        return jnp.sum(values, axis=0, keepdims=True)

    shards_in[3].wait()
    shards_in[4].wait()
    cond = cond_ref[...]
    cond_act = (cond * jax.nn.sigmoid(cond)).astype(b16)
    shards_in[0].wait()
    line[0 : ada_ref.shape[0], :] = ada_ref[...].astype(f32)
    unit[0:lead, :] = jnp.zeros((lead, width), f32)
    for k in range(6):
        for t in range(tiles):
            unit[lead + ada_rows * k : lead + ada_rows * (k + 1), lanes(t)] = strided(
                tiles * k + t, ada_rows, 6 * tiles
            )
    unit[0:1, 0 : sizes.bias] = bias_ref[...].astype(f32).reshape(1, sizes.bias)
    unit[1 : 1 + slots, :] = cond_act.astype(f32)
    all_ada[hi, lo, z, c] = unit[0 : head_rows + tail_rows, :].astype(b16)

    def cut_rows(ref, start, size):
        return [(ref, start + at, min(SUBLANES, size - at)) for at in range(0, size, SUBLANES)]

    pieces = cut_rows(all_ada, 0, head_rows), cut_rows(all_attn, 0, sizes.attn_rows)
    pieces += cut_rows(all_ada, head_rows, tail_rows), cut_rows(all_mlp, 0, sizes.mlp_rows)
    ends = [sum(len(piece) for piece in pieces[: k + 1]) for k in range(len(pieces))]
    shares = [
        Share(mover, ref, start, size, axis_order(k))
        for k, (ref, start, size) in enumerate(entry for piece in pieces for entry in piece)
    ]
    agenda, begun = [], ends[1]
    for t in range(len(shares) + 3 * LAG):
        while begun < min(len(shares), t + 2 + LAG):
            agenda.append((begun, "begin"))
            begun += 1
        for k, name in enumerate(("first", "second", "third", "end")):
            if 0 <= t - k * LAG < len(shares):
                agenda.append((t - k * LAG, name))

    def until(share, name):
        while (share, name) in agenda:
            k, step = agenda.pop(0)
            getattr(shares[k], step)()

    met()
    for share in shares[: ends[0]]:
        share.begin()

    shards_in[1].wait()
    line[0 : attn_ref.shape[0], :] = attn_ref[...].astype(f32)

    @pl.when(me < sizes.qkv_devices)
    def _():
        rows = sizes.qkv_rows
        for k in range(3):
            for t in range(tiles):
                unit[rows * k : rows * (k + 1), lanes(t)] = strided(tiles * k + t, rows, 3 * tiles)

    @pl.when(me >= sizes.qkv_devices)
    def _():
        for t in range(tiles):
            unit[0 : sizes.attn_rows, lanes(t)] = strided(t, sizes.attn_rows, tiles)

    all_attn[hi, lo, z, c] = unit[0 : sizes.attn_rows, :].astype(b16)
    for share in shares[ends[0] : ends[1]]:
        share.begin()

    one_rows, per_core = sizes.one_rows, parts // pair
    shards_in[2].wait()
    line[0 : mlp_ref.shape[0], :] = mlp_ref[...].astype(f32)

    @pl.when(me < sizes.one_devices)
    def _():
        for k in range(parts):
            for t in range(tiles):
                local_rows[one_rows * k : one_rows * (k + 1), lanes(t)] = strided(
                    tiles * k + t, one_rows, parts * tiles
                )
        for k in range(per_core):
            unit[pl.ds(pl.multiple_of(2 * one_rows * k + one_rows * c, 8), one_rows), :] = local_rows[
                pl.ds(pl.multiple_of(one_rows * (per_core * c + k), 8), one_rows), :
            ]

    @pl.when(me >= sizes.one_devices)
    def _():
        for t in range(tiles):
            unit[0 : sizes.mlp_rows, lanes(t)] = strided(t, sizes.mlp_rows, tiles)
        local_rows[...] = jnp.zeros_like(local_rows)

    cut = one_rows * per_core
    swap_out[...] = local_rows[pl.ds(pl.multiple_of(cut * (1 - c), 8), cut), :].astype(b16)
    partner = grid.peer(here, 3, 1)
    swap = mover.push(swap_out, swap_in, partner)

    def picks(total, span, skip, target):
        at = lax.broadcasted_iota(jnp.int32, (1, total), 1)
        device, row = at // span, at % span - skip
        entry = jnp.where(row >= 0, device * ada_rows + row % ada_rows, -1)
        source = lax.broadcasted_iota(jnp.int32, (width, total), 0)
        target[...] = jnp.where(source == entry, 1.0, 0.0).astype(b16)

    def owner_mask(total, span, skip, blocks):
        at = lax.broadcasted_iota(jnp.int32, (blocks * slots, total), 1)
        block = lax.broadcasted_iota(jnp.int32, (blocks * slots, total), 0) // slots
        row = at % span - skip
        return jnp.logical_and(row >= 0, row // ada_rows == block)

    def spread_cond(pick, total, span, skip, blocks):
        wide_cond = dot(cond_act, pick[...])
        stacked = jnp.concatenate([wide_cond] * blocks, axis=0)
        return jnp.where(owner_mask(total, span, skip, blocks), stacked, 0.0).astype(b16)

    head_total, tail_total = grid.count * head_rows, grid.count * tail_rows

    def norm_first(s):
        rows = slice(s * length, (s + 1) * length)
        normed, inverse = layer_norm(x_ref[s])
        norm_one[rows, :] = normed
        inv_one[rows, :] = inverse

    def part(s, k):
        return mod[k * slots + s : k * slots + s + 1, :]

    picks(head_total, head_rows, lead, pick_head)
    swap.wait_recv()

    @pl.when(me < sizes.one_devices)
    def _():
        local_rows[0:cut, :] = swap_in[...].astype(f32)
        for k in range(per_core):
            unit[pl.ds(pl.multiple_of(2 * one_rows * k + one_rows * (1 - c), 8), one_rows), :] = local_rows[
                one_rows * k : one_rows * (k + 1), :
            ]

    all_mlp[hi, lo, z, c] = unit[0 : sizes.mlp_rows, :].astype(b16)
    x_in.wait()
    until(ends[0] - 1, "first")
    for s in range(slots):
        norm_first(s)
        until(min(ends[0] + s, ends[1] - 1), "first")
    head_cond = spread_cond(pick_head, head_total, head_rows, lead, 2)
    picks(tail_total, tail_rows, 0, pick_tail)
    until(ends[0] - 1, "third")
    tail_cond = spread_cond(pick_tail, tail_total, tail_rows, 0, 4)
    until(ends[0] - 1, "end")

    def rows_of(ref, start, size):
        return ref[:, :, :, :, start : start + size, :].reshape(grid.count * size, width)

    mod[0 : 2 * slots, :] = dot(head_cond, rows_of(all_ada, 0, head_rows))

    bias_rows[...] = jnp.zeros_like(bias_rows)
    lane = lax.broadcasted_iota(jnp.int32, (1, width), 1)
    for d in range(grid.count):
        values = all_ada[d // (low * group), d // group % low, d // pair % depth, d % pair, 0:SUBLANES, :].astype(f32)[0:1]
        row, shift = divmod(d * sizes.bias, width)
        turned = pltpu.roll(values, shift, 1) if shift else values
        end = shift + sizes.bias
        bias_rows[row : row + 1, :] += jnp.where(jnp.logical_and(lane >= shift, lane < end), turned, 0.0)
        if end > width:
            bias_rows[row + 1 : row + 2, :] += jnp.where(lane < end - width, turned, 0.0)

    def add_mod_bias(first, last):
        for k in range(first, last):
            span = slice(k * slots, (k + 1) * slots)
            mod[span, :] = mod[span, :] + bias_rows[k : k + 1, :]

    add_mod_bias(0, 2)

    def modulate_first(s):
        rows = slice(s * length, (s + 1) * length)
        h_one[rows, :] = (norm_one[rows, :] * (1.0 + part(s, 1)) + part(s, 0)).astype(b16)

    for s in range(slots):
        modulate_first(s)
    until(ends[1] - 1, "end")

    def devices(ref, first, last, rows):
        pieces = []
        for g in range(first // group, last // group):
            piece = ref[g // low, g % low, :, :, rows, :]
            pieces.append(piece.reshape(group * piece.shape[2], width))
        return pieces[0] if len(pieces) == 1 else jnp.concatenate(pieces, axis=0)

    def qkv_weight(k):
        return devices(all_attn, 0, sizes.qkv_devices, slice(sizes.qkv_rows * k, sizes.qkv_rows * (k + 1)))

    def proj_weight():
        return devices(all_attn, sizes.qkv_devices, grid.count, slice(0, sizes.attn_rows))

    tall = 2 * one_rows

    def one_weight(t):
        core, k = t // per_core, t % per_core
        pieces = [
            all_mlp[g // low, g % low, :, core, tall * k : tall * (k + 1), :].reshape(depth * tall, width)
            for g in range(sizes.one_devices // group)
        ]
        return pieces[0] if len(pieces) == 1 else jnp.concatenate(pieces, axis=0)

    per_tile = width // sizes.mlp_rows

    def two_place(t):
        first = sizes.one_devices + per_tile * t
        g, at = first // group, first % group // pair
        return g // low, g % low, slice(at, at + per_tile // pair)

    def two_weight(t):
        a, b, zs = two_place(t)
        return all_mlp[a, b, zs, :, :, :].reshape(width, width)

    cut_head = 2 * head_dim
    upper = lax.broadcasted_iota(jnp.int32, (length, cut_head), 1) >= head_dim

    def both(block):
        zero = jnp.zeros_like(block)
        return jnp.concatenate([jnp.where(upper, zero, block), jnp.where(upper, block, zero)], axis=0)

    for k, row in enumerate((6, None, 7)):
        value = dot(h_one[...], qkv_weight(k))
        if row is not None:
            value = value + bias_rows[row : row + 1, :]
        qkv[:, k * width : (k + 1) * width] = value.astype(b16)

    def attend(s):
        rows = slice(s * length, (s + 1) * length)
        for p in range(heads // 2):
            at = p * cut_head
            query = qkv[rows, at : at + cut_head]
            key = qkv[rows, width + at : width + at + cut_head]
            value = qkv[rows, 2 * width + at : 2 * width + at + cut_head]
            scores = dot(both(query), key, (1, 1)) * score_scale
            total = jnp.log(jnp.sum(jnp.exp(scores), axis=-1, keepdims=True))
            prob = jnp.exp(scores - total)
            probs[s, 2 * p] = prob[:length]
            probs[s, 2 * p + 1] = prob[length:]
            prob = prob.astype(b16)
            side = jnp.concatenate([prob[:length], prob[length:]], axis=1)
            mixed[rows, at : at + cut_head] = dot(side, both(value)).astype(b16)

    for s in range(slots):
        attend(s)
        if s + 1 < slots:
            until(min(ends[1] + s, ends[2] - 1), "end")
    branch[...] = dot(mixed[...], proj_weight()) + bias_rows[8:9, :]
    until(ends[2] - 1, "end")
    mod[2 * slots :, :] = dot(tail_cond, rows_of(all_ada, head_rows, tail_rows))
    add_mod_bias(2, 6)

    def norm_second(s):
        rows = slice(s * length, (s + 1) * length)
        after = x_ref[s] + part(s, 2) * branch[rows, :]
        dx[rows, :] = after
        normed, inverse = layer_norm(after)
        norm_two[rows, :] = normed
        inv_two[rows, :] = inverse
        h_two[rows, :] = (normed * (1.0 + part(s, 4)) + part(s, 3)).astype(b16)

    for s in range(slots):
        norm_second(s)

    note_rows = note_a.shape[4]
    own_lane = lax.broadcasted_iota(jnp.int32, (SUBLANES, width), 1)
    own_row = lax.broadcasted_iota(jnp.int32, (SUBLANES, width), 0)
    own_pick = jnp.where(own_lane == own_row + me * ada_rows, 1.0, 0.0).astype(b16)
    columns = dot(own_pick, rows_of(all_ada, 0, head_rows), (1, 1)).astype(b16)
    note_total = grid.count * note_rows
    at = lax.broadcasted_iota(jnp.int32, (1, note_total), 1)
    wanted = at // note_rows * head_rows + 1 + at % note_rows % slots
    source = lax.broadcasted_iota(jnp.int32, (head_total, note_total), 0)
    spread[...] = dot(columns, jnp.where(source == wanted, 1.0, 0.0).astype(b16)).astype(b16)

    def up(t):
        cols = slice(t * width, (t + 1) * width)
        pre = dot(h_two[...], one_weight(t)) + bias_rows[9 + t : 10 + t, :]
        square = pre * pre
        tanh_part = jnp.tanh(ROOT_TWO_OVER_PI * (pre + GELU_COEF * pre * square))
        half = 0.5 * (1.0 + tanh_part)
        act[:, cols] = (pre * half).astype(b16)
        slope[:, cols] = half + 0.5 * pre * (1.0 - tanh_part * tanh_part) * ROOT_TWO_OVER_PI * (
            1.0 + 3.0 * GELU_COEF * square
        )

    for k in range(per_core):
        until(ends[2] - 1 + -(-tall * (k + 1) // SUBLANES), "end")
        for core in range(pair):
            up(core * per_core + k)
    until(ends[3] - 1, "end")

    gbias[...] = jnp.zeros_like(gbias)
    last = gbias.shape[0] - 1
    cot_in.wait()

    for s in range(slots):
        grad = jnp.where(s < count, cot_ref[s], 0.0)
        cot_ref[s] = grad
        small[s * length : (s + 1) * length, :] = (grad * part(s, 5)).astype(b16)

    def finish(s):
        rows = slice(s * length, (s + 1) * length)
        value, grad = mlp[rows, :], cot_ref[s]
        out_ref[s] = jnp.where(s < count, dx[rows, :] + part(s, 5) * value, 0.0)
        dmod[5 * slots + s : 5 * slots + s + 1, :] = column_sum(grad * value)
        gbias[last : last + 1, :] += column_sum(grad * part(s, 5))


    bufs_mlp = (grad_mlp, pair_mlp, acc_mlp, one_mlp, two_mlp, side_mlp, line_mlp, sum_mlp)
    bufs_attn = (grad_attn, pair_attn, acc_attn, one_attn, two_attn, side_attn, line_attn, sum_attn)
    early = [
        Reduce(mover, bufs_mlp, pl.ds(start, size), slice(None), sum_order(k))
        for k, (_, start, size) in enumerate(cut_rows(all_mlp, 0, sizes.mlp_rows))
    ]
    late = [
        Reduce(mover, bufs_attn, slice(None), pl.ds(p * cut_head, cut_head), sum_order(p % 2))
        for p in range(heads // 2)
    ]
    reduces = early + late
    n_early, n_all = len(early), len(reduces)
    note_first = Share(mover, note_a, 0, note_rows, axis_order(1))
    note_last = Share(mover, note_b, 0, note_rows, axis_order(1))

    def run(name, first, last):
        for reduce in reduces[first:last]:
            getattr(reduce, name)()

    def mlp_grads(t):
        cols = slice(t * width, (t + 1) * width)
        a, b, zs = two_place(t)
        grad_mlp[a, b, zs, :, :, :] = (
            dot(act[:, cols], small[...], (0, 0)).astype(b16).reshape(per_tile // pair, pair, sizes.mlp_rows, width)
        )

    def mlp_down(t):
        cols = slice(t * width, (t + 1) * width)
        full = dot(small[...], two_weight(t), (1, 1)) * slope[:, cols]
        gbias[3 + t : 4 + t, :] = column_sum(full)
        grad = full.astype(b16)
        wide[:, cols] = grad
        core, k = t // per_core, t % per_core
        whole = dot(h_two[...], grad, (0, 0)).astype(b16)
        for g in range(sizes.one_devices // group):
            grad_mlp[g // low, g % low, :, core, tall * k : tall * (k + 1), :] = whole[
                g * depth * tall : (g + 1) * depth * tall
            ].reshape(depth, tall, width)

    for t in range(parts):
        mlp_grads(t)
    sent = 0
    for k in range(per_core):
        for core in range(pair):
            mlp_down(core * per_core + k)
        ready = n_early if k + 1 == per_core else tall * (k + 1) // SUBLANES
        run("begin", sent, ready)
        sent = ready
    two_all = jnp.concatenate([two_weight(t) for t in range(parts)], axis=0)
    mlp[...] = dot(act[...], two_all) + bias_rows[9 + parts : 10 + parts, :]
    for s in range(slots):
        finish(s)
    third = -(-n_early // 3)
    marks = [min(n_early, third * k) for k in range(4)]
    run("one", 0, marks[1])
    one_all = jnp.concatenate([one_weight(t) for t in range(parts)], axis=1)
    back[...] = dot(wide[...], one_all, (1, 1))
    run("one", marks[1], marks[2])

    def mlp_back(s):
        rows = slice(s * length, (s + 1) * length)
        grad_two = back[rows, :]
        normed = norm_two[rows, :]
        dmod[4 * slots + s : 4 * slots + s + 1, :] = column_sum(grad_two * normed)
        dmod[3 * slots + s : 3 * slots + s + 1, :] = column_sum(grad_two)
        after = cot_ref[s] + norm_backward(grad_two * (1.0 + part(s, 4)), normed, inv_two[rows, :])
        dx[rows, :] = after
        dmod[2 * slots + s : 2 * slots + s + 1, :] = column_sum(after * branch[rows, :])
        full = after * part(s, 2)
        gbias[2:3, :] += column_sum(full)
        small[rows, :] = full.astype(b16)

    for s in range(slots):
        mlp_back(s)
    note_a[hi, lo, z, c] = dmod[2 * slots :, :].astype(b16)
    note_first.begin()
    whole = dot(mixed[...], small[...], (0, 0)).astype(b16)
    for g in range(sizes.qkv_devices // group, grid.count // group):
        base = (g * group - sizes.qkv_devices) * sizes.attn_rows
        grad_attn[g // low, g % low] = whole[base : base + group * sizes.attn_rows].reshape(
            depth, pair, sizes.attn_rows, width
        )
    mixed[...] = dot(small[...], proj_weight(), (1, 1)).astype(b16)

    def attend_back(s, p):
        rows = slice(s * length, (s + 1) * length)
        at = p * cut_head
        span = slice(at, at + cut_head)
        query = qkv[rows, span]
        key = qkv[rows, width + at : width + at + cut_head]
        value = qkv[rows, 2 * width + at : 2 * width + at + cut_head]
        grad = both(mixed[rows, span])
        prob = jnp.concatenate([probs[s, 2 * p], probs[s, 2 * p + 1]], axis=0)
        d_prob = dot(grad, value, (1, 1))
        d_value = dot(prob.astype(b16), grad, (0, 0)).astype(b16)
        delta = jnp.sum(prob * d_prob, axis=-1, keepdims=True)
        d_score = (prob * (d_prob - delta) * score_scale).astype(b16)
        side = jnp.concatenate([d_score[:length], d_score[length:]], axis=1)
        d_query = dot(side, both(key)).astype(b16)
        d_key = dot(d_score, both(query), (0, 0)).astype(b16)
        dqkv[rows, span] = d_query
        dqkv[rows, width + at : width + at + cut_head] = d_key
        dqkv[rows, 2 * width + at : 2 * width + at + cut_head] = d_value
        gbias[0:1, span] += column_sum(d_query.astype(f32))
        gbias[1:2, span] += column_sum(d_value.astype(f32))

    between = {
        0: lambda: (run("two", 0, marks[1]), run("one", marks[2], marks[3])),
        1: lambda: (run("one", n_early, n_early + 1), note_first.first(), run("two", marks[1], marks[2])),
        2: lambda: (run("one", n_early + 1, n_early + 2), run("three", 0, marks[1])),
    }
    for p in range(heads // 2):
        for s in range(slots):
            attend_back(s, p)
        sides = [dqkv[:, k * width + p * cut_head : k * width + (p + 1) * cut_head] for k in range(3)]
        whole = dot(h_one[...], jnp.concatenate(sides, axis=1), (0, 0)).astype(b16)
        for k in range(3):
            block = whole[:, k * cut_head : (k + 1) * cut_head]
            for g in range(sizes.qkv_devices // group):
                base = g * group * sizes.qkv_rows
                grad_attn[
                    g // low, g % low, :, :, sizes.qkv_rows * k : sizes.qkv_rows * (k + 1),
                    p * cut_head : (p + 1) * cut_head,
                ] = block[base : base + group * sizes.qkv_rows].reshape(depth, pair, sizes.qkv_rows, cut_head)
        run("begin", n_early + p, n_early + p + 1)
        if p in between:
            between.pop(p)()
    for action in between.values():
        action()
    back[...] = dot(dqkv[:, 0:width], qkv_weight(0), (1, 1)) + (
        dot(dqkv[:, width : 2 * width], qkv_weight(1), (1, 1)) + dot(dqkv[:, 2 * width :], qkv_weight(2), (1, 1))
    )
    run("one", n_early + 2, n_all)

    def attn_back(s):
        rows = slice(s * length, (s + 1) * length)
        grad_one = back[rows, :]
        normed = norm_one[rows, :]
        dmod[slots + s : slots + s + 1, :] = column_sum(grad_one * normed)
        dmod[s : s + 1, :] = column_sum(grad_one)

    def input_back(s):
        rows = slice(s * length, (s + 1) * length)
        grad_one = back[rows, :]
        normed = norm_one[rows, :]
        gx_ref[s] = dx[rows, :] + norm_backward(grad_one * (1.0 + part(s, 1)), normed, inv_one[rows, :])

    for s in range(slots):
        attn_back(s)
    note_b[hi, lo, z, c] = jnp.concatenate([dmod[0 : 2 * slots, :], gbias[...]], axis=0).astype(b16)
    note_last.begin()
    for s in range(slots):
        input_back(s)
    run("two", marks[2], marks[3])
    run("three", marks[1], marks[2])
    run("two", n_early, n_early + 2)
    note_first.second()
    run("finish", 0, marks[1])

    def gather_entries(first, blocks, start, rows, total, span, skip, pick):
        grad_mod = dmod[first * slots : (first + blocks) * slots, :].astype(b16)
        values = dot(grad_mod, rows_of(all_ada, start, rows), (1, 1))
        values = jnp.where(owner_mask(total, span, skip, blocks), values, 0.0)
        merged = values[0:slots]
        for k in range(1, blocks):
            merged = merged + values[k * slots : (k + 1) * slots]
        upper_part = merged.astype(b16)
        lower_part = (merged - upper_part.astype(f32)).astype(b16)
        return dot(upper_part, pick[...], (1, 1)) + dot(lower_part, pick[...], (1, 1))

    grad_act = gather_entries(2, 4, head_rows, tail_rows, tail_total, tail_rows, 0, pick_tail)
    note_last.first()
    run("two", n_early + 2, n_all)
    run("three", marks[2], marks[3])
    run("finish", marks[1], marks[2])
    run("three", n_early, n_early + 2)
    note_first.third()
    grad_act = grad_act + gather_entries(0, 2, 0, head_rows, head_total, head_rows, lead, pick_head)
    gcond_ref[...] = grad_act * silu_slope(cond)
    note_last.second()
    run("three", n_early + 2, n_all)
    note_first.end()

    def from_notes(note, blocks, extra):
        kept = []
        entry = lax.broadcasted_iota(jnp.int32, (SUBLANES, note_total), 1) % note_rows
        for k in range(blocks):
            kept.append(jnp.where(entry // slots == k, spread[...].astype(f32), 0.0))
        line_at = lax.broadcasted_iota(jnp.int32, (SUBLANES, note_total), 0)
        wanted = jnp.where(entry < blocks * slots, entry // slots, entry - blocks * slots + blocks)
        kept.append(jnp.where(wanted == line_at, 1.0, 0.0))
        left = jnp.concatenate(kept, axis=0).astype(b16)
        return dot(left, rows_of(note, 0, note_rows))

    def store_ada(source, first, blocks):
        for k in range(blocks):
            for t in range(tiles):
                g_ada_out[pl.ds(tiles * (first + k) + t, ada_rows, stride=6 * tiles), :] = source[
                    k * SUBLANES : k * SUBLANES + ada_rows, lanes(t)
                ]

    early = from_notes(note_a, 4, 0)
    store_ada(early, 2, 4)
    note_last.third()
    run("finish", marks[2], marks[3])
    home = [
        mover.push(
            sum_mlp.at[pl.ds(pl.multiple_of(tall * k + one_rows * (1 - c), 8), one_rows)], back_in.at[k], partner
        )
        for k in range(per_core)
    ]
    arrive(home)
    for core in range(pair):
        @pl.when(jnp.logical_and(me < sizes.one_devices, c == core))
        def _():
            for k in range(per_core):
                for t in range(tiles):
                    own_at, far_at = per_core * core + k, per_core * (1 - core) + k
                    base = tall * k + one_rows * core
                    g_mlp_out[pl.ds(tiles * own_at + t, one_rows, stride=parts * tiles), :] = sum_mlp[
                        base : base + one_rows, lanes(t)
                    ]
                    g_mlp_out[pl.ds(tiles * far_at + t, one_rows, stride=parts * tiles), :] = back_in[k, :, lanes(t)]

    @pl.when(me >= sizes.one_devices)
    def _():
        for t in range(tiles):
            g_mlp_out[pl.ds(t, sizes.mlp_rows, stride=tiles), :] = sum_mlp[:, lanes(t)]

    note_last.end()
    late = from_notes(note_b, 2, gbias.shape[0])
    store_ada(late, 0, 2)
    bias_rows[0:2, :] = late[2 * SUBLANES : 2 * SUBLANES + 2]
    bias_rows[2:6, :] = early[4 * SUBLANES : 4 * SUBLANES + 4]
    bias_rows[6 : 6 + gbias.shape[0], :] = late[2 * SUBLANES + 2 : 2 * SUBLANES + 2 + gbias.shape[0]]
    begin = me * sizes.bias
    row, shift = begin // width, begin % width
    pair_rows = jnp.concatenate(
        [bias_rows[pl.ds(row, 1), :], bias_rows[pl.ds(row + 1, 1), :]], axis=1
    )
    turned = pltpu.roll(pair_rows, 2 * width - shift, 1)
    for t in range(g_bias_out.shape[0]):
        g_bias_out[t : t + 1, :] = turned[:, lanes(t)]

    run("finish", n_early, n_all)

    @pl.when(me < sizes.qkv_devices)
    def _():
        rows = sizes.qkv_rows
        for k in range(3):
            for t in range(tiles):
                g_attn_out[pl.ds(tiles * k + t, rows, stride=3 * tiles), :] = sum_attn[rows * k : rows * (k + 1), lanes(t)]

    @pl.when(me >= sizes.qkv_devices)
    def _():
        for t in range(tiles):
            g_attn_out[pl.ds(t, sizes.attn_rows, stride=tiles), :] = sum_attn[:, lanes(t)]

    mover.drain()
    assert len(mover.started) == send_sem.shape[0]


def run_fused(grid, sizes, counts, latents, conditioning, cotangent, shards, bias):
    slots, length, width, hidden = sizes.slots, sizes.length, sizes.width, sizes.hidden
    high, low, depth, pair = grid.sizes
    f32, b16 = jnp.float32, jnp.bfloat16
    rows = slots * length
    ada, attn, mlp = (shard.reshape(-1, LANES) for shard in shards)
    attn_rows, mlp_rows, one_rows = sizes.attn_rows, sizes.mlp_rows, sizes.one_rows
    ada_all = sizes.head_rows + sizes.tail_rows
    note_rows = 4 * slots
    extra = 4 + sizes.parts
    per_core = sizes.parts // pair
    side = max(high, low)
    tails = [(attn_rows, width), (mlp_rows, width)]
    leads = [
        (high, low, depth), (high, low, depth), (max(side - 1, 1), side, depth),
        (max(side - 1, 1), depth), (max(depth - 1, 1), side), (max(depth - 1, side - 1, 1),),
    ]
    scratch = [(grid.sizes + (n, width), b16) for n in (ada_all, attn_rows, mlp_rows, note_rows, note_rows)]
    scratch += [(grid.sizes + tail, b16) for tail in tails]
    scratch += [(lead + tail, b16) for lead in leads for tail in tails]
    scratch += [(tail, f32) for tail in tails]
    cut = per_core * one_rows
    scratch += [((cut, width), b16), ((cut, width), b16), ((per_core, one_rows, width), f32)]
    scratch += [(latents.shape, f32)] * 2 + [(array.shape, b16) for array in (ada, attn, mlp)]
    scratch += [(conditioning.shape, f32), (bias.shape, b16)]
    scratch += [
        ((max(ada.shape[0], attn.shape[0], mlp.shape[0]), LANES), f32), ((max(mlp_rows, attn_rows, ada_all), width), f32),
        ((sizes.parts * one_rows, width), f32),
        ((width, grid.count * sizes.head_rows), b16), ((width, grid.count * sizes.tail_rows), b16),
        ((SUBLANES, grid.count * note_rows), b16), ((-(-(7 + extra) // 8) * 8, width), f32),
    ]
    scratch += [
        ((6 * slots, width), f32), ((rows, width), f32), ((rows, 1), f32), ((rows, width), b16),
        ((rows, 3 * width), b16), ((slots, HEADS, length, length), f32), ((rows, width), b16),
        ((rows, width), f32), ((rows, width), f32), ((rows, 1), f32), ((rows, width), b16),
        ((rows, hidden), f32), ((rows, hidden), b16), ((rows, width), f32), ((rows, hidden), b16),
        ((rows, width), f32), ((rows, width), f32), ((rows, width), b16), ((rows, 3 * width), b16),
        ((6 * slots, width), f32), ((extra, width), f32),
    ]
    ceil = lambda n: -(-n // SUBLANES)
    gathers = ceil(sizes.head_rows) + ceil(sizes.tail_rows) + ceil(attn_rows) + ceil(mlp_rows)
    copies = sum(Share.copies(grid, axis_order(k)) for k in list(range(gathers)) + [1, 1])
    copies += (HEADS // 2 + ceil(mlp_rows)) * (high + low + depth + pair - 4)
    copies += 1 + per_core
    vmem, anywhere = pl.BlockSpec(memory_space=pltpu.VMEM), pl.BlockSpec(memory_space=pl.ANY)
    far = pl.BlockSpec(memory_space=pltpu.HBM)
    outs = [
        (latents.shape, f32), (latents.shape, f32), (conditioning.shape, f32),
        (ada.shape, f32), (attn.shape, f32), (mlp.shape, f32), ((-(-bias.shape[0] // LANES), LANES), f32),
    ]
    pinned = lambda array: pltpu.with_memory_space_constraint(array, pltpu.HBM)
    results = pl.pallas_call(
        partial(fused_kernel, grid, sizes),
        out_shape=[jax.ShapeDtypeStruct(shape, kind) for shape, kind in outs],
        in_specs=[pl.BlockSpec(memory_space=pltpu.SMEM)] + [far] * 7,
        out_specs=[vmem] * len(outs),
        scratch_shapes=[pltpu.VMEM(shape, kind) for shape, kind in scratch]
        + [pltpu.SemaphoreType.DMA((copies,)), pltpu.SemaphoreType.DMA((copies,)), pltpu.SemaphoreType.DMA((7,))],
        compiler_params=pltpu.CompilerParams(
            collective_id=2, has_side_effects=True, vmem_limit_bytes=50 * 1024 * 1024
        ),
    )(counts, *[pinned(a) for a in (latents, conditioning, cotangent, ada, attn, mlp, bias)])
    return pl.pallas_call(
        hand_on,
        out_shape=[jax.ShapeDtypeStruct(shape, kind) for shape, kind in outs],
        in_specs=[anywhere] * len(outs),
        out_specs=[far] * len(outs),
        scratch_shapes=[pltpu.SemaphoreType.DMA((len(outs),))],
        compiler_params=pltpu.CompilerParams(vmem_limit_bytes=4 * 1024 * 1024),
    )(*results)


def hand_on(*refs):
    ins, outs, sem = refs[: len(refs) // 2], refs[len(refs) // 2 : -1], refs[-1]
    copies = [pltpu.make_async_copy(a, b, sem.at[n]) for n, (a, b) in enumerate(zip(ins, outs))]
    for copy in copies:
        copy.start()
    for copy in copies:
        copy.wait()


def local(
    grid, latents, conditioning, counts, cotangent, ada_weights, attn_weights, mlp_weights, flat_biases
):
    model_width = latents.shape[-1]
    slots = latents.shape[0]
    shards = (ada_weights, attn_weights, mlp_weights, flat_biases)
    sizes = Sizes(grid, latents, shards)
    if sizes.fits:
        outs = run_fused(
            grid, sizes, counts, latents, conditioning, cotangent, shards[:3], flat_biases
        )
        return tuple(outs[:3]) + tuple(
            total.reshape(-1)[: shard.shape[0]] for total, shard in zip(outs[3:], shards)
        )
    whole_ada, whole_attn, whole_mlp, whole_bias = gather_all(
        grid, [pack([shard], ()) for shard in shards]
    )
    bias_flat = whole_bias.reshape(grid.count, -1)[:, : flat_biases.shape[0]].reshape(-1)
    weights = (
        whole_ada.reshape(model_width, 6 * model_width),
        whole_attn.reshape(-1, LANES),
        whole_mlp.reshape(-1, LANES),
    )
    biases = bias_flat.astype(jnp.float32)[None]
    output, grad_latents, grad_conditioning, cond_act, grad_mod, g_attn, g_mlp, g_bias = (
        run_block(counts, latents, conditioning, cotangent, weights, biases)
    )

    gap = padded_rows(flat_biases.shape[0]) * LANES - flat_biases.shape[0]
    bias_lines = jnp.pad(
        g_bias.astype(jnp.bfloat16).reshape(grid.count, -1), ((0, 0), (0, gap))
    )
    all_mod, all_act, *sums = scatter_sum(
        grid,
        [flat.reshape(grid.sizes + (-1, LANES)) for flat in (g_attn, g_mlp, bias_lines)],
        [grad_mod, cond_act],
    )
    all_mod = all_mod.reshape(grid.count * slots, -1)
    all_act = all_act.reshape(grid.count * slots, -1)
    grads = [own_rows(all_act, all_mod, ada_weights.shape[0])]
    grads += [total.reshape(-1)[: shard.shape[0]] for total, shard in zip(sums, shards[1:])]
    return (output, grad_latents, grad_conditioning) + tuple(grads)


def own_rows(left, right, extent):
    wide = right.shape[1]
    start = lax.axis_index(AXES) * extent
    rows = min(-(-extent // wide) + (1 if extent % wide else 0), left.shape[1])
    top = jnp.minimum(start // wide, left.shape[1] - rows)
    part = lax.dynamic_slice_in_dim(left, top, rows, 1)
    whole = dot(part, right, (0, 0)).reshape(-1)
    if rows * wide == extent:
        return whole
    return lax.dynamic_slice_in_dim(whole, start - top * wide, extent, 0)


def solution(mesh):
    in_specs = (
        P(("dp", "fsdp"), None, None),
        P(("dp", "fsdp"), None),
        P(("dp", "fsdp")),
        P(("dp", "fsdp"), None, None),
        P(("dp", "fsdp")),
        P(("dp", "fsdp")),
        P(("dp", "fsdp")),
        P(("dp", "fsdp")),
    )
    out_specs = (
        P(("dp", "fsdp"), None, None),
        P(("dp", "fsdp"), None, None),
        P(("dp", "fsdp"), None),
        P(("dp", "fsdp")),
        P(("dp", "fsdp")),
        P(("dp", "fsdp")),
        P(("dp", "fsdp")),
    )
    return jax.shard_map(partial(local, Grid(mesh)), mesh=mesh, in_specs=in_specs, out_specs=out_specs, check_vma=False)
```
